32 devices in a mesh: blk: 16 (over z, y, x), lay: 2 (over core).
Axes of the slice: x: 2, y: 2, z: 4, core: 2. Of those that a mesh axis runs over, the one named last changes fastest.
Arguments:
- matrix_source: float32 [32, 256, 256], P('lay', 'blk'), may hold values from -6 to 6
- accum: float32 [32, 256, 256], P('lay', 'blk'), may hold values from 0.02 to 0.5
- faces: float32 [6, 32, 256, 256], P(None, 'lay', 'blk'), may hold values from 0.03 to 30, as said below
- basis: float32 [4, 32, 256, 256], P(None, 'lay', 'blk'), may hold values from 0.05 to 0.5
- coarse_diag: float32 [8, 64], P('lay', 'blk'), may hold values from 32 to 128
- coarse_ratio: float32 [4, 8, 64], P(None, 'lay', 'blk'), may hold values from 0.1 to 0.24
- frac_source: float32 [16384], P(('blk', 'lay')), may hold values from -6 to 6
- frac_accum: float32 [16384], P(('blk', 'lay')), may hold values from 0.05 to 0.5
- frac_link: float32 [16384], P(('blk', 'lay')), may hold values from 0.5 to 5
- frac_trans: float32 [2, 16384], P(None, ('blk', 'lay')), may hold values from 0.5 to 5
- frac_cell: int32 [16384], P(('blk', 'lay')), may hold values from 0 to 65535
- frac_peer: int32 [2, 16384], P(None, ('blk', 'lay')), may hold values from 0 to 16383, as said below
- frac_count: int32 [32], P(('blk', 'lay')), may hold values from 1 to 512, as said below
Outputs:
- pressure: float32 [32, 256, 256], P('lay', 'blk')
- fracture: float32 [16384], P(('blk', 'lay'))
The draws below stay inside these ranges and needn't reach their ends.
Inputs may be any that keep to these rules, and one draw needn't show every extreme that they name: `faces`: the x+ face of a cell equals the x- face of the next cell along the first dimension, likewise y and z. `frac_count`: some owner has exactly 512 live slots in every draw. `frac_peer`: each entry is a live slot (slot index below its owner's count) of the same owner or of the owner just before or after it in the order blk index * 2 + lay index.
All inputs are finite; a program needn't handle non-finite values.
Results may differ from the reference program's by a relative error of at most 0.0001.
Values sent between devices are 32-bit elements; how exact they have to be, the bound alone decides.
No kernel may reach another device: no remote copies, remote signals or barrier semaphores. Data moves between devices by JAX's collectives and lax.ppermute only.
A program may use at most 64 MiB of HBM per device.

```python
import math
import jax
import jax.numpy as jnp

CX = 16
CY = 16
CZ = 256
FS = 512
BLOCK = 4
NP = 2
ITERS = 2
GX = 32
GY = 256
NCX = 8
NCY = 64
FRAC = 16384
N_LAY = 2


def fracture_counts(key):
    devices = FRAC // FS
    first_pick = jax.random.randint(jax.random.fold_in(key, 11), (devices,), 0, FS + 1)
    second_pick = jax.random.randint(jax.random.fold_in(key, 12), (devices,), 0, FS + 1)
    counts = 1 + first_pick * second_pick // (FS + 1)
    busiest = jax.random.randint(jax.random.fold_in(key, 13), (), 0, devices)
    return jnp.where(jnp.arange(devices) == busiest, FS, counts).astype(jnp.int32)


def draw_frac_count(key, part):
    return fracture_counts(key)


def draw_frac_peer(key, part):
    devices = FRAC // FS
    counts = fracture_counts(key)
    owner_device = jnp.arange(FRAC, dtype=jnp.int32) // FS
    offset = jax.random.randint(jax.random.fold_in(key, 21), (NP, FRAC), -1, 2)
    target = jnp.clip(owner_device[None] + offset, 0, devices - 1)
    raw_bits = jax.random.randint(jax.random.fold_in(key, 22), (NP, FRAC), 0, 1 << 30)
    slot_pick = raw_bits % counts[target]
    return (target * FS + slot_pick).astype(jnp.int32)


def draw_faces(key, part):

    def log_draw(salt_value, array_shape, low_value, high_value):
        return jnp.exp(jax.random.uniform(jax.random.fold_in(key, salt_value), array_shape, jnp.float32, jnp.log(low_value), jnp.log(high_value)))
    face_x = log_draw(31, (GX + 1, GY, CZ), 0.1, 10.0)
    face_y = log_draw(32, (GX, GY + 1, CZ), 0.1, 10.0)
    face_z = log_draw(33, (GX, GY, CZ + 1), 0.1, 10.0)
    return jnp.stack([face_x[1:], face_x[:-1], face_y[:, 1:], face_y[:, :-1], face_z[:, :, 1:], face_z[:, :, :-1]]).astype(jnp.float32)


def place_ends(entries, key, least, high):
    longest = entries.shape.index(max(entries.shape))
    spots = []
    for shift in (0, 1):
        where = [jax.random.randint(jax.random.fold_in(key, axis), (), 0, length) for axis, length in enumerate(entries.shape)]
        where[longest] = (where[longest] + shift) % entries.shape[longest]
        spots.append(tuple(where))
    return entries.at[spots[0]].set(least).at[spots[1]].set(high)


def levels(key, shape, cuts, least, largest):
    gain = 1.0
    for position, blocks in cuts:
        draws = jax.random.uniform(jax.random.fold_in(jax.random.fold_in(key, 6), position), (blocks,), jnp.float32, least / len(cuts), largest / len(cuts))
        gain = gain * jnp.repeat(jnp.exp(draws), shape[position] // blocks).reshape((-1,) + (1,) * (len(shape) - 1 - position))
    return gain


def centred(key, dims, deviation, bound, cuts=(), held_as=jnp.bfloat16):
    level = levels(key, dims, cuts, -0.22, 0.18) if cuts else 1.0
    values = jax.random.normal(key, dims, jnp.float32) * deviation * level
    return jnp.minimum(jnp.maximum(values, -bound), bound).astype(held_as)


def setup_inputs(seed: int = 0) -> dict:
    streams_of = jax.random.split(jax.random.key(seed), 14)
    return {
        "matrix_source": centred(streams_of[0], (GX, GY, CZ), 1.0, 6.0, ((0, 2), (1, 16)), jnp.float32),
        "accum": jnp.clip(jnp.exp(math.log(0.5) - 3.218876 * jax.random.uniform(streams_of[1], (GX, GY, CZ), jnp.float32) ** levels(streams_of[1], (GX, GY, CZ), ((0, 2), (1, 16)), -0.2, 0.2)), 0.02, 0.5),
        "faces": draw_faces(jax.random.fold_in(streams_of[13], 71), 0),
        "basis": jnp.clip(0.05 + 0.45 * jax.random.uniform(streams_of[3], (4, GX, GY, CZ), jnp.float32) ** levels(streams_of[3], (4, GX, GY, CZ), ((1, 2), (2, 16)), -0.2, 0.2), 0.05, 0.5),
        "coarse_diag": jnp.clip(32.0 + 96.0 * jax.random.uniform(streams_of[4], (NCX, NCY), jnp.float32) ** levels(streams_of[4], (NCX, NCY), ((0, 2), (1, 16)), -0.2, 0.2), 32.0, 128.0),
        "coarse_ratio": jnp.clip(0.1 + 0.13999999 * jax.random.uniform(streams_of[5], (4, NCX, NCY), jnp.float32) ** levels(streams_of[5], (4, NCX, NCY), ((1, 2), (2, 16)), -0.2, 0.2), 0.1, 0.24),
        "frac_source": centred(streams_of[6], (FRAC,), 1.0, 6.0, ((0, 32),), jnp.float32),
        "frac_accum": jnp.clip(jnp.exp(math.log(0.5) - 2.3025851 * jax.random.uniform(streams_of[7], (FRAC,), jnp.float32) ** levels(streams_of[7], (FRAC,), ((0, 32),), -0.2, 0.2)), 0.05, 0.5),
        "frac_link": jnp.clip(jnp.exp(math.log(5.0) - 2.3025851 * jax.random.uniform(streams_of[8], (FRAC,), jnp.float32) ** levels(streams_of[8], (FRAC,), ((0, 32),), -0.2, 0.2)), 0.5, 5.0),
        "frac_trans": jnp.clip(jnp.exp(math.log(5.0) - 2.3025851 * jax.random.uniform(streams_of[9], (NP, FRAC), jnp.float32) ** levels(streams_of[9], (NP, FRAC), ((1, 32),), -0.2, 0.2)), 0.5, 5.0),
        "frac_cell": place_ends(jax.random.randint(streams_of[10], (FRAC,), 0, CX * CY * CZ), jax.random.fold_in(streams_of[10], 1), 0, (CX * CY * CZ) - 1).astype(jnp.int32),
        "frac_peer": draw_frac_peer(jax.random.fold_in(streams_of[13], 71), 0),
        "frac_count": draw_frac_count(jax.random.fold_in(streams_of[13], 71), 0),
    }


OMEGA = 0.8


def place(block_sums, row_start, col_start):
    return jnp.pad(block_sums, ((row_start, 2 - row_start), (col_start, 2 - col_start)))


def spread(node_terms):
    low_mask = (jnp.arange(BLOCK) < BLOCK // 2).astype(jnp.float32)
    high_mask = 1.0 - low_mask
    x_low = low_mask[None, :, None, None]
    x_high = high_mask[None, :, None, None]
    y_low = low_mask[None, None, None, :]
    y_high = high_mask[None, None, None, :]

    def masked_sum(values, weight):
        return jnp.sum(values * weight, axis=(1, 3))

    spread_sum = place(jnp.sum(node_terms[0], axis=(1, 3)), 1, 1)
    spread_sum = spread_sum + place(masked_sum(node_terms[1], x_low), 0, 1) + place(masked_sum(node_terms[1], x_high), 2, 1)
    spread_sum = spread_sum + place(masked_sum(node_terms[2], y_low), 1, 0) + place(masked_sum(node_terms[2], y_high), 1, 2)
    spread_sum = spread_sum + place(masked_sum(node_terms[3], x_low * y_low), 0, 0) + place(masked_sum(node_terms[3], x_low * y_high), 0, 2)
    spread_sum = spread_sum + place(masked_sum(node_terms[3], x_high * y_low), 2, 0) + place(masked_sum(node_terms[3], x_high * y_high), 2, 2)
    return spread_sum


def node_values(extended):
    node_rows = extended.shape[0] - 2
    node_cols = extended.shape[1] - 2
    low_mask = jnp.arange(BLOCK) < BLOCK // 2
    x_low = low_mask[None, :, None, None]
    y_low = low_mask[None, None, None, :]

    def node_grid(row_start, col_start):
        return extended[row_start:row_start + node_rows, col_start:col_start + node_cols][:, None, :, None]

    full_shape = (node_rows, BLOCK, node_cols, BLOCK)
    centre = jnp.broadcast_to(node_grid(1, 1), full_shape)
    side_x = jnp.broadcast_to(jnp.where(x_low, node_grid(0, 1), node_grid(2, 1)), full_shape)
    side_y = jnp.broadcast_to(jnp.where(y_low, node_grid(1, 0), node_grid(1, 2)), full_shape)
    corner = jnp.broadcast_to(jnp.where(x_low, jnp.where(y_low, node_grid(0, 0), node_grid(0, 2)), jnp.where(y_low, node_grid(2, 0), node_grid(2, 2))), full_shape)
    stacked = jnp.stack([centre, side_x, side_y, corner])
    return stacked.reshape(4, node_rows * BLOCK, node_cols * BLOCK)


def prolong(basis, extended):
    fields = node_values(extended)
    return jnp.sum(basis * fields[..., None], axis=0)


def restrict_terms(basis, residual):
    node_sums = jnp.sum(basis * residual[None], axis=3)
    node_rows = node_sums.shape[1] // BLOCK
    node_cols = node_sums.shape[2] // BLOCK
    return spread(node_sums.reshape(4, node_rows, BLOCK, node_cols, BLOCK))


def coarse_second(first_sweep, first_padded, coarse_ratio):
    neighbours = [first_padded[:-2, 1:-1], first_padded[2:, 1:-1], first_padded[1:-1, :-2], first_padded[1:-1, 2:]]
    second = first_sweep
    for direction in range(4):
        second = second + coarse_ratio[direction] * neighbours[direction]
    return second


def flow_rows(padded, faces, accum):
    centre = padded[1:-1, 1:-1, 1:-1]
    beside = [padded[2:, 1:-1, 1:-1], padded[:-2, 1:-1, 1:-1], padded[1:-1, 2:, 1:-1],
              padded[1:-1, :-2, 1:-1], padded[1:-1, 1:-1, 2:], padded[1:-1, 1:-1, :-2]]
    result = accum * centre
    for direction in range(6):
        result = result + faces[direction] * (centre - beside[direction])
    return result


def matrix_rows(padded, pressure, fracture, faces, accum, cell_index, couple):
    result = flow_rows(padded, faces, accum)
    pressure_at = pressure.reshape(-1)[cell_index]
    link_flux = couple * (pressure_at - fracture)
    linked = jax.ops.segment_sum(link_flux, cell_index, num_segments=pressure.size).reshape(pressure.shape)
    return result + linked, pressure_at


def fracture_rows(fracture, pressure_at, peer_values, frac_accum, couple, frac_trans):
    return frac_accum * fracture + couple * (fracture - pressure_at) + jnp.sum(frac_trans * (fracture[None] - peer_values), axis=0)


def reference(matrix_source, accum, faces, basis, coarse_diag, coarse_ratio, frac_source, frac_accum, frac_link, frac_trans, frac_cell, frac_peer, frac_count):
    slot_index = jnp.arange(FRAC, dtype=jnp.int32)
    owner_device = (slot_index // FS).astype(jnp.int32)
    live_mask = (slot_index % FS < frac_count[owner_device]).astype(jnp.float32)
    couple = live_mask * frac_link
    local_x = frac_cell // (CY * CZ)
    local_y = (frac_cell // CZ) % CY
    local_z = frac_cell % CZ
    global_x = (owner_device % N_LAY) * CX + local_x
    global_y = (owner_device // N_LAY) * CY + local_y
    cell_index = ((global_x * GY + global_y) * CZ + local_z).astype(jnp.int32)
    matrix_diag = accum + jnp.sum(faces, axis=0) + jax.ops.segment_sum(couple, cell_index, num_segments=GX * GY * CZ).reshape(accum.shape)
    frac_diag = frac_accum + couple + jnp.sum(frac_trans, axis=0)
    pressure = jnp.zeros(matrix_source.shape, jnp.float32)
    fracture = jnp.zeros(frac_source.shape, jnp.float32)
    for iteration in range(ITERS):
        rows_now, pressure_at = matrix_rows(jnp.pad(pressure, 1), pressure, fracture, faces, accum, cell_index, couple)
        residual = matrix_source - rows_now
        extended = restrict_terms(basis, residual)
        coarse_rhs = extended[1:-1, 1:-1]
        first_sweep = coarse_rhs / coarse_diag
        second = coarse_second(first_sweep, jnp.pad(first_sweep, 1), coarse_ratio)
        pressure = pressure + prolong(basis, jnp.pad(second, 1))
        rows_now, pressure_at = matrix_rows(jnp.pad(pressure, 1), pressure, fracture, faces, accum, cell_index, couple)
        peer_values = fracture[frac_peer]
        frac_now = fracture_rows(fracture, pressure_at, peer_values, frac_accum, couple, frac_trans)
        pressure = pressure + OMEGA * (matrix_source - rows_now) / matrix_diag
        fracture = fracture + OMEGA * live_mask * (frac_source - frac_now) / frac_diag
    return pressure, fracture
```

```python
import jax
import jax.numpy as jnp
from jax import lax
from jax.experimental import pallas as pl
from jax.experimental.pallas import tpu as pltpu
from jax.sharding import PartitionSpec as P

BLOCK = 4
OMEGA = 0.8
TILE = 8
LANES = 128
F32 = jnp.float32
BF16 = jnp.bfloat16


def pair_lists(count):
    even = [(i, i ^ 1) for i in range(count) if i ^ 1 < count]
    odd = [(i, i + 1 if i % 2 else i - 1) for i in range(1, count)]
    return even, [(a, b) for a, b in odd if 0 < b < count]


def swap_pairs(even_load, odd_load, axis):
    even, odd = pair_lists(lax.axis_size(axis))
    got = [lax.ppermute(even_load, axis, even)]
    if odd:
        got.append(lax.ppermute(odd_load, axis, odd))
    return got


def run(kernel, name, outs, args, scratch=(), smem=()):
    spec = pl.BlockSpec(memory_space=pltpu.VMEM)
    scalar = pl.BlockSpec(memory_space=pltpu.SMEM)
    return pl.pallas_call(
        kernel,
        name=name,
        out_shape=[jax.ShapeDtypeStruct(shape, dtype) for shape, dtype in outs],
        in_specs=[scalar if i in smem else spec for i in range(len(args))],
        out_specs=[spec] * len(outs),
        scratch_shapes=list(scratch),
        compiler_params=pltpu.CompilerParams(vmem_limit_bytes=24 << 20),
    )(*args)


def iota(shape, dim):
    return lax.broadcasted_iota(jnp.int32, shape, dim)


def own_node(cell):
    return cell // BLOCK


def side_node(cell):
    return cell // BLOCK + (-1 if cell % BLOCK < BLOCK // 2 else 1)


def own_nodes(cells):
    return lax.shift_right_arithmetic(cells, 2)


def side_nodes(cells):
    low = jnp.bitwise_and(cells, BLOCK - 1) < BLOCK // 2
    return own_nodes(cells) + jnp.where(low, -1, 1)


def node_masks(cells):
    index = iota((cells, LANES), 0)
    lane = iota((cells, LANES), 1)
    return own_nodes(index) + 2 == lane, side_nodes(index) + 2 == lane


def fold_lanes(value):
    total = value[:, :LANES]
    for start in range(LANES, value.shape[1], LANES):
        total = total + value[:, start : start + LANES]
    return total


def by_parity(is_even, even_value, odd_value):
    return jnp.where(jnp.full(even_value.shape, is_even, jnp.int32) > 0, even_value, odd_value)


def low_high(is_even, even_got, odd_got):
    low = by_parity(is_even, odd_got, even_got)
    high = by_parity(is_even, even_got, odd_got)
    return low, high


def restrict_tile(columns, rows, cell_rows, cell_cols):
    sums = {}
    for x, residual, weight in columns:
        for k in range(4):
            node = (own_node(x) if k % 2 == 0 else side_node(x)) + 2
            part = fold_lanes(weight(k) * residual)
            key = (k // 2, node)
            sums[key] = sums[key] + part if key in sums else part
    masks = node_masks(cell_cols)
    row_index = iota((TILE, LANES), 0)
    tile = jnp.zeros((TILE, LANES), F32)
    nodes = sorted({node for _, node in sums})
    wide = {}
    if rows:
        lane = iota((cell_rows, LANES), 1)
        for y, residual, weight in rows:
            for k in range(4):
                node = (own_node(y) if k < 2 else side_node(y)) + 2
                part = jnp.sum(fold_lanes(weight(k) * residual), axis=1, keepdims=True)
                part = jnp.where(lane == node, part, 0.0)
                wide[k % 2] = wide[k % 2] + part if k % 2 in wide else part
        x_index = iota((cell_rows, LANES), 0)
        x_nodes = (own_nodes(x_index) + 2, side_nodes(x_index) + 2)
    for node in nodes:
        total = jnp.zeros((cell_cols, LANES), F32)
        for kind in range(2):
            if (kind, node) in sums:
                lane_sum = jnp.sum(sums[(kind, node)], axis=1, keepdims=True)
                total = total + jnp.where(masks[kind], lane_sum, 0.0)
        line = jnp.sum(total, axis=0, keepdims=True)
        if rows:
            extra = jnp.where(x_nodes[0] == node, wide[0], 0.0) + jnp.where(
                x_nodes[1] == node, wide[1], 0.0
            )
            line = line + jnp.sum(extra, axis=0, keepdims=True)
        tile = jnp.where(row_index == node, line, tile)
    return tile


def join_rows(tile, low, high):
    row = iota((TILE, LANES), 0)
    half = TILE // 2
    return (
        tile
        + jnp.where(row < half, pltpu.roll(low, half, 0), 0.0)
        + jnp.where(row >= half, pltpu.roll(high, half, 0), 0.0)
    )


def join_lanes(tile, low, high):
    part = jnp.bitwise_and(iota((TILE, LANES), 1), TILE - 1)
    half = TILE // 2
    return (
        tile
        + jnp.where(part < half, pltpu.roll(low, LANES - half, 1), 0.0)
        + jnp.where(part >= half, pltpu.roll(high, half, 1), 0.0)
    )


def coarse_solve(tile, table):
    lane = iota((TILE, LANES), 1)
    diag = pltpu.roll(table, LANES - TILE, 1)
    live = (lane < TILE) & (diag > 0.0)
    first = jnp.where(live, tile / jnp.where(live, diag, 1.0), 0.0)
    near = (
        pltpu.roll(first, 1, 0),
        pltpu.roll(first, TILE - 1, 0),
        pltpu.roll(first, 1, 1),
        pltpu.roll(first, LANES - 1, 1),
    )
    second = first
    for direction in range(4):
        ratio = pltpu.roll(table, LANES - TILE * (2 + direction), 1)
        second = second + jnp.where(lane < TILE, ratio, 0.0) * near[direction]
    return second


class Fields:
    def __init__(self, second, cell_rows, cell_cols):
        masks = node_masks(cell_cols)
        self.columns = {}
        for node in range(1, TILE - 1):
            line = jnp.broadcast_to(second[node : node + 1, :], (cell_cols, LANES))
            for kind in range(2):
                self.columns[(kind, node)] = jnp.sum(
                    jnp.where(masks[kind], line, 0.0), axis=1, keepdims=True
                )
        x_index = iota((cell_rows, LANES), 0)
        self.wide = []
        for nodes in (own_nodes(x_index) + 2, side_nodes(x_index) + 2):
            value = jnp.zeros((cell_rows, LANES), F32)
            for node in range(1, TILE - 1):
                value = jnp.where(nodes == node, second[node : node + 1, :], value)
            self.wide.append(value)

    def column(self, x, weight):
        own, side = own_node(x) + 2, side_node(x) + 2
        return (
            weight(0) * self.columns[(0, own)]
            + weight(1) * self.columns[(0, side)]
            + weight(2) * self.columns[(1, own)]
            + weight(3) * self.columns[(1, side)]
        )

    def row(self, y, weight):
        lane = iota(self.wide[0].shape, 1)

        def pick(kind, node):
            return jnp.sum(jnp.where(lane == node, self.wide[kind], 0.0), axis=1, keepdims=True)

        own, side = own_node(y) + 2, side_node(y) + 2
        return (
            weight(0) * pick(0, own)
            + weight(1) * pick(1, own)
            + weight(2) * pick(0, side)
            + weight(3) * pick(1, side)
        )


def neighbour_sum(faces, x, left, centre, right, low_row, high_row):
    cols, depth = centre.shape
    row = iota(centre.shape, 0)
    lane = iota(centre.shape, 1)
    above = pltpu.roll(centre, cols - 1, 0)
    below = pltpu.roll(centre, 1, 0)
    above = jnp.where(row == cols - 1, 0.0 if high_row is None else high_row, above)
    below = jnp.where(row == 0, 0.0 if low_row is None else low_row, below)
    deep = jnp.where(lane == depth - 1, 0.0, pltpu.roll(centre, depth - 1, 1))
    shallow = jnp.where(lane == 0, 0.0, pltpu.roll(centre, 1, 1))
    total = faces[2, x] * above + faces[3, x] * below + faces[4, x] * deep + faces[5, x] * shallow
    if right is not None:
        total = total + faces[0, x] * right
    if left is not None:
        total = total + faces[1, x] * left
    return total


def split3(value):
    high = value.astype(BF16)
    rest = value - high.astype(F32)
    mid = rest.astype(BF16)
    return high, mid, (rest - mid.astype(F32)).astype(BF16)


def gather_cells(pressure, hot_row, hot_depth):
    picked = None
    for part in split3(pressure):
        product = jnp.dot(part, hot_depth, preferred_element_type=F32)
        picked = product if picked is None else picked + product
    return jnp.sum(picked * hot_row.astype(F32), axis=0, keepdims=True)


def scatter_cells(values, hot_row, hot_depth):
    total = None
    for part in split3(values):
        spread = hot_row * part
        product = lax.dot_general(
            spread, hot_depth, (((1,), (1,)), ((), ())), preferred_element_type=F32
        )
        total = product if total is None else total + product
    return total


def as_line(value):
    return jnp.concatenate([value[i : i + 1, :] for i in range(value.shape[0])], axis=1)


def as_rows(line, width):
    return jnp.concatenate(
        [line[:, start : start + width] for start in range(0, line.shape[1], width)], axis=0
    )


def local(
    matrix_source,
    accum,
    faces,
    basis,
    coarse_diag,
    coarse_ratio,
    frac_source,
    frac_accum,
    frac_link,
    frac_trans,
    frac_cell,
    frac_peer,
    frac_count,
):
    slots = frac_source.shape[0]
    cell_rows, cell_cols, depth = matrix_source.shape
    cells = cell_rows * cell_cols
    node_rows, node_cols = cell_rows // BLOCK, cell_cols // BLOCK
    assert node_rows + 4 == TILE and node_cols + 4 == TILE
    assert depth & (depth - 1) == 0 and cell_rows == cell_cols
    depth_bits = depth.bit_length() - 1
    lay_size = lax.axis_size("lay")
    lay_pairs = len([p for p in pair_lists(lay_size) if p])
    layer_rows = 4 * cell_cols
    load_one = (layer_rows + TILE, depth)
    slot_rows = slots // depth
    load_two = (cell_cols + 2 * TILE, depth)
    block = matrix_source.shape

    table = jnp.zeros((TILE, LANES), F32)
    table = lax.dynamic_update_slice(table, coarse_diag, (2, TILE + 2))
    for direction in range(4):
        table = lax.dynamic_update_slice(
            table, coarse_ratio[direction], (2, TILE * (2 + direction) + 2)
        )

    def is_even(axis):
        return 1 - jnp.bitwise_and(lax.axis_index(axis), 1)

    def lay_got(refs):
        got = [ref for ref in refs]
        return got if len(got) == 2 else [got[0], None]

    def kernel_a(basis_ref, source_ref, table_ref, tile_ref, *loads):
        def column(x):
            return x, source_ref[x], lambda k: basis_ref[k, x]

        tile = restrict_tile([column(x) for x in range(cell_rows)], [], cell_rows, cell_cols)
        tile = tile + table_ref[...]
        tile_ref[...] = tile
        even = is_even("lay")
        edges = (even * (cell_rows - 1), (1 - even) * (cell_rows - 1))
        for load, edge in zip(loads, edges):
            for k in range(4):
                load[k * cell_cols : (k + 1) * cell_cols, :] = basis_ref[k, edge]
            load[layer_rows:, :LANES] = tile
            load[layer_rows:, LANES:] = jnp.zeros((TILE, depth - LANES), F32)

    outs = [((TILE, LANES), F32)] + [(load_one, F32)] * lay_pairs
    tile_own, *loads = run(kernel_a, "restrict_source", outs, (basis, matrix_source, table))
    lay_one = swap_pairs(loads[0], loads[-1], "lay")

    def lay_sides(refs, window):
        even = is_even("lay")
        first = refs[0][window]
        second = refs[1][window] if len(refs) > 1 else jnp.zeros(first.shape, F32)
        return low_high(even, first, second)

    def blk_sides(even_ref, odd_ref, window):
        return low_high(is_even("blk"), even_ref[window], odd_ref[window])

    def kernel_e(tile_ref, basis_ref, *refs):
        got, (join_ref, even_ref, odd_ref) = refs[:-3], refs[-3:]
        low, high = lay_sides(got, (slice(layer_rows, layer_rows + TILE), slice(0, LANES)))
        joined = join_rows(tile_ref[...], low, high)
        join_ref[...] = joined
        even = is_even("blk")
        edges = (even * (cell_cols - 1), (1 - even) * (cell_cols - 1))
        for ref, edge in zip((even_ref, odd_ref), edges):
            for k in range(4):
                for x in range(cell_rows):
                    line = k * cell_rows + x
                    ref[line : line + 1, :] = basis_ref[k, x, pl.ds(edge, 1), :]
            ref[layer_rows:, :LANES] = joined
            ref[layer_rows:, LANES:] = jnp.zeros((TILE, depth - LANES), F32)

    outs = [((TILE, LANES), F32), (load_one, F32), (load_one, F32)]
    joined_one, even_one, odd_one = run(kernel_e, "join", outs, (tile_own, basis, *lay_one))
    blk_one = swap_pairs(even_one, odd_one, "blk")

    def kernel_p(
        faces_ref, accum_ref, cell_ref, link_ref, facc_ref, trans_ref, peer_ref, count_ref,
        diag_ref, scale_ref, row_ref, depth_ref, frac_ref, low_ref,
    ):
        slot = iota((1, slots), 1)
        live = (slot < count_ref[0]).astype(F32)
        couple = live * as_line(link_ref[...])
        frac_diag = as_line(facc_ref[...]) + couple
        for j in range(trans_ref.shape[0]):
            frac_diag = frac_diag + trans_ref[j : j + 1, :]
        frac_ref[0:1, :] = couple
        frac_ref[1:2, :] = OMEGA * live / frac_diag
        cell = as_line(cell_ref[...])
        at_row = lax.shift_right_logical(cell, depth_bits)
        at_depth = jnp.bitwise_and(cell, depth - 1)
        hot_row = (iota((cells, slots), 0) == at_row).astype(F32).astype(BF16)
        hot_depth = (iota((depth, slots), 0) == at_depth).astype(F32).astype(BF16)
        row_ref[...] = hot_row
        depth_ref[...] = hot_depth
        linked = scatter_cells(couple, hot_row, hot_depth)
        for x in range(cell_rows):
            diag = accum_ref[x]
            for d in range(6):
                diag = diag + faces_ref[d, x]
            diag = diag + linked[x * cell_cols : (x + 1) * cell_cols, :]
            diag_ref[x] = diag
            scale_ref[x] = OMEGA / diag
        owner = lax.axis_index("blk") * lay_size + lax.axis_index("lay")
        peer = peer_ref[...] - (owner - 1) * slots
        peer = jnp.concatenate([peer[j : j + 1, :] for j in range(peer.shape[0])], axis=1)
        low_ref[...] = (
            (iota((LANES, peer.shape[1]), 0) == jnp.bitwise_and(peer, LANES - 1))
            .astype(F32)
            .astype(BF16)
        )
        frac_ref[2:4, :] = as_rows(lax.shift_right_logical(peer, 7), slots).astype(F32)

    links = frac_trans.shape[0]
    outs = [
        (block, F32),
        (block, F32),
        ((cells, slots), BF16),
        ((depth, slots), BF16),
        ((TILE, slots), F32),
        ((LANES, links * slots), BF16),
    ]
    small = (slots // LANES, LANES)
    diag, scale, hot_row, hot_depth, frac_pack, hot_low = run(
        kernel_p,
        "prepare",
        outs,
        (
            faces,
            accum,
            frac_cell.reshape(small),
            frac_link.reshape(small),
            frac_accum.reshape(small),
            frac_trans,
            frac_peer,
            frac_count,
        ),
        smem=(7,),
    )

    layer = (slice(0, layer_rows), slice(0, depth))

    def rims_of(lay_refs, blk_even, blk_odd):
        lay_low, lay_high = lay_sides(lay_refs, layer)
        blk_low, blk_high = blk_sides(blk_even, blk_odd, layer)

        def pick(value):
            return lambda k: value[k * cell_cols : (k + 1) * cell_cols, :]

        return pick(lay_low), pick(lay_high), pick(blk_low), pick(blk_high)

    def kernel_b(
        faces_ref, basis_ref, source_ref, diag_ref, scale_ref, row_ref, depth_ref, frac_ref,
        fsrc_ref, joined_ref, blk_even, blk_odd, *refs,
    ):
        lay_refs = refs[:lay_pairs]
        p2_ref, right_ref, f_ref, tile_ref, second_ref = refs[lay_pairs : lay_pairs + 5]
        loads = refs[lay_pairs + 5 : -2]
        p1_ref, link_ref = refs[-2:]
        at_tile = (slice(layer_rows, layer_rows + TILE), slice(0, LANES))
        low, high = blk_sides(blk_even, blk_odd, at_tile)
        table = join_lanes(joined_ref[...], low, high)
        second_ref[...] = table
        fields = Fields(coarse_solve(table, table), cell_rows, cell_cols)
        x_low, x_high, y_low, y_high = rims_of(lay_refs, blk_even, blk_odd)

        def weight(x):
            return lambda k: basis_ref[k, x]

        for x in range(cell_rows):
            p1_ref[x] = fields.column(x, weight(x))
        left_rim = fields.column(-1, x_low)
        right_rim = fields.column(cell_rows, x_high)
        low_rim = fields.row(-1, y_low)
        high_rim = fields.row(cell_cols, y_high)

        flat = p1_ref[...].reshape(cells, depth)
        pressure_at = gather_cells(flat, row_ref[...], depth_ref[...])
        couple = frac_ref[0:1, :]
        fracture = frac_ref[1:2, :] * (as_line(fsrc_ref[...]) + couple * pressure_at)
        f_ref[...] = fracture
        linked = scatter_cells(couple * fracture, row_ref[...], depth_ref[...])
        link_ref[...] = linked.reshape(block)

        for x in range(cell_rows):
            centre = p1_ref[x]
            left = p1_ref[x - 1] if x else left_rim
            right = p1_ref[x + 1] if x + 1 < cell_rows else right_rim
            around = neighbour_sum(
                faces_ref, x, left, centre, right, low_rim[x : x + 1, :], high_rim[x : x + 1, :]
            )
            p2_ref[x] = (1.0 - OMEGA) * centre + scale_ref[x] * (source_ref[x] + around)

        columns = []
        low_lines, high_lines = [], []
        for x in range(cell_rows):
            centre = p2_ref[x]
            forced = source_ref[x] + link_ref[x]
            right_ref[x] = forced
            left = p2_ref[x - 1] if x else None
            right = p2_ref[x + 1] if x + 1 < cell_rows else None
            around = neighbour_sum(faces_ref, x, left, centre, right, None, None)
            columns.append((x, forced - diag_ref[x] * centre + around, weight(x)))
            low_lines.append(faces_ref[3, x, 0:1, :] * p2_ref[x, 0:1, :])
            high_lines.append(
                faces_ref[2, x, cell_cols - 1 : cell_cols, :]
                * p2_ref[x, cell_cols - 1 : cell_cols, :]
            )
        columns.append((-1, faces_ref[1, 0] * p2_ref[0], x_low))
        last = cell_rows - 1
        columns.append((cell_rows, faces_ref[0, last] * p2_ref[last], x_high))
        rows = [
            (-1, jnp.concatenate(low_lines, axis=0), y_low),
            (cell_cols, jnp.concatenate(high_lines, axis=0), y_high),
        ]
        tile = restrict_tile(columns, rows, cell_rows, cell_cols)
        tile_ref[...] = tile
        even = is_even("lay")
        edges = (even * (cell_rows - 1), (1 - even) * (cell_rows - 1))
        for load, edge in zip(loads, edges):
            load[:cell_cols, :] = p2_ref[edge]
            load[cell_cols : cell_cols + TILE, :LANES] = tile
            load[cell_cols : cell_cols + TILE, LANES:] = jnp.zeros((TILE, depth - LANES), F32)
            load[cell_cols + TILE :, :] = jnp.zeros((TILE, depth), F32)
            load[cell_cols + TILE : cell_cols + TILE + slot_rows, :] = as_rows(fracture, depth)

    outs = [(block, F32), (block, F32), ((1, slots), F32), ((TILE, LANES), F32), ((TILE, LANES), F32)]
    outs = outs + [(load_two, F32)] * lay_pairs
    frac_source_rows = frac_source.reshape(small)
    pressure, forced, fracture, tile_two, table_all, *loads = run(
        kernel_b,
        "cycle",
        outs,
        (
            faces, basis, matrix_source, diag, scale, hot_row, hot_depth, frac_pack,
            frac_source_rows, joined_one, *blk_one, *lay_one,
        ),
        scratch=(pltpu.VMEM(block, F32), pltpu.VMEM(block, F32)),
    )
    lay_two = swap_pairs(loads[0], loads[-1], "lay")

    tile_rows = (slice(cell_cols, cell_cols + TILE), slice(0, LANES))
    frac_rows = (slice(cell_cols + TILE, cell_cols + TILE + slot_rows), slice(0, depth))

    def kernel_f(tile_ref, p_ref, *refs):
        got, (join_ref, even_ref, odd_ref) = refs[:-3], refs[-3:]
        low, high = lay_sides(got, tile_rows)
        joined = join_rows(tile_ref[...], low, high)
        join_ref[...] = joined
        even = is_even("blk")
        edges = (even * (cell_cols - 1), (1 - even) * (cell_cols - 1))
        for ref, edge in zip((even_ref, odd_ref), edges):
            for x in range(cell_rows):
                ref[x : x + 1, :] = p_ref[x, pl.ds(edge, 1), :]
            ref[cell_cols : cell_cols + TILE, :LANES] = joined
            ref[cell_cols : cell_cols + TILE, LANES:] = jnp.zeros((TILE, depth - LANES), F32)
            ref[cell_cols + TILE :, :] = got[0][cell_cols + TILE :, :]

    outs = [((TILE, LANES), F32), (load_two, F32), (load_two, F32)]
    joined_two, even_two, odd_two = run(
        kernel_f, "join_two", outs, (tile_two, pressure, *lay_two)
    )
    blk_two = swap_pairs(even_two, odd_two, "blk")
    ring = []
    if lay_size != 2:
        owners = lax.axis_size("blk") * lay_size
        ahead = [(i, i + 1) for i in range(owners - 1)]
        line = fracture.reshape(slot_rows, depth)
        ring = [
            lax.ppermute(line, ("blk", "lay"), ahead),
            lax.ppermute(line, ("blk", "lay"), [(b, a) for a, b in ahead]),
        ]

    def kernel_c(
        faces_ref, basis_ref, forced_ref, scale_ref, row_ref, depth_ref, frac_ref, low_ref,
        fsrc_ref, trans_ref, p2_ref, f_ref, joined_ref, table_ref,
        one_even, one_odd, two_even, two_odd, *refs,
    ):
        lay_first, lay_second = refs[:lay_pairs], refs[lay_pairs : 2 * lay_pairs]
        ring_refs = refs[2 * lay_pairs : -3]
        p_out, f_out, p3_ref = refs[-3:]
        low, high = blk_sides(two_even, two_odd, tile_rows)
        tile = join_lanes(joined_ref[...], low, high)
        fields = Fields(coarse_solve(tile, table_ref[...]), cell_rows, cell_cols)
        x_low, x_high, y_low, y_high = rims_of(lay_first, one_even, one_odd)
        window = (slice(0, cell_cols), slice(0, depth))
        p_left, p_right = lay_sides(lay_second, window)
        p_low, p_high = blk_sides(two_even, two_odd, window)

        for x in range(cell_rows):
            p3_ref[x] = p2_ref[x] + fields.column(x, lambda k: basis_ref[k, x])
        left_rim = p_left + fields.column(-1, x_low)
        right_rim = p_right + fields.column(cell_rows, x_high)
        low_rim = p_low + fields.row(-1, y_low)
        high_rim = p_high + fields.row(cell_cols, y_high)
        for x in range(cell_rows):
            centre = p3_ref[x]
            left = p3_ref[x - 1] if x else left_rim
            right = p3_ref[x + 1] if x + 1 < cell_rows else right_rim
            around = neighbour_sum(
                faces_ref, x, left, centre, right, low_rim[x : x + 1, :], high_rim[x : x + 1, :]
            )
            p_out[x] = (1.0 - OMEGA) * centre + scale_ref[x] * (forced_ref[x] + around)

        flat = p3_ref[...].reshape(cells, depth)
        pressure_at = gather_cells(flat, row_ref[...], depth_ref[...])
        mine = as_rows(f_ref[...], LANES)
        if ring_refs:
            before, after = ring_refs[0][...], ring_refs[1][...]
        else:
            partner = lay_second[0][frac_rows]
            from_low, from_high = blk_sides(two_even, two_odd, frac_rows)
            before = by_parity(is_even("lay"), from_low, partner)
            after = by_parity(is_even("lay"), partner, from_high)
        width = mine.shape[0]
        wide = jnp.concatenate(
            [as_rows(as_line(before), LANES), mine, as_rows(as_line(after), LANES)]
            + [jnp.zeros((-3 * width % TILE, LANES), F32)] * (3 * width % TILE > 0),
            axis=0,
        )
        peer_high = as_line(frac_ref[2:4, :])
        picked = None
        for part in split3(wide):
            product = jnp.dot(part, low_ref[...], preferred_element_type=F32)
            picked = product if picked is None else picked + product
        match = iota(picked.shape, 0).astype(F32) == peer_high
        peers = jnp.sum(jnp.where(match, picked, 0.0), axis=0, keepdims=True)
        flux = as_line(fsrc_ref[...]) + frac_ref[0:1, :] * pressure_at
        for j in range(links):
            flux = flux + trans_ref[j : j + 1, :] * peers[:, j * slots : (j + 1) * slots]
        result = (1.0 - OMEGA) * f_ref[...] + frac_ref[1:2, :] * flux
        f_out[...] = as_rows(result, LANES)

    final, frac_final = run(
        kernel_c,
        "finish",
        [(block, F32), (small, F32)],
        (
            faces, basis, forced, scale, hot_row, hot_depth, frac_pack, hot_low,
            frac_source_rows, frac_trans, pressure, fracture, joined_two, table_all,
            *blk_one, *blk_two, *lay_one, *lay_two, *ring,
        ),
        scratch=(pltpu.VMEM(block, F32),),
    )
    return final, frac_final.reshape(slots)


def solution(mesh):
    return jax.shard_map(
        local,
        mesh=mesh,
        in_specs=(
            P("lay", "blk", None),
            P("lay", "blk", None),
            P(None, "lay", "blk", None),
            P(None, "lay", "blk", None),
            P("lay", "blk"),
            P(None, "lay", "blk"),
            P(("blk", "lay")),
            P(("blk", "lay")),
            P(("blk", "lay")),
            P(None, ("blk", "lay")),
            P(("blk", "lay")),
            P(None, ("blk", "lay")),
            P(("blk", "lay")),
        ),
        out_specs=(P("lay", "blk", None), P(("blk", "lay"))),
        check_vma=False,
    )
```

```python
import jax
import jax.numpy as jnp
from jax import lax
from jax.experimental import pallas as pl
from jax.experimental.pallas import tpu as pltpu
from jax.sharding import PartitionSpec as P

BLOCK = 4
OMEGA = 0.8
TILE = 8
LANES = 128
F32 = jnp.float32
BF16 = jnp.bfloat16


def pair_lists(count):
    even = [(i, i ^ 1) for i in range(count) if i ^ 1 < count]
    odd = [(i, i + 1 if i % 2 else i - 1) for i in range(1, count)]
    return even, [(a, b) for a, b in odd if 0 < b < count]


def swap_pairs(even_load, odd_load, axis):
    even, odd = pair_lists(lax.axis_size(axis))
    got = [lax.ppermute(even_load, axis, even)]
    if odd:
        got.append(lax.ppermute(odd_load, axis, odd))
    return got


def run(kernel, outs, args, scratch=(), smem=(), in_place=(), out_place=()):
    spec = pl.BlockSpec(memory_space=pltpu.VMEM)
    scalar = pl.BlockSpec(memory_space=pltpu.SMEM)
    there = pl.BlockSpec(memory_space=pltpu.HBM)

    def place(i):
        return scalar if i in smem else there if i in in_place else spec

    return pl.pallas_call(
        kernel,
        out_shape=[jax.ShapeDtypeStruct(shape, dtype) for shape, dtype in outs],
        in_specs=[place(i) for i in range(len(args))],
        out_specs=[there if i in out_place else spec for i in range(len(outs))],
        scratch_shapes=list(scratch),
        compiler_params=pltpu.CompilerParams(vmem_limit_bytes=24 << 20),
    )(*args)


def iota(shape, dim):
    return lax.broadcasted_iota(jnp.int32, shape, dim)


def own_node(cell):
    return cell // BLOCK


def side_node(cell):
    return cell // BLOCK + (-1 if cell % BLOCK < BLOCK // 2 else 1)


def own_nodes(cells):
    return lax.shift_right_arithmetic(cells, 2)


def side_nodes(cells):
    low = jnp.bitwise_and(cells, BLOCK - 1) < BLOCK // 2
    return own_nodes(cells) + jnp.where(low, -1, 1)


def node_masks(cells):
    index = iota((cells, LANES), 0)
    lane = iota((cells, LANES), 1)
    return own_nodes(index) + 2 == lane, side_nodes(index) + 2 == lane


def fold_lanes(value):
    total = value[:, :LANES]
    for start in range(LANES, value.shape[1], LANES):
        total = total + value[:, start : start + LANES]
    return total


def by_parity(is_even, even_value, odd_value):
    return jnp.where(jnp.full(even_value.shape, is_even, jnp.int32) > 0, even_value, odd_value)


def low_high(is_even, even_got, odd_got):
    low = by_parity(is_even, odd_got, even_got)
    high = by_parity(is_even, even_got, odd_got)
    return low, high


def restrict_tile(columns, rows, cell_rows, cell_cols):
    sums = {}
    for x, residual, weight in columns:
        for k in range(4):
            node = (own_node(x) if k % 2 == 0 else side_node(x)) + 2
            part = fold_lanes(weight(k) * residual)
            key = (k // 2, node)
            sums[key] = sums[key] + part if key in sums else part
    masks = node_masks(cell_cols)
    row_index = iota((TILE, LANES), 0)
    tile = jnp.zeros((TILE, LANES), F32)
    nodes = sorted({node for _, node in sums})
    wide = {}
    if rows:
        lane = iota((cell_rows, LANES), 1)
        for y, residual, weight in rows:
            for k in range(4):
                node = (own_node(y) if k < 2 else side_node(y)) + 2
                part = jnp.sum(fold_lanes(weight(k) * residual), axis=1, keepdims=True)
                part = jnp.where(lane == node, part, 0.0)
                wide[k % 2] = wide[k % 2] + part if k % 2 in wide else part
        x_index = iota((cell_rows, LANES), 0)
        x_nodes = (own_nodes(x_index) + 2, side_nodes(x_index) + 2)
    for node in nodes:
        total = jnp.zeros((cell_cols, LANES), F32)
        for kind in range(2):
            if (kind, node) in sums:
                lane_sum = jnp.sum(sums[(kind, node)], axis=1, keepdims=True)
                total = total + jnp.where(masks[kind], lane_sum, 0.0)
        line = jnp.sum(total, axis=0, keepdims=True)
        if rows:
            extra = jnp.where(x_nodes[0] == node, wide[0], 0.0) + jnp.where(
                x_nodes[1] == node, wide[1], 0.0
            )
            line = line + jnp.sum(extra, axis=0, keepdims=True)
        tile = jnp.where(row_index == node, line, tile)
    return tile


def join_rows(tile, low, high):
    row = iota((TILE, LANES), 0)
    half = TILE // 2
    return (
        tile
        + jnp.where(row < half, pltpu.roll(low, half, 0), 0.0)
        + jnp.where(row >= half, pltpu.roll(high, half, 0), 0.0)
    )


def join_lanes(tile, low, high):
    part = jnp.bitwise_and(iota((TILE, LANES), 1), TILE - 1)
    half = TILE // 2
    return (
        tile
        + jnp.where(part < half, pltpu.roll(low, LANES - half, 1), 0.0)
        + jnp.where(part >= half, pltpu.roll(high, half, 1), 0.0)
    )


def coarse_solve(tile, table):
    lane = iota((TILE, LANES), 1)
    diag = pltpu.roll(table, LANES - TILE, 1)
    live = (lane < TILE) & (diag > 0.0)
    first = jnp.where(live, tile / jnp.where(live, diag, 1.0), 0.0)
    near = (
        pltpu.roll(first, 1, 0),
        pltpu.roll(first, TILE - 1, 0),
        pltpu.roll(first, 1, 1),
        pltpu.roll(first, LANES - 1, 1),
    )
    second = first
    for direction in range(4):
        ratio = pltpu.roll(table, LANES - TILE * (2 + direction), 1)
        second = second + jnp.where(lane < TILE, ratio, 0.0) * near[direction]
    return second


class Fields:
    def __init__(self, second, cell_rows, cell_cols):
        masks = node_masks(cell_cols)
        self.columns = {}
        for node in range(1, TILE - 1):
            line = jnp.broadcast_to(second[node : node + 1, :], (cell_cols, LANES))
            for kind in range(2):
                self.columns[(kind, node)] = jnp.sum(
                    jnp.where(masks[kind], line, 0.0), axis=1, keepdims=True
                )
        x_index = iota((cell_rows, LANES), 0)
        self.wide = []
        for nodes in (own_nodes(x_index) + 2, side_nodes(x_index) + 2):
            value = jnp.zeros((cell_rows, LANES), F32)
            for node in range(1, TILE - 1):
                value = jnp.where(nodes == node, second[node : node + 1, :], value)
            self.wide.append(value)

    def column(self, x, weight):
        own, side = own_node(x) + 2, side_node(x) + 2
        return (
            weight(0) * self.columns[(0, own)]
            + weight(1) * self.columns[(0, side)]
            + weight(2) * self.columns[(1, own)]
            + weight(3) * self.columns[(1, side)]
        )

    def row(self, y, weight):
        lane = iota(self.wide[0].shape, 1)

        def pick(kind, node):
            return jnp.sum(jnp.where(lane == node, self.wide[kind], 0.0), axis=1, keepdims=True)

        own, side = own_node(y) + 2, side_node(y) + 2
        return (
            weight(0) * pick(0, own)
            + weight(1) * pick(1, own)
            + weight(2) * pick(0, side)
            + weight(3) * pick(1, side)
        )


def neighbour_sum(faces, x, left, centre, right, low_row, high_row):
    cols, depth = centre.shape
    row = iota(centre.shape, 0)
    lane = iota(centre.shape, 1)
    above = pltpu.roll(centre, cols - 1, 0)
    below = pltpu.roll(centre, 1, 0)
    above = jnp.where(row == cols - 1, 0.0 if high_row is None else high_row, above)
    below = jnp.where(row == 0, 0.0 if low_row is None else low_row, below)
    deep = jnp.where(lane == depth - 1, 0.0, pltpu.roll(centre, depth - 1, 1))
    shallow = jnp.where(lane == 0, 0.0, pltpu.roll(centre, 1, 1))
    total = faces[2, x] * above + faces[3, x] * below + faces[4, x] * deep + faces[5, x] * shallow
    if right is not None:
        total = total + faces[0, x] * right
    if left is not None:
        total = total + faces[1, x] * left
    return total


def split3(value):
    high = value.astype(BF16)
    rest = value - high.astype(F32)
    mid = rest.astype(BF16)
    return high, mid, (rest - mid.astype(F32)).astype(BF16)


def gather_cells(pressure, hot_row, hot_depth):
    picked = None
    for part in split3(pressure):
        product = jnp.dot(part, hot_depth, preferred_element_type=F32)
        picked = product if picked is None else picked + product
    return jnp.sum(picked * hot_row.astype(F32), axis=0, keepdims=True)


def scatter_cells(values, hot_row, hot_depth):
    total = None
    for part in split3(values):
        spread = hot_row * part
        product = lax.dot_general(
            spread, hot_depth, (((1,), (1,)), ((), ())), preferred_element_type=F32
        )
        total = product if total is None else total + product
    return total


def nodes_at_slots(second, hot_node, node_weight):
    picked = None
    for part in split3(second):
        product = jnp.dot(part, hot_node, preferred_element_type=F32)
        picked = product if picked is None else picked + product
    total = jnp.sum(picked * node_weight, axis=0, keepdims=True)
    half = total.shape[1] // 2
    return total[:, :half] + total[:, half:]


def slots_at_nodes(values, hot_node, node_weight):
    total = None
    for part in split3(node_weight * jnp.concatenate([values, values], axis=1)):
        product = lax.dot_general(
            part, hot_node, (((1,), (1,)), ((), ())), preferred_element_type=F32
        )
        total = product if total is None else total + product
    return total


def as_line(value):
    return jnp.concatenate([value[i : i + 1, :] for i in range(value.shape[0])], axis=1)


def as_rows(line, width):
    return jnp.concatenate(
        [line[:, start : start + width] for start in range(0, line.shape[1], width)], axis=0
    )


def local(
    matrix_source,
    accum,
    faces,
    basis,
    coarse_diag,
    coarse_ratio,
    frac_source,
    frac_accum,
    frac_link,
    frac_trans,
    frac_cell,
    frac_peer,
    frac_count,
):
    slots = frac_source.shape[0]
    cell_rows, cell_cols, depth = matrix_source.shape
    cells = cell_rows * cell_cols
    node_rows, node_cols = cell_rows // BLOCK, cell_cols // BLOCK
    assert node_rows + 4 == TILE and node_cols + 4 == TILE
    assert depth & (depth - 1) == 0 and cell_rows == cell_cols
    depth_bits = depth.bit_length() - 1
    lay_size = lax.axis_size("lay")
    lay_pairs = len([p for p in pair_lists(lay_size) if p])
    layer_rows = 4 * cell_cols
    load_one = (layer_rows + TILE, depth)
    slot_rows = slots // depth
    load_two = (cell_cols + 2 * TILE, depth)
    block = matrix_source.shape

    def is_even(axis):
        return 1 - jnp.bitwise_and(lax.axis_index(axis), 1)

    piece = BLOCK
    pieces = cell_rows // piece

    def kernel_a(basis_hbm, source_hbm, cdiag_hbm, ratio_hbm, basis_ref, source_ref, tile_ref, *refs):
        loads, (cdiag_ref, ratio_ref, sems, small_sems) = refs[:-4], refs[-4:]
        copies = []
        for i in range(pieces):
            part = pl.ds(i * piece, piece)
            copies.append(
                (
                    pltpu.make_async_copy(source_hbm.at[part], source_ref.at[part], sems.at[0, i]),
                    pltpu.make_async_copy(
                        basis_hbm.at[:, part], basis_ref.at[:, part], sems.at[1, i]
                    ),
                )
            )
        small_copies = [
            pltpu.make_async_copy(cdiag_hbm, cdiag_ref, small_sems.at[0]),
            pltpu.make_async_copy(ratio_hbm, ratio_ref, small_sems.at[1]),
        ]
        for pair in copies + [small_copies]:
            for copy in pair:
                copy.start()

        def widen(value):
            lines = jnp.concatenate(
                [
                    jnp.zeros((node_rows, 2), F32),
                    value,
                    jnp.zeros((node_rows, TILE - 2 - node_cols), F32),
                ],
                axis=1,
            )
            edge = jnp.zeros((2, TILE), F32)
            return jnp.concatenate([edge, lines, edge], axis=0)

        def column(x):
            if x % piece == 0:
                for copy in copies[x // piece]:
                    copy.wait()
            return x, source_ref[x], lambda k: basis_ref[k, x]

        tile = restrict_tile((column(x) for x in range(cell_rows)), [], cell_rows, cell_cols)
        for copy in small_copies:
            copy.wait()
        parts = [jnp.zeros((TILE, TILE), F32), widen(cdiag_ref[...])]
        parts = parts + [widen(ratio_ref[d]) for d in range(4)]
        parts.append(jnp.zeros((TILE, LANES - TILE * len(parts)), F32))
        table = jnp.concatenate(parts, axis=1)
        tile = tile + table
        tile_ref[...] = tile
        even = is_even("lay")
        edges = (even * (cell_rows - 1), (1 - even) * (cell_rows - 1))
        for load, edge in zip(loads, edges):
            for k in range(4):
                load[k * cell_cols : (k + 1) * cell_cols, :] = basis_ref[k, edge]
            load[layer_rows:, :LANES] = tile
            load[layer_rows:, LANES:] = jnp.zeros((TILE, depth - LANES), F32)

    outs = [(basis.shape, F32), (block, F32), ((TILE, LANES), F32)] + [(load_one, F32)] * lay_pairs
    basis, matrix_source, tile_own, *loads = run(
        kernel_a,
        outs,
        [
            pltpu.with_memory_space_constraint(value, pltpu.HBM)
            for value in (basis, matrix_source, coarse_diag, coarse_ratio)
        ],
        scratch=(
            pltpu.VMEM(coarse_diag.shape, F32),
            pltpu.VMEM(coarse_ratio.shape, F32),
            pltpu.SemaphoreType.DMA((2, pieces)),
            pltpu.SemaphoreType.DMA((2,)),
        ),
        in_place=(0, 1, 2, 3),
    )
    lay_one = swap_pairs(loads[0], loads[-1], "lay")

    def lay_sides(refs, window):
        even = is_even("lay")
        first = refs[0][window]
        second = refs[1][window] if len(refs) > 1 else jnp.zeros(first.shape, F32)
        return low_high(even, first, second)

    def blk_sides(even_ref, odd_ref, window):
        return low_high(is_even("blk"), even_ref[window], odd_ref[window])

    def kernel_e(tile_ref, basis_ref, *refs):
        got, (join_ref, even_ref, odd_ref) = refs[:-3], refs[-3:]
        low, high = lay_sides(got, (slice(layer_rows, layer_rows + TILE), slice(0, LANES)))
        joined = join_rows(tile_ref[...], low, high)
        join_ref[...] = joined
        even = is_even("blk")
        edges = (even * (cell_cols - 1), (1 - even) * (cell_cols - 1))
        for ref, edge in zip((even_ref, odd_ref), edges):
            for k in range(4):
                for x in range(cell_rows):
                    line = k * cell_rows + x
                    ref[line : line + 1, :] = basis_ref[k, x, pl.ds(edge, 1), :]
            ref[layer_rows:, :LANES] = joined
            ref[layer_rows:, LANES:] = jnp.zeros((TILE, depth - LANES), F32)

    outs = [((TILE, LANES), F32), (load_one, F32), (load_one, F32)]
    joined_one, even_one, odd_one = run(kernel_e, outs, (tile_own, basis, *lay_one))
    blk_one = swap_pairs(even_one, odd_one, "blk")

    def kernel_p(
        faces_ref, accum_ref, basis_ref, cell_ref, link_ref, facc_ref, trans_ref, peer_ref,
        count_ref, diag_ref, scale_ref, row_ref, depth_ref, frac_ref, low_ref, node_ref, weight_ref,
    ):
        slot = iota((1, slots), 1)
        live = (slot < count_ref[0]).astype(F32)
        couple = live * as_line(link_ref[...])
        frac_diag = as_line(facc_ref[...]) + couple
        for j in range(trans_ref.shape[0]):
            frac_diag = frac_diag + trans_ref[j : j + 1, :]
        frac_ref[0:1, :] = couple
        frac_ref[1:2, :] = OMEGA * live / frac_diag
        cell = as_line(cell_ref[...])
        at_row = lax.shift_right_logical(cell, depth_bits)
        at_depth = jnp.bitwise_and(cell, depth - 1)
        hot_row = (iota((cells, slots), 0) == at_row).astype(F32).astype(BF16)
        hot_depth = (iota((depth, slots), 0) == at_depth).astype(F32).astype(BF16)
        row_ref[...] = hot_row
        depth_ref[...] = hot_depth
        linked = scatter_cells(couple, hot_row, hot_depth)
        for x in range(cell_rows):
            diag = accum_ref[x]
            for d in range(6):
                diag = diag + faces_ref[d, x]
            diag = diag + linked[x * cell_cols : (x + 1) * cell_cols, :]
            diag_ref[x] = diag
            scale_ref[x] = OMEGA / diag
        across = lax.shift_right_logical(at_row, cell_cols.bit_length() - 1)
        along = jnp.bitwise_and(at_row, cell_cols - 1)
        line = iota((TILE, slots), 0)
        lane = iota((LANES, slots), 0)
        near = (own_nodes(across) + 2 == line, side_nodes(across) + 2 == line)
        for j, nodes in enumerate((own_nodes(along), side_nodes(along))):
            node_ref[:, j * slots : (j + 1) * slots] = (
                (lane == nodes + 2).astype(F32).astype(BF16)
            )
            total = None
            for i in range(2):
                flat = basis_ref[2 * j + i].reshape(cells, depth)
                part = jnp.where(near[i], gather_cells(flat, hot_row, hot_depth), 0.0)
                total = part if total is None else total + part
            weight_ref[:, j * slots : (j + 1) * slots] = total
        owner = lax.axis_index("blk") * lay_size + lax.axis_index("lay")
        peer = peer_ref[...] - (owner - 1) * slots
        peer = jnp.concatenate([peer[j : j + 1, :] for j in range(peer.shape[0])], axis=1)
        low_ref[...] = (
            (iota((LANES, peer.shape[1]), 0) == jnp.bitwise_and(peer, LANES - 1))
            .astype(F32)
            .astype(BF16)
        )
        frac_ref[2:4, :] = as_rows(lax.shift_right_logical(peer, 7), slots).astype(F32)

    links = frac_trans.shape[0]
    outs = [
        (block, F32),
        (block, F32),
        ((cells, slots), BF16),
        ((depth, slots), BF16),
        ((TILE, slots), F32),
        ((LANES, links * slots), BF16),
        ((LANES, 2 * slots), BF16),
        ((TILE, 2 * slots), F32),
    ]
    small = (slots // LANES, LANES)
    diag, scale, hot_row, hot_depth, frac_pack, hot_low, hot_node, node_weight = run(
        kernel_p,
        outs,
        (
            faces,
            accum,
            basis,
            frac_cell.reshape(small),
            frac_link.reshape(small),
            frac_accum.reshape(small),
            frac_trans,
            frac_peer,
            frac_count,
        ),
        smem=(8,),
    )

    layer = (slice(0, layer_rows), slice(0, depth))

    def rims_of(lay_refs, blk_even, blk_odd):
        lay_low, lay_high = lay_sides(lay_refs, layer)
        blk_low, blk_high = blk_sides(blk_even, blk_odd, layer)

        def pick(value):
            return lambda k: value[k * cell_cols : (k + 1) * cell_cols, :]

        return pick(lay_low), pick(lay_high), pick(blk_low), pick(blk_high)

    def kernel_b(
        faces_ref, basis_ref, source_ref, diag_ref, scale_ref, node_ref, weight_ref, frac_ref,
        fsrc_ref, joined_ref, blk_even, blk_odd, *refs,
    ):
        lay_refs = refs[:lay_pairs]
        p2_ref, f_ref, tile_ref, second_ref = refs[lay_pairs : lay_pairs + 4]
        loads = refs[lay_pairs + 4 : -1]
        p1_ref = refs[-1]
        at_tile = (slice(layer_rows, layer_rows + TILE), slice(0, LANES))
        low, high = blk_sides(blk_even, blk_odd, at_tile)
        table = join_lanes(joined_ref[...], low, high)
        second_ref[...] = table
        second = coarse_solve(table, table)
        fields = Fields(second, cell_rows, cell_cols)
        x_low, x_high, y_low, y_high = rims_of(lay_refs, blk_even, blk_odd)

        def weight(x):
            return lambda k: basis_ref[k, x]

        for x in range(cell_rows):
            p1_ref[x] = fields.column(x, weight(x))
        left_rim = fields.column(-1, x_low)
        right_rim = fields.column(cell_rows, x_high)
        low_rim = fields.row(-1, y_low)
        high_rim = fields.row(cell_cols, y_high)

        couple = frac_ref[0:1, :]
        pressure_at = nodes_at_slots(second, node_ref[...], weight_ref[...])
        fracture = frac_ref[1:2, :] * (as_line(fsrc_ref[...]) + couple * pressure_at)
        f_ref[...] = fracture
        linked = slots_at_nodes(couple * fracture, node_ref[...], weight_ref[...])

        for x in range(cell_rows):
            centre = p1_ref[x]
            left = p1_ref[x - 1] if x else left_rim
            right = p1_ref[x + 1] if x + 1 < cell_rows else right_rim
            around = neighbour_sum(
                faces_ref, x, left, centre, right, low_rim[x : x + 1, :], high_rim[x : x + 1, :]
            )
            p2_ref[x] = (1.0 - OMEGA) * centre + scale_ref[x] * (source_ref[x] + around)

        columns = []
        low_lines, high_lines = [], []
        for x in range(cell_rows):
            centre = p2_ref[x]
            left = p2_ref[x - 1] if x else None
            right = p2_ref[x + 1] if x + 1 < cell_rows else None
            around = neighbour_sum(faces_ref, x, left, centre, right, None, None)
            columns.append((x, source_ref[x] - diag_ref[x] * centre + around, weight(x)))
            low_lines.append(faces_ref[3, x, 0:1, :] * p2_ref[x, 0:1, :])
            high_lines.append(
                faces_ref[2, x, cell_cols - 1 : cell_cols, :]
                * p2_ref[x, cell_cols - 1 : cell_cols, :]
            )
        columns.append((-1, faces_ref[1, 0] * p2_ref[0], x_low))
        last = cell_rows - 1
        columns.append((cell_rows, faces_ref[0, last] * p2_ref[last], x_high))
        rows = [
            (-1, jnp.concatenate(low_lines, axis=0), y_low),
            (cell_cols, jnp.concatenate(high_lines, axis=0), y_high),
        ]
        tile = restrict_tile(columns, rows, cell_rows, cell_cols) + linked
        tile_ref[...] = tile
        even = is_even("lay")
        edges = (even * (cell_rows - 1), (1 - even) * (cell_rows - 1))
        for load, edge in zip(loads, edges):
            load[:cell_cols, :] = p2_ref[edge]
            load[cell_cols : cell_cols + TILE, :LANES] = tile
            load[cell_cols : cell_cols + TILE, LANES:] = jnp.zeros((TILE, depth - LANES), F32)
            load[cell_cols + TILE :, :] = jnp.zeros((TILE, depth), F32)
            load[cell_cols + TILE : cell_cols + TILE + slot_rows, :] = as_rows(fracture, depth)

    outs = [(block, F32), ((1, slots), F32), ((TILE, LANES), F32), ((TILE, LANES), F32)]
    outs = outs + [(load_two, F32)] * lay_pairs
    frac_source_rows = frac_source.reshape(small)
    pressure, fracture, tile_two, second_one, *loads = run(
        kernel_b,
        outs,
        (
            faces, basis, matrix_source, diag, scale, hot_node, node_weight, frac_pack,
            frac_source_rows, joined_one, *blk_one, *lay_one,
        ),
        scratch=(pltpu.VMEM(block, F32),),
    )
    lay_two = swap_pairs(loads[0], loads[-1], "lay")

    tile_rows = (slice(cell_cols, cell_cols + TILE), slice(0, LANES))
    frac_rows = (slice(cell_cols + TILE, cell_cols + TILE + slot_rows), slice(0, depth))

    def kernel_f(tile_ref, p_ref, *refs):
        got, (join_ref, even_ref, odd_ref) = refs[:-3], refs[-3:]
        low, high = lay_sides(got, tile_rows)
        joined = join_rows(tile_ref[...], low, high)
        join_ref[...] = joined
        even = is_even("blk")
        edges = (even * (cell_cols - 1), (1 - even) * (cell_cols - 1))
        for ref, edge in zip((even_ref, odd_ref), edges):
            for x in range(cell_rows):
                ref[x : x + 1, :] = p_ref[x, pl.ds(edge, 1), :]
            ref[cell_cols : cell_cols + TILE, :LANES] = joined
            ref[cell_cols : cell_cols + TILE, LANES:] = jnp.zeros((TILE, depth - LANES), F32)
            ref[cell_cols + TILE :, :] = got[0][cell_cols + TILE :, :]

    outs = [((TILE, LANES), F32), (load_two, F32), (load_two, F32)]
    joined_two, even_two, odd_two = run(kernel_f, outs, (tile_two, pressure, *lay_two))
    blk_two = swap_pairs(even_two, odd_two, "blk")

    def kernel_m(source_ref, p2_ref, f_ref, row_ref, depth_ref, frac_ref, forced_ref, at_ref):
        hot_row, hot_depth = row_ref[...], depth_ref[...]
        linked = scatter_cells(frac_ref[0:1, :] * f_ref[...], hot_row, hot_depth)
        for x in range(cell_rows):
            forced_ref[x] = source_ref[x] + linked[x * cell_cols : (x + 1) * cell_cols, :]
        at_ref[...] = gather_cells(p2_ref[...].reshape(cells, depth), hot_row, hot_depth)

    forced, slot_pressure = run(
        kernel_m,
        [(block, F32), ((1, slots), F32)],
        (matrix_source, pressure, fracture, hot_row, hot_depth, frac_pack),
    )
    ring = []
    if lay_size != 2:
        owners = lax.axis_size("blk") * lay_size
        ahead = [(i, i + 1) for i in range(owners - 1)]
        line = fracture.reshape(slot_rows, depth)
        ring = [
            lax.ppermute(line, ("blk", "lay"), ahead),
            lax.ppermute(line, ("blk", "lay"), [(b, a) for a, b in ahead]),
        ]

    def kernel_c(
        faces_ref, basis_ref, forced_ref, scale_ref, node_ref, weight_ref, frac_ref, low_ref,
        fsrc_ref, trans_ref, p2_ref, f_ref, at_ref, joined_ref, table_ref,
        one_even, one_odd, two_even, two_odd, *refs,
    ):
        lay_first, lay_second = refs[:lay_pairs], refs[lay_pairs : 2 * lay_pairs]
        ring_refs = refs[2 * lay_pairs : -6]
        p_hbm, f_hbm, p3_ref, p_out, f_out, sems = refs[-6:]
        low, high = blk_sides(two_even, two_odd, tile_rows)
        tile = join_lanes(joined_ref[...], low, high)
        second = coarse_solve(tile, table_ref[...])
        fields = Fields(second, cell_rows, cell_cols)
        x_low, x_high, y_low, y_high = rims_of(lay_first, one_even, one_odd)
        window = (slice(0, cell_cols), slice(0, depth))
        p_left, p_right = lay_sides(lay_second, window)
        p_low, p_high = blk_sides(two_even, two_odd, window)

        for x in range(cell_rows):
            p3_ref[x] = p2_ref[x] + fields.column(x, lambda k: basis_ref[k, x])
        left_rim = p_left + fields.column(-1, x_low)
        right_rim = p_right + fields.column(cell_rows, x_high)
        low_rim = p_low + fields.row(-1, y_low)
        high_rim = p_high + fields.row(cell_cols, y_high)
        pressure_at = at_ref[...] + nodes_at_slots(second, node_ref[...], weight_ref[...])
        mine = as_rows(f_ref[...], LANES)
        if ring_refs:
            before, after = ring_refs[0][...], ring_refs[1][...]
        else:
            partner = lay_second[0][frac_rows]
            from_low, from_high = blk_sides(two_even, two_odd, frac_rows)
            before = by_parity(is_even("lay"), from_low, partner)
            after = by_parity(is_even("lay"), partner, from_high)
        width = mine.shape[0]
        wide = jnp.concatenate(
            [as_rows(as_line(before), LANES), mine, as_rows(as_line(after), LANES)]
            + [jnp.zeros((-3 * width % TILE, LANES), F32)] * (3 * width % TILE > 0),
            axis=0,
        )
        peer_high = as_line(frac_ref[2:4, :])
        picked = None
        for part in split3(wide):
            product = jnp.dot(part, low_ref[...], preferred_element_type=F32)
            picked = product if picked is None else picked + product
        match = iota(picked.shape, 0).astype(F32) == peer_high
        peers = jnp.sum(jnp.where(match, picked, 0.0), axis=0, keepdims=True)
        flux = as_line(fsrc_ref[...]) + frac_ref[0:1, :] * pressure_at
        for j in range(links):
            flux = flux + trans_ref[j : j + 1, :] * peers[:, j * slots : (j + 1) * slots]
        result = (1.0 - OMEGA) * f_ref[...] + frac_ref[1:2, :] * flux
        f_out[...] = as_rows(result, LANES)
        copies = []
        for x in range(cell_rows):
            centre = p3_ref[x]
            left = p3_ref[x - 1] if x else left_rim
            right = p3_ref[x + 1] if x + 1 < cell_rows else right_rim
            around = neighbour_sum(
                faces_ref, x, left, centre, right, low_rim[x : x + 1, :], high_rim[x : x + 1, :]
            )
            p_out[x] = (1.0 - OMEGA) * centre + scale_ref[x] * (forced_ref[x] + around)
            if (x + 1) % piece == 0:
                part = pl.ds(x + 1 - piece, piece)
                copies.append(
                    pltpu.make_async_copy(p_out.at[part], p_hbm.at[part], sems.at[x // piece])
                )
                copies[-1].start()
                if x + 1 == 2 * piece:
                    copies.append(pltpu.make_async_copy(f_out, f_hbm, sems.at[pieces]))
                    copies[-1].start()
        for copy in copies:
            copy.wait()

    final, frac_final = run(
        kernel_c,
        [(block, F32), (small, F32)],
        (
            faces, basis, forced, scale, hot_node, node_weight, frac_pack, hot_low,
            frac_source_rows, frac_trans, pressure, fracture, slot_pressure, joined_two, second_one,
            *blk_one, *blk_two, *lay_one, *lay_two, *ring,
        ),
        scratch=(
            pltpu.VMEM(block, F32),
            pltpu.VMEM(block, F32),
            pltpu.VMEM(small, F32),
            pltpu.SemaphoreType.DMA((pieces + 1,)),
        ),
        out_place=(0, 1),
    )
    return final, frac_final.reshape(slots)


def solution(mesh):
    return jax.shard_map(
        local,
        mesh=mesh,
        in_specs=(
            P("lay", "blk", None),
            P("lay", "blk", None),
            P(None, "lay", "blk", None),
            P(None, "lay", "blk", None),
            P("lay", "blk"),
            P(None, "lay", "blk"),
            P(("blk", "lay")),
            P(("blk", "lay")),
            P(("blk", "lay")),
            P(None, ("blk", "lay")),
            P(("blk", "lay")),
            P(None, ("blk", "lay")),
            P(("blk", "lay")),
        ),
        out_specs=(P("lay", "blk", None), P(("blk", "lay"))),
        check_vma=False,
    )
```

```python
import jax
import jax.numpy as jnp
from jax import lax
from jax.experimental import pallas as pl
from jax.experimental.pallas import tpu as pltpu
from jax.sharding import PartitionSpec as P

BLOCK = 4
OMEGA = 0.8
TILE = 8
LANES = 128
F32 = jnp.float32
BF16 = jnp.bfloat16


def pair_lists(count):
    even = [(i, i ^ 1) for i in range(count) if i ^ 1 < count]
    odd = [(i, i + 1 if i % 2 else i - 1) for i in range(1, count)]
    return even, [(a, b) for a, b in odd if 0 < b < count]


def swap_pairs(even_load, odd_load, axis):
    even, odd = pair_lists(lax.axis_size(axis))
    got = [lax.ppermute(even_load, axis, even)]
    if odd:
        got.append(lax.ppermute(odd_load, axis, odd))
    return got


def run(kernel, outs, args, scratch=(), smem=(), in_place=(), out_place=()):
    spec = pl.BlockSpec(memory_space=pltpu.VMEM)
    scalar = pl.BlockSpec(memory_space=pltpu.SMEM)
    there = pl.BlockSpec(memory_space=pltpu.HBM)

    def place(i):
        return scalar if i in smem else there if i in in_place else spec

    return pl.pallas_call(
        kernel,
        out_shape=[jax.ShapeDtypeStruct(shape, dtype) for shape, dtype in outs],
        in_specs=[place(i) for i in range(len(args))],
        out_specs=[there if i in out_place else spec for i in range(len(outs))],
        scratch_shapes=list(scratch),
        compiler_params=pltpu.CompilerParams(vmem_limit_bytes=24 << 20),
    )(*args)


def iota(shape, dim):
    return lax.broadcasted_iota(jnp.int32, shape, dim)


def own_node(cell):
    return cell // BLOCK


def side_node(cell):
    return cell // BLOCK + (-1 if cell % BLOCK < BLOCK // 2 else 1)


def near_terms(x):
    own, near = own_node(x) + 2, side_node(x) + 2
    terms = [(0, 0, own), (1, 0, near), (2, 1, own), (3, 1, near), (4, 2, own), (5, 2, near)]
    if 0 < x % BLOCK < BLOCK - 1:
        terms = terms + [(6, 0, 2 * own - near), (7, 1, 2 * own - near)]
    return terms


def own_nodes(cells):
    return lax.shift_right_arithmetic(cells, 2)


def side_nodes(cells):
    low = jnp.bitwise_and(cells, BLOCK - 1) < BLOCK // 2
    return own_nodes(cells) + jnp.where(low, -1, 1)


def node_masks(cells):
    index = iota((cells, LANES), 0)
    lane = iota((cells, LANES), 1)
    own, side = own_nodes(index) + 2, side_nodes(index) + 2
    return own == lane, side == lane, 2 * own - side == lane


def fold_lanes(value):
    total = value[:, :LANES]
    for start in range(LANES, value.shape[1], LANES):
        total = total + value[:, start : start + LANES]
    return total


def by_parity(is_even, even_value, odd_value):
    return jnp.where(jnp.full(even_value.shape, is_even, jnp.int32) > 0, even_value, odd_value)


def low_high(is_even, even_got, odd_got):
    low = by_parity(is_even, odd_got, even_got)
    high = by_parity(is_even, even_got, odd_got)
    return low, high


def basis_terms(x, residual, weight):
    own, near = own_node(x) + 2, side_node(x) + 2
    nodes = (own, near, own, near)
    return residual, [(k // 2, nodes[k], weight(k)) for k in range(4)]


def restrict_tile(columns, rows, cell_rows, cell_cols):
    sums = {}
    for value, terms in columns:
        for kind, node, weight in terms:
            part = fold_lanes(weight * value)
            key = (kind, node)
            sums[key] = sums[key] + part if key in sums else part
    masks = node_masks(cell_cols)
    row_index = iota((TILE, LANES), 0)
    tile = jnp.zeros((TILE, LANES), F32)
    nodes = sorted({node for _, node in sums})
    wide = {}
    if rows:
        lane = iota((cell_rows, LANES), 1)
        for y, residual, weight in rows():
            for k in range(4):
                node = (own_node(y) if k < 2 else side_node(y)) + 2
                part = jnp.sum(fold_lanes(weight(k) * residual), axis=1, keepdims=True)
                part = jnp.where(lane == node, part, 0.0)
                wide[k % 2] = wide[k % 2] + part if k % 2 in wide else part
        x_index = iota((cell_rows, LANES), 0)
        x_nodes = (own_nodes(x_index) + 2, side_nodes(x_index) + 2)
    for node in nodes:
        total = jnp.zeros((cell_cols, LANES), F32)
        for kind in range(3):
            if (kind, node) in sums:
                lane_sum = jnp.sum(sums[(kind, node)], axis=1, keepdims=True)
                total = total + jnp.where(masks[kind], lane_sum, 0.0)
        line = jnp.sum(total, axis=0, keepdims=True)
        if rows:
            extra = jnp.where(x_nodes[0] == node, wide[0], 0.0) + jnp.where(
                x_nodes[1] == node, wide[1], 0.0
            )
            line = line + jnp.sum(extra, axis=0, keepdims=True)
        tile = jnp.where(row_index == node, line, tile)
    return tile


def join_rows(tile, low, high):
    row = iota((TILE, LANES), 0)
    half = TILE // 2
    return (
        tile
        + jnp.where(row < half, pltpu.roll(low, half, 0), 0.0)
        + jnp.where(row >= half, pltpu.roll(high, half, 0), 0.0)
    )


def join_lanes(tile, low, high):
    part = jnp.bitwise_and(iota((TILE, LANES), 1), TILE - 1)
    half = TILE // 2
    return (
        tile
        + jnp.where(part < half, pltpu.roll(low, LANES - half, 1), 0.0)
        + jnp.where(part >= half, pltpu.roll(high, half, 1), 0.0)
    )


def coarse_parts(table):
    lane = iota((TILE, LANES), 1)
    diag = pltpu.roll(table, LANES - TILE, 1)
    live = (lane < TILE) & (diag > 0.0)
    parts = [jnp.where(live, 1.0 / jnp.where(live, diag, 1.0), 0.0)]
    for direction in range(4):
        ratio = pltpu.roll(table, LANES - TILE * (2 + direction), 1)
        parts.append(jnp.where(lane < TILE, ratio, 0.0))
    return parts


def coarse_solve(tile, parts):
    first = tile * parts[0]
    near = (
        pltpu.roll(first, 1, 0),
        pltpu.roll(first, TILE - 1, 0),
        pltpu.roll(first, 1, 1),
        pltpu.roll(first, LANES - 1, 1),
    )
    second = first
    for direction in range(4):
        second = second + parts[1 + direction] * near[direction]
    return second


class Fields:
    def __init__(self, second, cell_rows, cell_cols):
        masks = node_masks(cell_cols)
        self.columns = {}
        for node in range(1, TILE - 1):
            line = jnp.broadcast_to(second[node : node + 1, :], (cell_cols, LANES))
            for kind in range(3):
                self.columns[(kind, node)] = jnp.sum(
                    jnp.where(masks[kind], line, 0.0), axis=1, keepdims=True
                )
        x_index = iota((cell_rows, LANES), 0)
        self.wide = []
        for nodes in (own_nodes(x_index) + 2, side_nodes(x_index) + 2):
            value = jnp.zeros((cell_rows, LANES), F32)
            for node in range(1, TILE - 1):
                value = jnp.where(nodes == node, second[node : node + 1, :], value)
            self.wide.append(value)

    def column(self, x, weight):
        own, side = own_node(x) + 2, side_node(x) + 2
        return (
            weight(0) * self.columns[(0, own)]
            + weight(1) * self.columns[(0, side)]
            + weight(2) * self.columns[(1, own)]
            + weight(3) * self.columns[(1, side)]
        )

    def terms(self, x, weight):
        total = None
        for table, kind, node in near_terms(x):
            part = weight(table) * self.columns[(kind, node)]
            total = part if total is None else total + part
        return total

    def row(self, y, weight):
        lane = iota(self.wide[0].shape, 1)

        def pick(kind, node):
            return jnp.sum(jnp.where(lane == node, self.wide[kind], 0.0), axis=1, keepdims=True)

        own, side = own_node(y) + 2, side_node(y) + 2
        return (
            weight(0) * pick(0, own)
            + weight(1) * pick(1, own)
            + weight(2) * pick(0, side)
            + weight(3) * pick(1, side)
        )


def shift_rows(value):
    row = iota((TILE, value.shape[1]), 0)
    parts = [value[i : i + TILE, :] for i in range(0, value.shape[0], TILE)]
    up = [pltpu.roll(part, TILE - 1, 0) for part in parts]
    down = [pltpu.roll(part, 1, 0) for part in parts]
    above = [
        jnp.where(row == TILE - 1, end, part) for end, part in zip(up[1:] + [0.0], up)
    ]
    below = [jnp.where(row == 0, end, part) for end, part in zip([0.0] + down[:-1], down)]
    return jnp.concatenate(above, axis=0), jnp.concatenate(below, axis=0)


def neighbour_sum(faces, x, left, centre, right):
    depth = centre.shape[1]
    above, below = shift_rows(centre)
    total = faces[2, x] * above + faces[3, x] * below
    total = total + faces[4, x] * pltpu.roll(centre, depth - 1, 1)
    total = total + faces[5, x] * pltpu.roll(centre, 1, 1)
    if right is not None:
        total = total + faces[0, x] * right
    if left is not None:
        total = total + faces[1, x] * left
    return total


def add_edge_rows(value, low_row, high_row):
    row = iota((TILE, value.shape[1]), 0)
    low = value[:TILE, :] + jnp.where(row == 0, low_row, 0.0)
    high = value[-TILE:, :] + jnp.where(row == TILE - 1, high_row, 0.0)
    return jnp.concatenate([low, value[TILE:-TILE, :], high] if value.shape[0] > 2 * TILE else [low, high], axis=0)


def split3(value):
    high = value.astype(BF16)
    rest = value - high.astype(F32)
    mid = rest.astype(BF16)
    return high, mid, (rest - mid.astype(F32)).astype(BF16)


def stacked(values, count=3):
    return jnp.concatenate([part for value in values for part in split3(value)[:count]], axis=0)


def unstack(product, rows, count=3):
    parts = [product[i : i + rows, :] for i in range(0, product.shape[0], rows)]
    return [sum(parts[i + 1 : i + count], parts[i]) for i in range(0, len(parts), count)]


def gather_cells(fields, hot_row, hot_depth, count=3):
    product = jnp.dot(stacked(fields, count), hot_depth, preferred_element_type=F32)
    at_row = hot_row.astype(F32)
    return [
        jnp.sum(picked * at_row, axis=0, keepdims=True)
        for picked in unstack(product, fields[0].shape[0], count)
    ]


def scatter_cells(values, hot_row, hot_depth):
    spread = jnp.concatenate([hot_row * part for part in split3(values)], axis=0)
    product = lax.dot_general(
        spread, hot_depth, (((1,), (1,)), ((), ())), preferred_element_type=F32
    )
    return unstack(product, hot_row.shape[0])[0]


def nodes_at_slots(second, hot_node, node_weight):
    product = jnp.dot(stacked([second]), hot_node, preferred_element_type=F32)
    picked = unstack(product, TILE)[0]
    total = jnp.sum(picked * node_weight, axis=0, keepdims=True)
    half = total.shape[1] // 2
    return total[:, :half] + total[:, half:]


def slots_at_nodes(values, hot_node, node_weight):
    weighted = node_weight * jnp.concatenate([values, values], axis=1)
    product = lax.dot_general(
        stacked([weighted]), hot_node, (((1,), (1,)), ((), ())), preferred_element_type=F32
    )
    return unstack(product, TILE)[0]


def as_line(value):
    return jnp.concatenate([value[i : i + 1, :] for i in range(value.shape[0])], axis=1)


def as_rows(line, width):
    return jnp.concatenate(
        [line[:, start : start + width] for start in range(0, line.shape[1], width)], axis=0
    )


def local(
    matrix_source,
    accum,
    faces,
    basis,
    coarse_diag,
    coarse_ratio,
    frac_source,
    frac_accum,
    frac_link,
    frac_trans,
    frac_cell,
    frac_peer,
    frac_count,
):
    slots = frac_source.shape[0]
    cell_rows, cell_cols, depth = matrix_source.shape
    cells = cell_rows * cell_cols
    node_rows, node_cols = cell_rows // BLOCK, cell_cols // BLOCK
    assert node_rows + 4 == TILE and node_cols + 4 == TILE
    assert depth & (depth - 1) == 0 and cell_rows == cell_cols
    depth_bits = depth.bit_length() - 1
    lay_size = lax.axis_size("lay")
    lay_pairs = len([p for p in pair_lists(lay_size) if p])
    layer_rows = 4 * cell_cols
    load_one = (layer_rows + TILE, depth)
    slot_rows = slots // depth
    load_two = (cell_cols + 2 * TILE, depth)
    block = matrix_source.shape

    def is_even(axis):
        return 1 - jnp.bitwise_and(lax.axis_index(axis), 1)

    piece = BLOCK
    pieces = cell_rows // piece

    small = (slots // LANES, LANES)
    slot_arrays = [frac_cell.reshape(small)]
    slot_kinds = len(slot_arrays)

    def kernel_a(basis_hbm, source_hbm, cdiag_hbm, ratio_hbm, *refs):
        slot_hbm, refs = refs[:slot_kinds], refs[slot_kinds:]
        (basis_ref, source_ref, tile_ref), refs = refs[:3], refs[3:]
        slot_refs, refs = refs[:slot_kinds], refs[slot_kinds:]
        loads, (cdiag_ref, ratio_ref, sems, small_sems) = refs[:-4], refs[-4:]
        copies = []
        for i in range(pieces):
            part = pl.ds(i * piece, piece)
            copies.append(
                (
                    pltpu.make_async_copy(source_hbm.at[part], source_ref.at[part], sems.at[0, i]),
                    pltpu.make_async_copy(
                        basis_hbm.at[:, part], basis_ref.at[:, part], sems.at[1, i]
                    ),
                )
            )
        small_copies = [
            pltpu.make_async_copy(cdiag_hbm, cdiag_ref, small_sems.at[0]),
            pltpu.make_async_copy(ratio_hbm, ratio_ref, small_sems.at[1]),
        ]
        for i, (there, here) in enumerate(zip(slot_hbm, slot_refs)):
            small_copies.append(pltpu.make_async_copy(there, here, small_sems.at[2 + i]))
        for pair in copies + [small_copies]:
            for copy in pair:
                copy.start()

        def widen(value):
            lines = jnp.concatenate(
                [
                    jnp.zeros((node_rows, 2), F32),
                    value,
                    jnp.zeros((node_rows, TILE - 2 - node_cols), F32),
                ],
                axis=1,
            )
            edge = jnp.zeros((2, TILE), F32)
            return jnp.concatenate([edge, lines, edge], axis=0)

        def column(x):
            if x % piece == 0:
                for copy in copies[x // piece]:
                    copy.wait()
            return basis_terms(x, source_ref[x], lambda k: basis_ref[k, x])

        tile = restrict_tile((column(x) for x in range(cell_rows)), None, cell_rows, cell_cols)
        for copy in small_copies:
            copy.wait()
        parts = [jnp.zeros((TILE, TILE), F32), widen(cdiag_ref[...])]
        parts = parts + [widen(ratio_ref[d]) for d in range(4)]
        parts.append(jnp.zeros((TILE, LANES - TILE * len(parts)), F32))
        table = jnp.concatenate(parts, axis=1)
        tile = tile + table
        tile_ref[...] = tile
        even = is_even("lay")
        edges = (even * (cell_rows - 1), (1 - even) * (cell_rows - 1))
        for load, edge in zip(loads, edges):
            for k in range(4):
                load[k * cell_cols : (k + 1) * cell_cols, :] = basis_ref[k, edge]
            load[layer_rows:, :LANES] = tile
            load[layer_rows:, LANES:] = jnp.zeros((TILE, depth - LANES), F32)

    outs = [(basis.shape, F32), (block, F32), ((TILE, LANES), F32)]
    outs = outs + [(value.shape, value.dtype) for value in slot_arrays]
    outs = outs + [(load_one, F32)] * lay_pairs
    basis, matrix_source, tile_own, *rest = run(
        kernel_a,
        outs,
        [
            pltpu.with_memory_space_constraint(value, pltpu.HBM)
            for value in (basis, matrix_source, coarse_diag, coarse_ratio, *slot_arrays)
        ],
        scratch=(
            pltpu.VMEM(coarse_diag.shape, F32),
            pltpu.VMEM(coarse_ratio.shape, F32),
            pltpu.SemaphoreType.DMA((2, pieces)),
            pltpu.SemaphoreType.DMA((2 + slot_kinds,)),
        ),
        in_place=range(4 + slot_kinds),
    )
    slot_cell, *loads = rest
    slot_source = frac_source.reshape(small)
    lay_one = swap_pairs(loads[0], loads[-1], "lay")

    def lay_sides(refs, window):
        even = is_even("lay")
        first = refs[0][window]
        second = refs[1][window] if len(refs) > 1 else jnp.zeros(first.shape, F32)
        return low_high(even, first, second)

    def blk_sides(even_ref, odd_ref, window):
        return low_high(is_even("blk"), even_ref[window], odd_ref[window])

    def kernel_e(tile_ref, basis_ref, *refs):
        got, (join_ref, even_ref, odd_ref) = refs[:-3], refs[-3:]
        low, high = lay_sides(got, (slice(layer_rows, layer_rows + TILE), slice(0, LANES)))
        joined = join_rows(tile_ref[...], low, high)
        join_ref[...] = joined
        even = is_even("blk")
        edges = (even * (cell_cols - 1), (1 - even) * (cell_cols - 1))
        for ref, edge in zip((even_ref, odd_ref), edges):
            for k in range(4):
                for x in range(cell_rows):
                    line = k * cell_rows + x
                    ref[line : line + 1, :] = basis_ref[k, x, pl.ds(edge, 1), :]
            ref[layer_rows:, :LANES] = joined
            ref[layer_rows:, LANES:] = jnp.zeros((TILE, depth - LANES), F32)

    outs = [((TILE, LANES), F32), (load_one, F32), (load_one, F32)]
    joined_one, even_one, odd_one = run(kernel_e, outs, (tile_own, basis, *lay_one))
    blk_one = swap_pairs(even_one, odd_one, "blk")

    links = frac_trans.shape[0]

    def kernel_p(
        basis_ref, cell_ref, row_ref, depth_ref, node_ref, weight_ref
    ):
        cell = as_line(cell_ref[...])
        at_row = lax.shift_right_logical(cell, depth_bits)
        at_depth = jnp.bitwise_and(cell, depth - 1)
        hot_row = (iota((cells, slots), 0) == at_row).astype(F32).astype(BF16)
        hot_depth = (iota((depth, slots), 0) == at_depth).astype(F32).astype(BF16)
        row_ref[...] = hot_row
        depth_ref[...] = hot_depth
        fields = [basis_ref[k].reshape(cells, depth) for k in range(4)]
        weights = gather_cells(fields, hot_row, hot_depth, 2)
        along = jnp.bitwise_and(at_row, cell_cols - 1)
        across = lax.shift_right_logical(at_row, cell_cols.bit_length() - 1)
        lane = iota((LANES, slots), 0)
        line = iota((TILE, slots), 0)
        match = (own_nodes(across) + 2 == line, side_nodes(across) + 2 == line)
        for j, nodes in enumerate((own_nodes(along), side_nodes(along))):
            part = slice(j * slots, (j + 1) * slots)
            node_ref[:, part] = (lane == nodes + 2).astype(F32).astype(BF16)
            weight_ref[:, part] = jnp.where(match[0], weights[2 * j], 0.0) + jnp.where(
                match[1], weights[2 * j + 1], 0.0
            )

    outs = [
        ((cells, slots), BF16),
        ((depth, slots), BF16),
        ((LANES, 2 * slots), BF16),
        ((TILE, 2 * slots), F32),
    ]
    hot_row, hot_depth, hot_node, node_weight = run(kernel_p, outs, (basis, slot_cell))

    tables = 8

    def kernel_q(
        faces_hbm, accum_hbm, basis_ref, source_ref, row_ref, depth_ref, link_ref, facc_ref,
        trans_ref, count_ref, sface_ref, forward_ref, back_ref, ssource_ref, scale_ref, edge_ref,
        sedge_ref, frac_ref, faces_ref, accum_ref, linked_ref, sems,
    ):
        copies = []
        for i in range(pieces):
            part = pl.ds(i * piece, piece)
            copies.append(
                (
                    pltpu.make_async_copy(accum_hbm.at[part], accum_ref.at[part], sems.at[0, i]),
                    pltpu.make_async_copy(
                        faces_hbm.at[:, part], faces_ref.at[:, part], sems.at[1, i]
                    ),
                )
            )
        for pair in copies:
            for copy in pair:
                copy.start()
        live = (iota((1, slots), 1) < count_ref[0]).astype(F32)
        couple = live * as_line(link_ref[...])
        frac_diag = as_line(facc_ref[...]) + couple
        for j in range(links):
            frac_diag = frac_diag + trans_ref[j : j + 1, :]
        frac_ref[0:1, :] = couple
        frac_ref[1:2, :] = OMEGA * live / frac_diag
        linked_ref[...] = scatter_cells(couple, row_ref[...], depth_ref[...])

        lane = iota((cell_cols, depth), 1)
        place = jnp.bitwise_and(iota((cell_cols, depth), 0), BLOCK - 1)
        for x in range(cell_rows):
            if x % piece == 0:
                for copy in copies[x // piece]:
                    copy.wait()
            diag = accum_ref[x] + linked_ref[x * cell_cols : (x + 1) * cell_cols, :]
            for d in range(6):
                diag = diag + faces_ref[d, x]
            scale = OMEGA / diag
            scale_ref[x] = scale
            ssource_ref[x] = scale * source_ref[x]
            deep = jnp.where(lane < depth - 1, faces_ref[4, x], 0.0)
            shallow = jnp.where(lane > 0, faces_ref[5, x], 0.0)
            for d in range(4):
                sface_ref[d, x] = scale * faces_ref[d, x]
            sface_ref[4, x] = scale * deep
            sface_ref[5, x] = scale * shallow
            near = {}
            for k in range(4):
                value = basis_ref[k, x]
                near[k] = (
                    deep * pltpu.roll(value, depth - 1, 1)
                    + shallow * pltpu.roll(value, 1, 1)
                    - diag * value
                )
            for i in range(2):
                own_up, own_down = shift_rows(basis_ref[i, x])
                side_up, side_down = shift_rows(basis_ref[2 + i, x])
                far = None
                for face, own, side, swap_at, far_at in (
                    (faces_ref[3, x], own_down, side_down, 0, BLOCK // 2),
                    (faces_ref[2, x], own_up, side_up, BLOCK - 1, BLOCK // 2 - 1),
                ):
                    own, side = face * own, face * side
                    swap, beyond = place == swap_at, place == far_at
                    near[i] = near[i] + jnp.where(swap, side, own)
                    near[2 + i] = near[2 + i] + jnp.where(
                        swap, own, jnp.where(beyond, 0.0, side)
                    )
                    far = jnp.where(beyond, side, 0.0 if far is None else far)
                near[4 + i] = far
            nodes = (own_node(x), side_node(x), 2 * own_node(x) - side_node(x))
            for other, d in ((x - 1, 1), (x + 1, 0)):
                if not 0 <= other < cell_rows:
                    continue
                face = faces_ref[d, x]
                for i, node in enumerate((own_node(other), side_node(other))):
                    kind = nodes.index(node)
                    for j in range(2):
                        table = kind + 2 * j if kind < 2 else 6 + j
                        part = face * basis_ref[2 * j + i, other]
                        near[table] = near[table] + part if table in near else part
            for table, _, _ in near_terms(x):
                back_ref[table, x] = near[table]
                value = scale * near[table]
                forward_ref[table, x] = basis_ref[table, x] + value if table < 4 else value
            edge_ref[2, x : x + 1, :] = faces_ref[3, x, 0:1, :]
            edge_ref[3, x : x + 1, :] = faces_ref[2, x, cell_cols - 1 : cell_cols, :]
            sedge_ref[0, x : x + 1, :] = sface_ref[3, x, 0:1, :]
            sedge_ref[1, x : x + 1, :] = sface_ref[2, x, cell_cols - 1 : cell_cols, :]
        edge_ref[0] = faces_ref[1, 0]
        edge_ref[1] = faces_ref[0, cell_rows - 1]

    outs = [
        (faces.shape, F32),
        ((tables, *block), F32),
        ((tables, *block), F32),
        (block, F32),
        (block, F32),
        ((4, cell_cols, depth), F32),
        ((2, cell_rows, depth), F32),
        ((TILE, slots), F32),
    ]
    sfaces, forward, back, ssource, scale, edge_faces, sedges, frac_pack = run(
        kernel_q,
        outs,
        (
            pltpu.with_memory_space_constraint(faces, pltpu.HBM),
            pltpu.with_memory_space_constraint(accum, pltpu.HBM),
            basis,
            matrix_source,
            hot_row,
            hot_depth,
            frac_link.reshape(small),
            frac_accum.reshape(small),
            frac_trans,
            frac_count,
        ),
        smem=(9,),
        scratch=(
            pltpu.VMEM(faces.shape, F32),
            pltpu.VMEM(block, F32),
            pltpu.VMEM((cells, depth), F32),
            pltpu.SemaphoreType.DMA((2, pieces)),
        ),
        in_place=(0, 1),
    )

    layer = (slice(0, layer_rows), slice(0, depth))

    def rims_of(lay_refs, blk_even, blk_odd):
        lay_low, lay_high = lay_sides(lay_refs, layer)
        blk_low, blk_high = blk_sides(blk_even, blk_odd, layer)

        def pick(value):
            return lambda k: value[k * cell_cols : (k + 1) * cell_cols, :]

        return pick(lay_low), pick(lay_high), pick(blk_low), pick(blk_high)

    last = cell_rows - 1

    def kernel_b(
        sface_ref, forward_ref, back_ref, ssource_ref, edge_ref, sedge_ref, node_ref, weight_ref,
        frac_ref, fsrc_ref, own_ref, joined_ref, blk_even, blk_odd, *refs,
    ):
        lay_refs = refs[:lay_pairs]
        p2_ref, rows_ref, f_ref, tile_ref, parts_ref = refs[lay_pairs : lay_pairs + 5]
        loads = refs[lay_pairs + 5 :]
        at_tile = (slice(layer_rows, layer_rows + TILE), slice(0, LANES))
        low, high = blk_sides(blk_even, blk_odd, at_tile)
        table = join_lanes(joined_ref[...], low, high)
        parts = coarse_parts(table)
        for i, part in enumerate(parts):
            parts_ref[i] = part
        second = coarse_solve(table, parts)
        fields = Fields(second, cell_rows, cell_cols)
        x_low, x_high, y_low, y_high = rims_of(lay_refs, blk_even, blk_odd)
        left_rim = sface_ref[1, 0] * fields.column(-1, x_low)
        right_rim = sface_ref[0, last] * fields.column(cell_rows, x_high)
        low_rim = sedge_ref[0] * fields.row(-1, y_low)
        high_rim = sedge_ref[1] * fields.row(cell_cols, y_high)

        couple = frac_ref[0:1, :]
        pressure_at = nodes_at_slots(second, node_ref[...], weight_ref[...])
        fracture = frac_ref[1:2, :] * (as_line(fsrc_ref[...]) + couple * pressure_at)
        f_ref[...] = fracture
        linked = slots_at_nodes(couple * fracture, node_ref[...], weight_ref[...])

        def columns():
            for x in range(cell_rows):
                value = ssource_ref[x] + fields.terms(x, lambda t: forward_ref[t, x])
                if x == 0:
                    value = value + left_rim
                if x == last:
                    value = value + right_rim
                value = add_edge_rows(value, low_rim[x : x + 1, :], high_rim[x : x + 1, :])
                p2_ref[x] = value
                rows_ref[0, x : x + 1, :] = value[0:1, :]
                rows_ref[1, x : x + 1, :] = value[cell_cols - 1 : cell_cols, :]
                if x == 0:
                    yield basis_terms(-1, edge_ref[0] * value, x_low)
                if x == last:
                    yield basis_terms(cell_rows, edge_ref[1] * value, x_high)
                yield value, [(kind, node, back_ref[t, x]) for t, kind, node in near_terms(x)]

        def rows():
            yield -1, edge_ref[2] * rows_ref[0], y_low
            yield cell_cols, edge_ref[3] * rows_ref[1], y_high

        tile = restrict_tile(columns(), rows, cell_rows, cell_cols) + linked
        tile = tile + jnp.where(iota((TILE, LANES), 1) < TILE, own_ref[...], 0.0)
        tile_ref[...] = tile
        even = is_even("lay")
        edges = (even * last, (1 - even) * last)
        for load, edge in zip(loads, edges):
            load[:cell_cols, :] = p2_ref[edge]
            load[cell_cols : cell_cols + TILE, :LANES] = tile
            load[cell_cols : cell_cols + TILE, LANES:] = jnp.zeros((TILE, depth - LANES), F32)
            load[cell_cols + TILE :, :] = jnp.zeros((TILE, depth), F32)
            load[cell_cols + TILE : cell_cols + TILE + slot_rows, :] = as_rows(fracture, depth)

    parts_shape = (5, TILE, LANES)
    row_pair = (2, cell_rows, depth)
    outs = [(block, F32), (row_pair, F32), ((1, slots), F32), ((TILE, LANES), F32)]
    outs = outs + [(parts_shape, F32)] + [(load_two, F32)] * lay_pairs
    pressure, edge_rows, fracture, tile_two, coarse, *loads = run(
        kernel_b,
        outs,
        (
            sfaces, forward, back, ssource, edge_faces, sedges, hot_node, node_weight,
            frac_pack, slot_source, tile_own, joined_one, *blk_one, *lay_one,
        ),
    )
    lay_two = swap_pairs(loads[0], loads[-1], "lay")

    tile_rows = (slice(cell_cols, cell_cols + TILE), slice(0, LANES))
    frac_rows = (slice(cell_cols + TILE, cell_cols + TILE + slot_rows), slice(0, depth))

    def kernel_f(tile_ref, rows_ref, *refs):
        got, (join_ref, even_ref, odd_ref) = refs[:-3], refs[-3:]
        low, high = lay_sides(got, tile_rows)
        joined = join_rows(tile_ref[...], low, high)
        join_ref[...] = joined
        even = is_even("blk")
        even_ref[:cell_cols, :] = rows_ref[even]
        odd_ref[:cell_cols, :] = rows_ref[1 - even]
        for ref in (even_ref, odd_ref):
            ref[cell_cols : cell_cols + TILE, :LANES] = joined
            ref[cell_cols : cell_cols + TILE, LANES:] = jnp.zeros((TILE, depth - LANES), F32)
            ref[cell_cols + TILE :, :] = got[0][cell_cols + TILE :, :]

    outs = [((TILE, LANES), F32), (load_two, F32), (load_two, F32)]
    joined_two, even_two, odd_two = run(kernel_f, outs, (tile_two, edge_rows, *lay_two))
    blk_two = swap_pairs(even_two, odd_two, "blk")

    def kernel_m(
        sface_ref, ssource_ref, scale_ref, p2_ref, f_ref, row_ref, depth_ref, frac_ref, peer_ref,
        base_ref, at_ref, high_ref, low_ref,
    ):
        owner = lax.axis_index("blk") * lay_size + lax.axis_index("lay")
        peer = as_line(peer_ref[...] - (owner - 1) * slots)
        low_ref[...] = (
            (iota((LANES, peer.shape[1]), 0) == jnp.bitwise_and(peer, LANES - 1))
            .astype(F32)
            .astype(BF16)
        )
        high_ref[...] = lax.shift_right_logical(peer, 7)
        hot_row, hot_depth = row_ref[...], depth_ref[...]
        flat = p2_ref[...].reshape(cells, depth)
        at_ref[...] = gather_cells([flat], hot_row, hot_depth)[0]
        linked = scatter_cells(frac_ref[0:1, :] * f_ref[...], hot_row, hot_depth)
        for x in range(cell_rows):
            centre = p2_ref[x]
            left = p2_ref[x - 1] if x else None
            right = p2_ref[x + 1] if x < last else None
            around = neighbour_sum(sface_ref, x, left, centre, right)
            part = linked[x * cell_cols : (x + 1) * cell_cols, :]
            base_ref[x] = ssource_ref[x] + scale_ref[x] * part + (1.0 - OMEGA) * centre + around

    outs = [
        (block, F32),
        ((1, slots), F32),
        ((1, links * slots), jnp.int32),
        ((LANES, links * slots), BF16),
    ]
    base, slot_pressure, peer_high, hot_low = run(
        kernel_m,
        outs,
        (sfaces, ssource, scale, pressure, fracture, hot_row, hot_depth, frac_pack, frac_peer),
    )
    ring = []
    if lay_size != 2:
        owners = lax.axis_size("blk") * lay_size
        ahead = [(i, i + 1) for i in range(owners - 1)]
        line = fracture.reshape(slot_rows, depth)
        ring = [
            lax.ppermute(line, ("blk", "lay"), ahead),
            lax.ppermute(line, ("blk", "lay"), [(b, a) for a, b in ahead]),
        ]

    def kernel_c(
        sface_ref, forward_ref, base_ref, sedge_ref, node_ref, weight_ref, frac_ref, high_ref,
        low_ref, fsrc_ref, trans_ref, f_ref, at_ref, joined_ref, parts_ref,
        one_even, one_odd, two_even, two_odd, *refs,
    ):
        lay_first, lay_second = refs[:lay_pairs], refs[lay_pairs : 2 * lay_pairs]
        ring_refs = refs[2 * lay_pairs : -5]
        p_hbm, f_hbm, p_out, f_out, sems = refs[-5:]
        low, high = blk_sides(two_even, two_odd, tile_rows)
        tile = join_lanes(joined_ref[...], low, high)
        second = coarse_solve(tile, [parts_ref[i] for i in range(5)])
        fields = Fields(second, cell_rows, cell_cols)
        x_low, x_high, y_low, y_high = rims_of(lay_first, one_even, one_odd)
        window = (slice(0, cell_cols), slice(0, depth))
        p_left, p_right = lay_sides(lay_second, window)
        p_low, p_high = blk_sides(two_even, two_odd, window)

        left_rim = sface_ref[1, 0] * (p_left + fields.column(-1, x_low))
        right_rim = sface_ref[0, last] * (p_right + fields.column(cell_rows, x_high))
        low_rim = sedge_ref[0] * (p_low + fields.row(-1, y_low))
        high_rim = sedge_ref[1] * (p_high + fields.row(cell_cols, y_high))
        pressure_at = at_ref[...] + nodes_at_slots(second, node_ref[...], weight_ref[...])
        mine = as_rows(f_ref[...], LANES)
        if ring_refs:
            before, after = ring_refs[0][...], ring_refs[1][...]
        else:
            partner = lay_second[0][frac_rows]
            from_low, from_high = blk_sides(two_even, two_odd, frac_rows)
            before = by_parity(is_even("lay"), from_low, partner)
            after = by_parity(is_even("lay"), partner, from_high)
        width = mine.shape[0]
        wide = jnp.concatenate(
            [as_rows(as_line(before), LANES), mine, as_rows(as_line(after), LANES)]
            + [jnp.zeros((-3 * width % TILE, LANES), F32)] * (3 * width % TILE > 0),
            axis=0,
        )
        product = jnp.dot(stacked([wide]), low_ref[...], preferred_element_type=F32)
        picked = unstack(product, wide.shape[0])[0]
        match = iota(picked.shape, 0) == high_ref[...]
        peers = jnp.sum(jnp.where(match, picked, 0.0), axis=0, keepdims=True)
        flux = as_line(fsrc_ref[...]) + frac_ref[0:1, :] * pressure_at
        for j in range(links):
            flux = flux + trans_ref[j : j + 1, :] * peers[:, j * slots : (j + 1) * slots]
        result = (1.0 - OMEGA) * f_ref[...] + frac_ref[1:2, :] * flux
        copies = []
        for x in range(cell_rows):
            value = base_ref[x] + fields.terms(x, lambda t: forward_ref[t, x])
            if x == 0:
                value = value + left_rim
            if x == last:
                value = value + right_rim
            p_out[x] = add_edge_rows(value, low_rim[x : x + 1, :], high_rim[x : x + 1, :])
            if (x + 1) % piece == 0:
                part = pl.ds(x + 1 - piece, piece)
                copies.append(
                    pltpu.make_async_copy(p_out.at[part], p_hbm.at[part], sems.at[x // piece])
                )
                copies[-1].start()
        f_out[...] = as_rows(result, LANES)
        copies.append(pltpu.make_async_copy(f_out, f_hbm, sems.at[pieces]))
        copies[-1].start()
        for copy in copies:
            copy.wait()

    final, frac_final = run(
        kernel_c,
        [(block, F32), (small, F32)],
        (
            sfaces, forward, base, sedges, hot_node, node_weight, frac_pack, peer_high,
            hot_low, slot_source, frac_trans, fracture, slot_pressure, joined_two, coarse,
            *blk_one, *blk_two, *lay_one, *lay_two, *ring,
        ),
        scratch=(
            pltpu.VMEM(block, F32),
            pltpu.VMEM(small, F32),
            pltpu.SemaphoreType.DMA((pieces + 1,)),
        ),
        out_place=(0, 1),
    )
    return final, frac_final.reshape(slots)


def solution(mesh):
    return jax.shard_map(
        local,
        mesh=mesh,
        in_specs=(
            P("lay", "blk", None),
            P("lay", "blk", None),
            P(None, "lay", "blk", None),
            P(None, "lay", "blk", None),
            P("lay", "blk"),
            P(None, "lay", "blk"),
            P(("blk", "lay")),
            P(("blk", "lay")),
            P(("blk", "lay")),
            P(None, ("blk", "lay")),
            P(("blk", "lay")),
            P(None, ("blk", "lay")),
            P(("blk", "lay")),
        ),
        out_specs=(P("lay", "blk", None), P(("blk", "lay"))),
        check_vma=False,
    )
```

```python
import jax
import jax.numpy as jnp
from jax import lax
from jax.experimental import pallas as pl
from jax.experimental.pallas import tpu as pltpu
from jax.sharding import PartitionSpec as P

BLOCK = 4
OMEGA = 0.8
TILE = 8
LANES = 128
F32 = jnp.float32
BF16 = jnp.bfloat16


def pair_lists(count):
    even = [(i, i ^ 1) for i in range(count) if i ^ 1 < count]
    odd = [(i, i + 1 if i % 2 else i - 1) for i in range(1, count)]
    return even, [(a, b) for a, b in odd if 0 < b < count]


def swap_pairs(even_load, odd_load, axis):
    even, odd = pair_lists(lax.axis_size(axis))
    got = [lax.ppermute(even_load, axis, even)]
    if odd:
        got.append(lax.ppermute(odd_load, axis, odd))
    return got


def run(kernel, outs, args, scratch=(), smem=(), in_place=(), out_place=()):
    spec = pl.BlockSpec(memory_space=pltpu.VMEM)
    scalar = pl.BlockSpec(memory_space=pltpu.SMEM)
    there = pl.BlockSpec(memory_space=pltpu.HBM)

    def place(i):
        return scalar if i in smem else there if i in in_place else spec

    return pl.pallas_call(
        kernel,
        out_shape=[jax.ShapeDtypeStruct(shape, dtype) for shape, dtype in outs],
        in_specs=[place(i) for i in range(len(args))],
        out_specs=[there if i in out_place else spec for i in range(len(outs))],
        scratch_shapes=list(scratch),
        compiler_params=pltpu.CompilerParams(vmem_limit_bytes=24 << 20),
    )(*args)


def iota(shape, dim):
    return lax.broadcasted_iota(jnp.int32, shape, dim)


def own_node(cell):
    return cell // BLOCK


def side_node(cell):
    return cell // BLOCK + (-1 if cell % BLOCK < BLOCK // 2 else 1)


def near_terms(x):
    own, near = own_node(x) + 2, side_node(x) + 2
    terms = [(0, 0, own), (1, 0, near), (2, 1, own), (3, 1, near), (4, 2, own), (5, 2, near)]
    if 0 < x % BLOCK < BLOCK - 1:
        terms = terms + [(6, 0, 2 * own - near), (7, 1, 2 * own - near)]
    return terms


def own_nodes(cells):
    return lax.shift_right_arithmetic(cells, 2)


def side_nodes(cells):
    low = jnp.bitwise_and(cells, BLOCK - 1) < BLOCK // 2
    return own_nodes(cells) + jnp.where(low, -1, 1)


def node_masks(cells):
    index = iota((cells, LANES), 0)
    lane = iota((cells, LANES), 1)
    own, side = own_nodes(index) + 2, side_nodes(index) + 2
    return own == lane, side == lane, 2 * own - side == lane


def fold_lanes(value):
    total = value[:, :LANES]
    for start in range(LANES, value.shape[1], LANES):
        total = total + value[:, start : start + LANES]
    return total


def by_parity(is_even, even_value, odd_value):
    return jnp.where(jnp.full(even_value.shape, is_even, jnp.int32) > 0, even_value, odd_value)


def low_high(is_even, even_got, odd_got):
    low = by_parity(is_even, odd_got, even_got)
    high = by_parity(is_even, even_got, odd_got)
    return low, high


def basis_terms(x, residual, weight):
    own, near = own_node(x) + 2, side_node(x) + 2
    nodes = (own, near, own, near)
    return residual, [(k // 2, nodes[k], weight(k)) for k in range(4)]


def restrict_tile(columns, rows, cell_rows, cell_cols):
    sums = {}
    for value, terms in columns:
        for kind, node, weight in terms:
            part = fold_lanes(weight * value)
            key = (kind, node)
            sums[key] = sums[key] + part if key in sums else part
    masks = node_masks(cell_cols)
    row_index = iota((TILE, LANES), 0)
    tile = jnp.zeros((TILE, LANES), F32)
    nodes = sorted({node for _, node in sums})
    wide = {}
    if rows:
        lane = iota((cell_rows, LANES), 1)
        for y, residual, weight in rows():
            for k in range(4):
                node = (own_node(y) if k < 2 else side_node(y)) + 2
                part = jnp.sum(fold_lanes(weight(k) * residual), axis=1, keepdims=True)
                part = jnp.where(lane == node, part, 0.0)
                wide[k % 2] = wide[k % 2] + part if k % 2 in wide else part
        x_index = iota((cell_rows, LANES), 0)
        x_nodes = (own_nodes(x_index) + 2, side_nodes(x_index) + 2)
    for node in nodes:
        total = jnp.zeros((cell_cols, LANES), F32)
        for kind in range(3):
            if (kind, node) in sums:
                lane_sum = jnp.sum(sums[(kind, node)], axis=1, keepdims=True)
                total = total + jnp.where(masks[kind], lane_sum, 0.0)
        line = jnp.sum(total, axis=0, keepdims=True)
        if rows:
            extra = jnp.where(x_nodes[0] == node, wide[0], 0.0) + jnp.where(
                x_nodes[1] == node, wide[1], 0.0
            )
            line = line + jnp.sum(extra, axis=0, keepdims=True)
        tile = jnp.where(row_index == node, line, tile)
    return tile


def join_rows(tile, low, high):
    row = iota((TILE, LANES), 0)
    half = TILE // 2
    return (
        tile
        + jnp.where(row < half, pltpu.roll(low, half, 0), 0.0)
        + jnp.where(row >= half, pltpu.roll(high, half, 0), 0.0)
    )


def join_lanes(tile, low, high):
    part = jnp.bitwise_and(iota((TILE, LANES), 1), TILE - 1)
    half = TILE // 2
    return (
        tile
        + jnp.where(part < half, pltpu.roll(low, LANES - half, 1), 0.0)
        + jnp.where(part >= half, pltpu.roll(high, half, 1), 0.0)
    )


def coarse_parts(table):
    lane = iota((TILE, LANES), 1)
    diag = pltpu.roll(table, LANES - TILE, 1)
    live = (lane < TILE) & (diag > 0.0)
    parts = [jnp.where(live, 1.0 / jnp.where(live, diag, 1.0), 0.0)]
    for direction in range(4):
        ratio = pltpu.roll(table, LANES - TILE * (2 + direction), 1)
        parts.append(jnp.where(lane < TILE, ratio, 0.0))
    return parts


def coarse_solve(tile, parts):
    first = tile * parts[0]
    near = (
        pltpu.roll(first, 1, 0),
        pltpu.roll(first, TILE - 1, 0),
        pltpu.roll(first, 1, 1),
        pltpu.roll(first, LANES - 1, 1),
    )
    second = first
    for direction in range(4):
        second = second + parts[1 + direction] * near[direction]
    return second


class Fields:
    def __init__(self, second, cell_rows, cell_cols):
        masks = node_masks(cell_cols)
        self.columns = {}
        for node in range(1, TILE - 1):
            line = jnp.broadcast_to(second[node : node + 1, :], (cell_cols, LANES))
            for kind in range(3):
                self.columns[(kind, node)] = jnp.sum(
                    jnp.where(masks[kind], line, 0.0), axis=1, keepdims=True
                )
        x_index = iota((cell_rows, LANES), 0)
        self.wide = []
        for nodes in (own_nodes(x_index) + 2, side_nodes(x_index) + 2):
            value = jnp.zeros((cell_rows, LANES), F32)
            for node in range(1, TILE - 1):
                value = jnp.where(nodes == node, second[node : node + 1, :], value)
            self.wide.append(value)

    def column(self, x, weight):
        own, side = own_node(x) + 2, side_node(x) + 2
        return (
            weight(0) * self.columns[(0, own)]
            + weight(1) * self.columns[(0, side)]
            + weight(2) * self.columns[(1, own)]
            + weight(3) * self.columns[(1, side)]
        )

    def terms(self, x, weight):
        total = None
        for table, kind, node in near_terms(x):
            part = weight(table) * self.columns[(kind, node)]
            total = part if total is None else total + part
        return total

    def row(self, y, weight):
        lane = iota(self.wide[0].shape, 1)

        def pick(kind, node):
            return jnp.sum(jnp.where(lane == node, self.wide[kind], 0.0), axis=1, keepdims=True)

        own, side = own_node(y) + 2, side_node(y) + 2
        return (
            weight(0) * pick(0, own)
            + weight(1) * pick(1, own)
            + weight(2) * pick(0, side)
            + weight(3) * pick(1, side)
        )


def shift_rows(value):
    row = iota((TILE, value.shape[1]), 0)
    parts = [value[i : i + TILE, :] for i in range(0, value.shape[0], TILE)]
    up = [pltpu.roll(part, TILE - 1, 0) for part in parts]
    down = [pltpu.roll(part, 1, 0) for part in parts]
    above = [
        jnp.where(row == TILE - 1, end, part) for end, part in zip(up[1:] + [0.0], up)
    ]
    below = [jnp.where(row == 0, end, part) for end, part in zip([0.0] + down[:-1], down)]
    return jnp.concatenate(above, axis=0), jnp.concatenate(below, axis=0)


def neighbour_sum(faces, x, left, centre, right):
    depth = centre.shape[1]
    above, below = shift_rows(centre)
    total = faces[2, x] * above + faces[3, x] * below
    total = total + faces[4, x] * pltpu.roll(centre, depth - 1, 1)
    total = total + faces[5, x] * pltpu.roll(centre, 1, 1)
    if right is not None:
        total = total + faces[0, x] * right
    if left is not None:
        total = total + faces[1, x] * left
    return total


def add_edge_rows(value, low_row, high_row):
    row = iota((TILE, value.shape[1]), 0)
    low = value[:TILE, :] + jnp.where(row == 0, low_row, 0.0)
    high = value[-TILE:, :] + jnp.where(row == TILE - 1, high_row, 0.0)
    return jnp.concatenate([low, value[TILE:-TILE, :], high] if value.shape[0] > 2 * TILE else [low, high], axis=0)


def split3(value):
    high = value.astype(BF16)
    rest = value - high.astype(F32)
    mid = rest.astype(BF16)
    return high, mid, (rest - mid.astype(F32)).astype(BF16)


def stacked(values, count=3):
    return jnp.concatenate([part for value in values for part in split3(value)[:count]], axis=0)


def unstack(product, rows, count=3):
    parts = [product[i : i + rows, :] for i in range(0, product.shape[0], rows)]
    return [sum(parts[i + 1 : i + count], parts[i]) for i in range(0, len(parts), count)]


def gather_cells(fields, hot_row, hot_depth, count=3):
    product = jnp.dot(stacked(fields, count), hot_depth, preferred_element_type=F32)
    at_row = hot_row.astype(F32)
    return [
        jnp.sum(picked * at_row, axis=0, keepdims=True)
        for picked in unstack(product, fields[0].shape[0], count)
    ]


def scatter_cells(values, hot_row, hot_depth):
    spread = jnp.concatenate([hot_row * part for part in split3(values)], axis=0)
    product = lax.dot_general(
        spread, hot_depth, (((1,), (1,)), ((), ())), preferred_element_type=F32
    )
    return unstack(product, hot_row.shape[0])[0]


def nodes_at_slots(second, hot_node, node_weight):
    product = jnp.dot(stacked([second]), hot_node, preferred_element_type=F32)
    picked = unstack(product, TILE)[0]
    total = jnp.sum(picked * node_weight, axis=0, keepdims=True)
    half = total.shape[1] // 2
    return total[:, :half] + total[:, half:]


def slots_at_nodes(values, hot_node, node_weight):
    weighted = node_weight * jnp.concatenate([values, values], axis=1)
    product = lax.dot_general(
        stacked([weighted]), hot_node, (((1,), (1,)), ((), ())), preferred_element_type=F32
    )
    return unstack(product, TILE)[0]


def as_line(value):
    return jnp.concatenate([value[i : i + 1, :] for i in range(value.shape[0])], axis=1)


def pack_slots(tile, line):
    rows = as_rows(line, LANES)
    wide = jnp.concatenate([pltpu.roll(rows, LANES // 2, 1), rows], axis=0)
    return jnp.where(iota((TILE, LANES), 1) < LANES // 2, tile, wide)


def unpack_slots(tile):
    half = TILE // 2
    low = iota((half, LANES), 1) < LANES // 2
    return jnp.where(low, pltpu.roll(tile[:half, :], LANES // 2, 1), tile[half:, :])


def as_rows(line, width):
    return jnp.concatenate(
        [line[:, start : start + width] for start in range(0, line.shape[1], width)], axis=0
    )


def local(
    matrix_source,
    accum,
    faces,
    basis,
    coarse_diag,
    coarse_ratio,
    frac_source,
    frac_accum,
    frac_link,
    frac_trans,
    frac_cell,
    frac_peer,
    frac_count,
):
    slots = frac_source.shape[0]
    cell_rows, cell_cols, depth = matrix_source.shape
    cells = cell_rows * cell_cols
    node_rows, node_cols = cell_rows // BLOCK, cell_cols // BLOCK
    assert node_rows + 4 == TILE and node_cols + 4 == TILE
    assert depth & (depth - 1) == 0 and cell_rows == cell_cols
    depth_bits = depth.bit_length() - 1
    lay_size = lax.axis_size("lay")
    lay_pairs = len([p for p in pair_lists(lay_size) if p])
    spans = [slice(start, start + LANES) for start in range(0, depth, LANES)]
    layer_rows = 4 * len(spans) * cell_cols
    load_one = (layer_rows + TILE, LANES)
    edge_size = len(spans) * cell_cols
    load_two = (edge_size + TILE, LANES)
    assert slots == TILE * LANES // 2
    block = matrix_source.shape

    def is_even(axis):
        return 1 - jnp.bitwise_and(lax.axis_index(axis), 1)

    piece = BLOCK
    pieces = cell_rows // piece

    small = (slots // LANES, LANES)
    slot_arrays = [frac_cell.reshape(small)]
    slot_kinds = len(slot_arrays)

    def kernel_a(basis_hbm, source_hbm, cdiag_hbm, ratio_hbm, *refs):
        slot_hbm, refs = refs[:slot_kinds], refs[slot_kinds:]
        (basis_ref, source_ref, tile_ref), refs = refs[:3], refs[3:]
        slot_refs, refs = refs[:slot_kinds], refs[slot_kinds:]
        loads, (cdiag_ref, ratio_ref, sems, small_sems) = refs[:-4], refs[-4:]
        copies = []
        for i in range(pieces):
            part = pl.ds(i * piece, piece)
            copies.append(
                (
                    pltpu.make_async_copy(source_hbm.at[part], source_ref.at[part], sems.at[0, i]),
                    pltpu.make_async_copy(
                        basis_hbm.at[:, part], basis_ref.at[:, part], sems.at[1, i]
                    ),
                )
            )
        small_copies = [
            pltpu.make_async_copy(cdiag_hbm, cdiag_ref, small_sems.at[0]),
            pltpu.make_async_copy(ratio_hbm, ratio_ref, small_sems.at[1]),
        ]
        for i, (there, here) in enumerate(zip(slot_hbm, slot_refs)):
            small_copies.append(pltpu.make_async_copy(there, here, small_sems.at[2 + i]))
        for pair in copies[:1] + [small_copies] + copies[1:]:
            for copy in pair:
                copy.start()

        def widen(value):
            lines = jnp.concatenate(
                [
                    jnp.zeros((node_rows, 2), F32),
                    value,
                    jnp.zeros((node_rows, TILE - 2 - node_cols), F32),
                ],
                axis=1,
            )
            edge = jnp.zeros((2, TILE), F32)
            return jnp.concatenate([edge, lines, edge], axis=0)

        def column(x):
            if x % piece == 0:
                for copy in copies[x // piece]:
                    copy.wait()
            return basis_terms(x, source_ref[x], lambda k: basis_ref[k, x])

        for copy in small_copies:
            copy.wait()
        parts = [jnp.zeros((TILE, TILE), F32), widen(cdiag_ref[...])]
        parts = parts + [widen(ratio_ref[d]) for d in range(4)]
        parts.append(jnp.zeros((TILE, LANES - TILE * len(parts)), F32))
        table = jnp.concatenate(parts, axis=1)

        tile = restrict_tile((column(x) for x in range(cell_rows)), None, cell_rows, cell_cols)
        tile = tile + table
        tile_ref[...] = tile
        even = is_even("lay")
        edges = (even * (cell_rows - 1), (1 - even) * (cell_rows - 1))
        for load, edge in zip(loads, edges):
            for k in range(4):
                for i, span in enumerate(spans):
                    start = (k * len(spans) + i) * cell_cols
                    load[start : start + cell_cols, :] = basis_ref[k, edge, :, span]
            load[layer_rows:, :] = tile

    outs = [(basis.shape, F32), (block, F32), ((TILE, LANES), F32)]
    outs = outs + [(value.shape, value.dtype) for value in slot_arrays]
    outs = outs + [(load_one, F32)] * lay_pairs
    basis, matrix_source, tile_own, *rest = run(
        kernel_a,
        outs,
        [
            pltpu.with_memory_space_constraint(value, pltpu.HBM)
            for value in (basis, matrix_source, coarse_diag, coarse_ratio, *slot_arrays)
        ],
        scratch=(
            pltpu.VMEM(coarse_diag.shape, F32),
            pltpu.VMEM(coarse_ratio.shape, F32),
            pltpu.SemaphoreType.DMA((2, pieces)),
            pltpu.SemaphoreType.DMA((2 + slot_kinds,)),
        ),
        in_place=range(4 + slot_kinds),
    )
    slot_cell, *loads = rest
    slot_source = frac_source.reshape(small)
    lay_one = swap_pairs(loads[0], loads[-1], "lay")

    def lay_sides(refs, window):
        even = is_even("lay")
        first = refs[0][window]
        second = refs[1][window] if len(refs) > 1 else jnp.zeros(first.shape, F32)
        return low_high(even, first, second)

    def blk_sides(even_ref, odd_ref, window):
        return low_high(is_even("blk"), even_ref[window], odd_ref[window])

    def kernel_e(tile_ref, basis_ref, *refs):
        got, (join_ref, even_ref, odd_ref) = refs[:-3], refs[-3:]
        low, high = lay_sides(got, (slice(layer_rows, layer_rows + TILE), slice(0, LANES)))
        joined = join_rows(tile_ref[...], low, high)
        join_ref[...] = joined
        even = is_even("blk")
        edges = (even * (cell_cols - 1), (1 - even) * (cell_cols - 1))
        for ref, edge in zip((even_ref, odd_ref), edges):
            for k in range(4):
                for x in range(cell_rows):
                    row = basis_ref[k, x, pl.ds(edge, 1), :]
                    for i, span in enumerate(spans):
                        line = (k * len(spans) + i) * cell_rows + x
                        ref[line : line + 1, :] = row[:, span]
            ref[layer_rows:, :] = joined

    outs = [((TILE, LANES), F32), (load_one, F32), (load_one, F32)]
    joined_one, even_one, odd_one = run(kernel_e, outs, (tile_own, basis, *lay_one))
    blk_one = swap_pairs(even_one, odd_one, "blk")

    links = frac_trans.shape[0]

    def kernel_p(
        basis_ref, cell_ref, row_ref, depth_ref, node_ref, weight_ref
    ):
        cell = as_line(cell_ref[...])
        at_row = lax.shift_right_logical(cell, depth_bits)
        at_depth = jnp.bitwise_and(cell, depth - 1)
        hot_row = (iota((cells, slots), 0) == at_row).astype(F32).astype(BF16)
        hot_depth = (iota((depth, slots), 0) == at_depth).astype(F32).astype(BF16)
        row_ref[...] = hot_row
        depth_ref[...] = hot_depth
        fields = [basis_ref[k].reshape(cells, depth) for k in range(4)]
        weights = gather_cells(fields, hot_row, hot_depth, 2)
        along = jnp.bitwise_and(at_row, cell_cols - 1)
        across = lax.shift_right_logical(at_row, cell_cols.bit_length() - 1)
        lane = iota((LANES, slots), 0)
        line = iota((TILE, slots), 0)
        match = (own_nodes(across) + 2 == line, side_nodes(across) + 2 == line)
        for j, nodes in enumerate((own_nodes(along), side_nodes(along))):
            part = slice(j * slots, (j + 1) * slots)
            node_ref[:, part] = (lane == nodes + 2).astype(F32).astype(BF16)
            weight_ref[:, part] = jnp.where(match[0], weights[2 * j], 0.0) + jnp.where(
                match[1], weights[2 * j + 1], 0.0
            )

    outs = [
        ((cells, slots), BF16),
        ((depth, slots), BF16),
        ((LANES, 2 * slots), BF16),
        ((TILE, 2 * slots), F32),
    ]
    hot_row, hot_depth, hot_node, node_weight = run(kernel_p, outs, (basis, slot_cell))

    tables = 8

    def kernel_q(
        faces_ref, accum_ref, basis_ref, source_ref, row_ref, depth_ref, link_ref, facc_ref,
        trans_ref, count_ref, sface_ref, forward_ref, back_ref, ssource_ref, scale_ref, edge_ref,
        sedge_ref, frac_ref, linked_ref,
    ):
        live = (iota((1, slots), 1) < count_ref[0]).astype(F32)
        couple = live * as_line(link_ref[...])
        frac_diag = as_line(facc_ref[...]) + couple
        for j in range(links):
            frac_diag = frac_diag + trans_ref[j : j + 1, :]
        frac_ref[0:1, :] = couple
        frac_ref[1:2, :] = OMEGA * live / frac_diag
        linked_ref[...] = scatter_cells(couple, row_ref[...], depth_ref[...])

        lane = iota((cell_cols, depth), 1)
        place = jnp.bitwise_and(iota((cell_cols, depth), 0), BLOCK - 1)
        for x in range(cell_rows):
            diag = accum_ref[x] + linked_ref[x * cell_cols : (x + 1) * cell_cols, :]
            for d in range(6):
                diag = diag + faces_ref[d, x]
            scale = OMEGA / diag
            scale_ref[x] = scale
            ssource_ref[x] = scale * source_ref[x]
            deep = jnp.where(lane < depth - 1, faces_ref[4, x], 0.0)
            shallow = jnp.where(lane > 0, faces_ref[5, x], 0.0)
            for d in range(4):
                sface_ref[d, x] = scale * faces_ref[d, x]
            sface_ref[4, x] = scale * deep
            sface_ref[5, x] = scale * shallow
            near = {}
            for k in range(4):
                value = basis_ref[k, x]
                near[k] = (
                    deep * pltpu.roll(value, depth - 1, 1)
                    + shallow * pltpu.roll(value, 1, 1)
                    - diag * value
                )
            for i in range(2):
                own_up, own_down = shift_rows(basis_ref[i, x])
                side_up, side_down = shift_rows(basis_ref[2 + i, x])
                far = None
                for face, own, side, swap_at, far_at in (
                    (faces_ref[3, x], own_down, side_down, 0, BLOCK // 2),
                    (faces_ref[2, x], own_up, side_up, BLOCK - 1, BLOCK // 2 - 1),
                ):
                    own, side = face * own, face * side
                    swap, beyond = place == swap_at, place == far_at
                    near[i] = near[i] + jnp.where(swap, side, own)
                    near[2 + i] = near[2 + i] + jnp.where(
                        swap, own, jnp.where(beyond, 0.0, side)
                    )
                    far = jnp.where(beyond, side, 0.0 if far is None else far)
                near[4 + i] = far
            nodes = (own_node(x), side_node(x), 2 * own_node(x) - side_node(x))
            for other, d in ((x - 1, 1), (x + 1, 0)):
                if not 0 <= other < cell_rows:
                    continue
                face = faces_ref[d, x]
                for i, node in enumerate((own_node(other), side_node(other))):
                    kind = nodes.index(node)
                    for j in range(2):
                        table = kind + 2 * j if kind < 2 else 6 + j
                        part = face * basis_ref[2 * j + i, other]
                        near[table] = near[table] + part if table in near else part
            for table, _, _ in near_terms(x):
                back_ref[table, x] = near[table]
                value = scale * near[table]
                forward_ref[table, x] = basis_ref[table, x] + value if table < 4 else value
            edge_ref[2, x : x + 1, :] = faces_ref[3, x, 0:1, :]
            edge_ref[3, x : x + 1, :] = faces_ref[2, x, cell_cols - 1 : cell_cols, :]
            sedge_ref[0, x : x + 1, :] = sface_ref[3, x, 0:1, :]
            sedge_ref[1, x : x + 1, :] = sface_ref[2, x, cell_cols - 1 : cell_cols, :]
        edge_ref[0] = faces_ref[1, 0]
        edge_ref[1] = faces_ref[0, cell_rows - 1]

    outs = [
        (faces.shape, F32),
        ((tables, *block), F32),
        ((tables, *block), F32),
        (block, F32),
        (block, F32),
        ((4, cell_cols, depth), F32),
        ((2, cell_rows, depth), F32),
        ((TILE, slots), F32),
    ]
    sfaces, forward, back, ssource, scale, edge_faces, sedges, frac_pack = run(
        kernel_q,
        outs,
        (
            faces,
            accum,
            basis,
            matrix_source,
            hot_row,
            hot_depth,
            frac_link.reshape(small),
            frac_accum.reshape(small),
            frac_trans,
            frac_count,
        ),
        smem=(9,),
        scratch=(pltpu.VMEM((cells, depth), F32),),
    )

    layer = (slice(0, layer_rows), slice(0, LANES))

    def widen_layer(value, start):
        first = start * edge_size
        parts = [
            value[first + i * cell_cols : first + (i + 1) * cell_cols, :]
            for i in range(len(spans))
        ]
        return jnp.concatenate(parts, axis=1)


    def rims_of(lay_refs, blk_even, blk_odd):
        lay_low, lay_high = lay_sides(lay_refs, layer)
        blk_low, blk_high = blk_sides(blk_even, blk_odd, layer)

        def pick(value):
            return lambda k: widen_layer(value, k)

        return pick(lay_low), pick(lay_high), pick(blk_low), pick(blk_high)

    last = cell_rows - 1

    def kernel_b(
        sface_ref, forward_ref, back_ref, ssource_ref, edge_ref, sedge_ref, node_ref, weight_ref,
        frac_ref, fsrc_ref, own_ref, joined_ref, blk_even, blk_odd, *refs,
    ):
        lay_refs = refs[:lay_pairs]
        p2_ref, rows_ref, f_ref, tile_ref, parts_ref = refs[lay_pairs : lay_pairs + 5]
        loads = refs[lay_pairs + 5 :]
        at_tile = (slice(layer_rows, layer_rows + TILE), slice(0, LANES))
        low, high = blk_sides(blk_even, blk_odd, at_tile)
        table = join_lanes(joined_ref[...], low, high)
        parts = coarse_parts(table)
        for i, part in enumerate(parts):
            parts_ref[i] = part
        second = coarse_solve(table, parts)
        fields = Fields(second, cell_rows, cell_cols)
        x_low, x_high, y_low, y_high = rims_of(lay_refs, blk_even, blk_odd)
        left_rim = sface_ref[1, 0] * fields.column(-1, x_low)
        right_rim = sface_ref[0, last] * fields.column(cell_rows, x_high)
        low_rim = sedge_ref[0] * fields.row(-1, y_low)
        high_rim = sedge_ref[1] * fields.row(cell_cols, y_high)

        couple = frac_ref[0:1, :]
        pressure_at = nodes_at_slots(second, node_ref[...], weight_ref[...])
        fracture = frac_ref[1:2, :] * (as_line(fsrc_ref[...]) + couple * pressure_at)
        f_ref[...] = fracture
        linked = slots_at_nodes(couple * fracture, node_ref[...], weight_ref[...])

        def columns():
            for x in range(cell_rows):
                value = ssource_ref[x] + fields.terms(x, lambda t: forward_ref[t, x])
                if x == 0:
                    value = value + left_rim
                if x == last:
                    value = value + right_rim
                value = add_edge_rows(value, low_rim[x : x + 1, :], high_rim[x : x + 1, :])
                p2_ref[x] = value
                rows_ref[0, x : x + 1, :] = value[0:1, :]
                rows_ref[1, x : x + 1, :] = value[cell_cols - 1 : cell_cols, :]
                if x == 0:
                    yield basis_terms(-1, edge_ref[0] * value, x_low)
                if x == last:
                    yield basis_terms(cell_rows, edge_ref[1] * value, x_high)
                yield value, [(kind, node, back_ref[t, x]) for t, kind, node in near_terms(x)]

        def rows():
            yield -1, edge_ref[2] * rows_ref[0], y_low
            yield cell_cols, edge_ref[3] * rows_ref[1], y_high

        tile = restrict_tile(columns(), rows, cell_rows, cell_cols) + linked
        tile = tile + jnp.where(iota((TILE, LANES), 1) < TILE, own_ref[...], 0.0)
        tile_ref[...] = tile
        even = is_even("lay")
        edges = (even * last, (1 - even) * last)
        for load, edge in zip(loads, edges):
            for i, span in enumerate(spans):
                load[i * cell_cols : (i + 1) * cell_cols, :] = p2_ref[edge, :, span]
            load[edge_size:, :] = pack_slots(tile, fracture)

    parts_shape = (5, TILE, LANES)
    row_pair = (2, cell_rows, depth)
    outs = [(block, F32), (row_pair, F32), ((1, slots), F32), ((TILE, LANES), F32)]
    outs = outs + [(parts_shape, F32)] + [(load_two, F32)] * lay_pairs
    pressure, edge_rows, fracture, tile_two, coarse, *loads = run(
        kernel_b,
        outs,
        (
            sfaces, forward, back, ssource, edge_faces, sedges, hot_node, node_weight,
            frac_pack, slot_source, tile_own, joined_one, *blk_one, *lay_one,
        ),
    )
    lay_two = swap_pairs(loads[0], loads[-1], "lay")

    tail_rows = (slice(edge_size, edge_size + TILE), slice(0, LANES))

    def kernel_f(tile_ref, rows_ref, *refs):
        got, (join_ref, even_ref, odd_ref) = refs[:-3], refs[-3:]
        low, high = lay_sides(got, tail_rows)
        joined = join_rows(tile_ref[...], low, high)
        join_ref[...] = joined
        even = is_even("blk")
        tail = jnp.where(iota((TILE, LANES), 1) < LANES // 2, joined, got[0][tail_rows])
        for ref, side in ((even_ref, even), (odd_ref, 1 - even)):
            for i, span in enumerate(spans):
                ref[i * cell_rows : (i + 1) * cell_rows, :] = rows_ref[side, :, span]
            ref[edge_size:, :] = tail

    outs = [((TILE, LANES), F32), (load_two, F32), (load_two, F32)]
    joined_two, even_two, odd_two = run(kernel_f, outs, (tile_two, edge_rows, *lay_two))
    blk_two = swap_pairs(even_two, odd_two, "blk")

    def kernel_m(
        sface_ref, ssource_ref, scale_ref, p2_ref, f_ref, row_ref, depth_ref, frac_ref, peer_ref,
        base_ref, at_ref, high_ref, low_ref,
    ):
        owner = lax.axis_index("blk") * lay_size + lax.axis_index("lay")
        peer = as_line(peer_ref[...] - (owner - 1) * slots)
        low_ref[...] = (
            (iota((LANES, peer.shape[1]), 0) == jnp.bitwise_and(peer, LANES - 1))
            .astype(F32)
            .astype(BF16)
        )
        high_ref[...] = lax.shift_right_logical(peer, 7)
        hot_row, hot_depth = row_ref[...], depth_ref[...]
        flat = p2_ref[...].reshape(cells, depth)
        at_ref[...] = gather_cells([flat], hot_row, hot_depth)[0]
        linked = scatter_cells(frac_ref[0:1, :] * f_ref[...], hot_row, hot_depth)
        for x in range(cell_rows):
            centre = p2_ref[x]
            left = p2_ref[x - 1] if x else None
            right = p2_ref[x + 1] if x < last else None
            around = neighbour_sum(sface_ref, x, left, centre, right)
            part = linked[x * cell_cols : (x + 1) * cell_cols, :]
            base_ref[x] = ssource_ref[x] + scale_ref[x] * part + (1.0 - OMEGA) * centre + around

    outs = [
        (block, F32),
        ((1, slots), F32),
        ((1, links * slots), jnp.int32),
        ((LANES, links * slots), BF16),
    ]
    base, slot_pressure, peer_high, hot_low = run(
        kernel_m,
        outs,
        (sfaces, ssource, scale, pressure, fracture, hot_row, hot_depth, frac_pack, frac_peer),
    )
    ring = []
    if lay_size != 2:
        owners = lax.axis_size("blk") * lay_size
        ahead = [(i, i + 1) for i in range(owners - 1)]
        line = fracture.reshape(small)
        ring = [
            lax.ppermute(line, ("blk", "lay"), ahead),
            lax.ppermute(line, ("blk", "lay"), [(b, a) for a, b in ahead]),
        ]

    def kernel_c(
        sface_ref, forward_ref, base_ref, sedge_ref, node_ref, weight_ref, frac_ref, high_ref,
        low_ref, fsrc_ref, trans_ref, f_ref, at_ref, joined_ref, parts_ref,
        one_even, one_odd, two_even, two_odd, *refs,
    ):
        lay_first, lay_second = refs[:lay_pairs], refs[lay_pairs : 2 * lay_pairs]
        ring_refs = refs[2 * lay_pairs : -5]
        p_hbm, f_hbm, p_out, f_out, sems = refs[-5:]
        low, high = blk_sides(two_even, two_odd, tail_rows)
        tile = join_lanes(joined_ref[...], low, high)
        second = coarse_solve(tile, [parts_ref[i] for i in range(5)])
        fields = Fields(second, cell_rows, cell_cols)
        x_low, x_high, y_low, y_high = rims_of(lay_first, one_even, one_odd)
        window = (slice(0, edge_size), slice(0, LANES))
        p_left, p_right = [widen_layer(value, 0) for value in lay_sides(lay_second, window)]
        p_low, p_high = [widen_layer(value, 0) for value in blk_sides(two_even, two_odd, window)]

        left_rim = sface_ref[1, 0] * (p_left + fields.column(-1, x_low))
        right_rim = sface_ref[0, last] * (p_right + fields.column(cell_rows, x_high))
        low_rim = sedge_ref[0] * (p_low + fields.row(-1, y_low))
        high_rim = sedge_ref[1] * (p_high + fields.row(cell_cols, y_high))
        pressure_at = at_ref[...] + nodes_at_slots(second, node_ref[...], weight_ref[...])
        mine = as_rows(f_ref[...], LANES)
        if ring_refs:
            before, after = ring_refs[0][...], ring_refs[1][...]
        else:
            partner = lay_second[0][tail_rows]
            before = unpack_slots(by_parity(is_even("lay"), low, partner))
            after = unpack_slots(by_parity(is_even("lay"), partner, high))
        width = mine.shape[0]
        wide = jnp.concatenate(
            [before, mine, after]
            + [jnp.zeros((-3 * width % TILE, LANES), F32)] * (3 * width % TILE > 0),
            axis=0,
        )
        product = jnp.dot(stacked([wide]), low_ref[...], preferred_element_type=F32)
        picked = unstack(product, wide.shape[0])[0]
        match = iota(picked.shape, 0) == high_ref[...]
        peers = jnp.sum(jnp.where(match, picked, 0.0), axis=0, keepdims=True)
        flux = as_line(fsrc_ref[...]) + frac_ref[0:1, :] * pressure_at
        for j in range(links):
            flux = flux + trans_ref[j : j + 1, :] * peers[:, j * slots : (j + 1) * slots]
        result = (1.0 - OMEGA) * f_ref[...] + frac_ref[1:2, :] * flux
        copies = []
        for x in range(cell_rows):
            value = base_ref[x] + fields.terms(x, lambda t: forward_ref[t, x])
            if x == 0:
                value = value + left_rim
            if x == last:
                value = value + right_rim
            p_out[x] = add_edge_rows(value, low_rim[x : x + 1, :], high_rim[x : x + 1, :])
            if (x + 1) % piece == 0:
                part = pl.ds(x + 1 - piece, piece)
                copies.append(
                    pltpu.make_async_copy(p_out.at[part], p_hbm.at[part], sems.at[x // piece])
                )
                copies[-1].start()
        f_out[...] = as_rows(result, LANES)
        copies.append(pltpu.make_async_copy(f_out, f_hbm, sems.at[pieces]))
        copies[-1].start()
        for copy in copies:
            copy.wait()

    final, frac_final = run(
        kernel_c,
        [(block, F32), (small, F32)],
        (
            sfaces, forward, base, sedges, hot_node, node_weight, frac_pack, peer_high,
            hot_low, slot_source, frac_trans, fracture, slot_pressure, joined_two, coarse,
            *blk_one, *blk_two, *lay_one, *lay_two, *ring,
        ),
        scratch=(
            pltpu.VMEM(block, F32),
            pltpu.VMEM(small, F32),
            pltpu.SemaphoreType.DMA((pieces + 1,)),
        ),
        out_place=(0, 1),
    )
    return final, frac_final.reshape(slots)


def solution(mesh):
    return jax.shard_map(
        local,
        mesh=mesh,
        in_specs=(
            P("lay", "blk", None),
            P("lay", "blk", None),
            P(None, "lay", "blk", None),
            P(None, "lay", "blk", None),
            P("lay", "blk"),
            P(None, "lay", "blk"),
            P(("blk", "lay")),
            P(("blk", "lay")),
            P(("blk", "lay")),
            P(None, ("blk", "lay")),
            P(("blk", "lay")),
            P(None, ("blk", "lay")),
            P(("blk", "lay")),
        ),
        out_specs=(P("lay", "blk", None), P(("blk", "lay"))),
        check_vma=False,
    )
```

```python
import jax
import jax.numpy as jnp
from jax import lax
from jax.experimental import pallas as pl
from jax.experimental.pallas import tpu as pltpu
from jax.sharding import PartitionSpec as P

BLOCK = 4
OMEGA = 0.8
TILE = 8
LANES = 128
F32 = jnp.float32
BF16 = jnp.bfloat16


def pair_lists(count):
    even = [(i, i ^ 1) for i in range(count) if i ^ 1 < count]
    odd = [(i, i + 1 if i % 2 else i - 1) for i in range(1, count)]
    return even, [(a, b) for a, b in odd if 0 < b < count]


def swap_pairs(even_load, odd_load, axis):
    even, odd = pair_lists(lax.axis_size(axis))
    got = [lax.ppermute(even_load, axis, even)]
    if odd:
        got.append(lax.ppermute(odd_load, axis, odd))
    return got


def run(kernel, outs, args, scratch=(), smem=(), in_place=(), out_place=(), aliases={}):
    spec = pl.BlockSpec(memory_space=pltpu.VMEM)
    scalar = pl.BlockSpec(memory_space=pltpu.SMEM)
    there = pl.BlockSpec(memory_space=pltpu.HBM)

    def place(i):
        return scalar if i in smem else there if i in in_place else spec

    return pl.pallas_call(
        kernel,
        out_shape=[jax.ShapeDtypeStruct(shape, dtype) for shape, dtype in outs],
        in_specs=[place(i) for i in range(len(args))],
        out_specs=[there if i in out_place else spec for i in range(len(outs))],
        scratch_shapes=list(scratch),
        input_output_aliases=aliases,
        compiler_params=pltpu.CompilerParams(vmem_limit_bytes=24 << 20),
    )(*args)


def iota(shape, dim):
    return lax.broadcasted_iota(jnp.int32, shape, dim)


def own_node(cell):
    return cell // BLOCK


def side_node(cell):
    return cell // BLOCK + (-1 if cell % BLOCK < BLOCK // 2 else 1)


def near_terms(x):
    own, near = own_node(x) + 2, side_node(x) + 2
    terms = [(0, 0, own), (1, 0, near), (2, 1, own), (3, 1, near), (4, 2, own), (5, 2, near)]
    if 0 < x % BLOCK < BLOCK - 1:
        terms = terms + [(6, 0, 2 * own - near), (7, 1, 2 * own - near)]
    return terms


def own_nodes(cells):
    return lax.shift_right_arithmetic(cells, 2)


def side_nodes(cells):
    low = jnp.bitwise_and(cells, BLOCK - 1) < BLOCK // 2
    return own_nodes(cells) + jnp.where(low, -1, 1)


def node_masks(cells):
    index = iota((cells, LANES), 0)
    lane = iota((cells, LANES), 1)
    own, side = own_nodes(index) + 2, side_nodes(index) + 2
    return own == lane, side == lane, 2 * own - side == lane


def fold_lanes(value):
    total = value[:, :LANES]
    for start in range(LANES, value.shape[1], LANES):
        total = total + value[:, start : start + LANES]
    return total


def by_parity(is_even, even_value, odd_value):
    return jnp.where(jnp.full(even_value.shape, is_even, jnp.int32) > 0, even_value, odd_value)


def low_high(is_even, even_got, odd_got):
    low = by_parity(is_even, odd_got, even_got)
    high = by_parity(is_even, even_got, odd_got)
    return low, high


def basis_terms(x, residual, weight):
    own, near = own_node(x) + 2, side_node(x) + 2
    nodes = (own, near, own, near)
    return residual, [(k // 2, nodes[k], weight(k)) for k in range(4)]


def restrict_tile(columns, rows, cell_rows, cell_cols):
    sums = {}
    for value, terms in columns:
        for kind, node, weight in terms:
            part = fold_lanes(weight * value)
            key = (kind, node)
            sums[key] = sums[key] + part if key in sums else part
    masks = node_masks(cell_cols)
    row_index = iota((TILE, LANES), 0)
    tile = jnp.zeros((TILE, LANES), F32)
    nodes = sorted({node for _, node in sums})
    wide = {}
    if rows:
        lane = iota((cell_rows, LANES), 1)
        for y, residual, weight in rows():
            for k in range(4):
                node = (own_node(y) if k < 2 else side_node(y)) + 2
                part = jnp.sum(fold_lanes(weight(k) * residual), axis=1, keepdims=True)
                part = jnp.where(lane == node, part, 0.0)
                wide[k % 2] = wide[k % 2] + part if k % 2 in wide else part
        x_index = iota((cell_rows, LANES), 0)
        x_nodes = (own_nodes(x_index) + 2, side_nodes(x_index) + 2)
    for node in nodes:
        total = jnp.zeros((cell_cols, LANES), F32)
        for kind in range(3):
            if (kind, node) in sums:
                lane_sum = jnp.sum(sums[(kind, node)], axis=1, keepdims=True)
                total = total + jnp.where(masks[kind], lane_sum, 0.0)
        line = jnp.sum(total, axis=0, keepdims=True)
        if rows:
            extra = jnp.where(x_nodes[0] == node, wide[0], 0.0) + jnp.where(
                x_nodes[1] == node, wide[1], 0.0
            )
            line = line + jnp.sum(extra, axis=0, keepdims=True)
        tile = jnp.where(row_index == node, line, tile)
    return tile


def join_rows(tile, low, high):
    row = iota((TILE, LANES), 0)
    half = TILE // 2
    return (
        tile
        + jnp.where(row < half, pltpu.roll(low, half, 0), 0.0)
        + jnp.where(row >= half, pltpu.roll(high, half, 0), 0.0)
    )


def join_lanes(tile, low, high):
    part = jnp.bitwise_and(iota((TILE, LANES), 1), TILE - 1)
    half = TILE // 2
    return (
        tile
        + jnp.where(part < half, pltpu.roll(low, LANES - half, 1), 0.0)
        + jnp.where(part >= half, pltpu.roll(high, half, 1), 0.0)
    )


def coarse_parts(table):
    lane = iota((TILE, LANES), 1)
    diag = pltpu.roll(table, LANES - TILE, 1)
    live = (lane < TILE) & (diag > 0.0)
    parts = [jnp.where(live, 1.0 / jnp.where(live, diag, 1.0), 0.0)]
    for direction in range(4):
        ratio = pltpu.roll(table, LANES - TILE * (2 + direction), 1)
        parts.append(jnp.where(lane < TILE, ratio, 0.0))
    return parts


def coarse_solve(tile, parts):
    first = tile * parts[0]
    near = (
        pltpu.roll(first, 1, 0),
        pltpu.roll(first, TILE - 1, 0),
        pltpu.roll(first, 1, 1),
        pltpu.roll(first, LANES - 1, 1),
    )
    second = first
    for direction in range(4):
        second = second + parts[1 + direction] * near[direction]
    return second


class Fields:
    def __init__(self, second, cell_rows, cell_cols):
        masks = node_masks(cell_cols)
        self.columns = {}
        for node in range(1, TILE - 1):
            line = jnp.broadcast_to(second[node : node + 1, :], (cell_cols, LANES))
            for kind in range(3):
                self.columns[(kind, node)] = jnp.sum(
                    jnp.where(masks[kind], line, 0.0), axis=1, keepdims=True
                )
        x_index = iota((cell_rows, LANES), 0)
        self.wide = []
        for nodes in (own_nodes(x_index) + 2, side_nodes(x_index) + 2):
            value = jnp.zeros((cell_rows, LANES), F32)
            for node in range(1, TILE - 1):
                value = jnp.where(nodes == node, second[node : node + 1, :], value)
            self.wide.append(value)

    def column(self, x, weight):
        own, side = own_node(x) + 2, side_node(x) + 2
        return (
            weight(0) * self.columns[(0, own)]
            + weight(1) * self.columns[(0, side)]
            + weight(2) * self.columns[(1, own)]
            + weight(3) * self.columns[(1, side)]
        )

    def terms(self, x, weight):
        total = None
        for table, kind, node in near_terms(x):
            part = weight(table) * self.columns[(kind, node)]
            total = part if total is None else total + part
        return total

    def row(self, y, weight):
        lane = iota(self.wide[0].shape, 1)

        def pick(kind, node):
            return jnp.sum(jnp.where(lane == node, self.wide[kind], 0.0), axis=1, keepdims=True)

        own, side = own_node(y) + 2, side_node(y) + 2
        return (
            weight(0) * pick(0, own)
            + weight(1) * pick(1, own)
            + weight(2) * pick(0, side)
            + weight(3) * pick(1, side)
        )


def shift_rows(value):
    row = iota((TILE, value.shape[1]), 0)
    parts = [value[i : i + TILE, :] for i in range(0, value.shape[0], TILE)]
    up = [pltpu.roll(part, TILE - 1, 0) for part in parts]
    down = [pltpu.roll(part, 1, 0) for part in parts]
    above = [
        jnp.where(row == TILE - 1, end, part) for end, part in zip(up[1:] + [0.0], up)
    ]
    below = [jnp.where(row == 0, end, part) for end, part in zip([0.0] + down[:-1], down)]
    return jnp.concatenate(above, axis=0), jnp.concatenate(below, axis=0)


def neighbour_sum(faces, x, left, centre, right):
    depth = centre.shape[1]
    above, below = shift_rows(centre)
    total = faces[2, x] * above + faces[3, x] * below
    total = total + faces[4, x] * pltpu.roll(centre, depth - 1, 1)
    total = total + faces[5, x] * pltpu.roll(centre, 1, 1)
    if right is not None:
        total = total + faces[0, x] * right
    if left is not None:
        total = total + faces[1, x] * left
    return total


def add_edge_rows(value, low_row, high_row):
    row = iota((TILE, value.shape[1]), 0)
    low = value[:TILE, :] + jnp.where(row == 0, low_row, 0.0)
    high = value[-TILE:, :] + jnp.where(row == TILE - 1, high_row, 0.0)
    return jnp.concatenate([low, value[TILE:-TILE, :], high] if value.shape[0] > 2 * TILE else [low, high], axis=0)


def split3(value):
    high = value.astype(BF16)
    rest = value - high.astype(F32)
    mid = rest.astype(BF16)
    return high, mid, (rest - mid.astype(F32)).astype(BF16)


def stacked(values, count=3):
    return jnp.concatenate([part for value in values for part in split3(value)[:count]], axis=0)


def unstack(product, rows, count=3):
    parts = [product[i : i + rows, :] for i in range(0, product.shape[0], rows)]
    return [sum(parts[i + 1 : i + count], parts[i]) for i in range(0, len(parts), count)]


def gather_cells(fields, hot_row, hot_depth, count=3):
    product = jnp.dot(stacked(fields, count), hot_depth, preferred_element_type=F32)
    at_row = hot_row.astype(F32)
    return [
        jnp.sum(picked * at_row, axis=0, keepdims=True)
        for picked in unstack(product, fields[0].shape[0], count)
    ]


def scatter_cells(values, hot_row, hot_depth):
    spread = jnp.concatenate([hot_row * part for part in split3(values)], axis=0)
    product = lax.dot_general(
        spread, hot_depth, (((1,), (1,)), ((), ())), preferred_element_type=F32
    )
    return unstack(product, hot_row.shape[0])[0]


def nodes_at_slots(second, hot_node, node_weight):
    product = jnp.dot(stacked([second]), hot_node, preferred_element_type=F32)
    picked = unstack(product, TILE)[0]
    total = jnp.sum(picked * node_weight, axis=0, keepdims=True)
    half = total.shape[1] // 2
    return total[:, :half] + total[:, half:]


def slots_at_nodes(values, node_hot, node_weight):
    weighted = node_weight * jnp.concatenate([values, values], axis=1)
    product = jnp.dot(stacked([weighted]), node_hot, preferred_element_type=F32)
    return unstack(product, TILE)[0]


def as_line(value):
    return jnp.concatenate([value[i : i + 1, :] for i in range(value.shape[0])], axis=1)


def pack_slots(tile, line):
    rows = as_rows(line, LANES)
    wide = jnp.concatenate([pltpu.roll(rows, LANES // 2, 1), rows], axis=0)
    return jnp.where(iota((TILE, LANES), 1) < LANES // 2, tile, wide)


def unpack_slots(tile):
    half = TILE // 2
    low = iota((half, LANES), 1) < LANES // 2
    return jnp.where(low, pltpu.roll(tile[:half, :], LANES // 2, 1), tile[half:, :])


def as_rows(line, width):
    return jnp.concatenate(
        [line[:, start : start + width] for start in range(0, line.shape[1], width)], axis=0
    )


def local(
    matrix_source,
    accum,
    faces,
    basis,
    coarse_diag,
    coarse_ratio,
    frac_source,
    frac_accum,
    frac_link,
    frac_trans,
    frac_cell,
    frac_peer,
    frac_count,
):
    slots = frac_source.shape[0]
    cell_rows, cell_cols, depth = matrix_source.shape
    cells = cell_rows * cell_cols
    node_rows, node_cols = cell_rows // BLOCK, cell_cols // BLOCK
    assert node_rows + 4 == TILE and node_cols + 4 == TILE
    assert depth & (depth - 1) == 0 and cell_rows == cell_cols
    depth_bits = depth.bit_length() - 1
    lay_size = lax.axis_size("lay")
    lay_pairs = len([p for p in pair_lists(lay_size) if p])
    spans = [slice(start, start + LANES) for start in range(0, depth, LANES)]
    layer_rows = 4 * len(spans) * cell_cols
    load_one = (layer_rows + TILE, LANES)
    edge_size = len(spans) * cell_cols
    load_two = (edge_size + TILE, LANES)
    assert slots == TILE * LANES // 2
    block = matrix_source.shape

    def is_even(axis):
        return 1 - jnp.bitwise_and(lax.axis_index(axis), 1)

    piece = BLOCK
    pieces = cell_rows // piece

    small = (slots // LANES, LANES)
    slot_arrays = [frac_cell.reshape(small)]
    slot_kinds = len(slot_arrays)

    def kernel_a(basis_hbm, source_hbm, cdiag_hbm, ratio_hbm, *refs):
        slot_hbm, refs = refs[:slot_kinds], refs[slot_kinds:]
        (basis_ref, source_ref, tile_ref), refs = refs[:3], refs[3:]
        slot_refs, refs = refs[:slot_kinds], refs[slot_kinds:]
        rim_refs, refs = refs[:2], refs[2:]
        loads, (cdiag_ref, ratio_ref, sems, small_sems) = refs[:-4], refs[-4:]
        copies = []
        for i in range(pieces):
            part = pl.ds(i * piece, piece)
            copies.append(
                (
                    pltpu.make_async_copy(source_hbm.at[part], source_ref.at[part], sems.at[0, i]),
                    pltpu.make_async_copy(
                        basis_hbm.at[:, part], basis_ref.at[:, part], sems.at[1, i]
                    ),
                )
            )
        small_copies = [
            pltpu.make_async_copy(cdiag_hbm, cdiag_ref, small_sems.at[0]),
            pltpu.make_async_copy(ratio_hbm, ratio_ref, small_sems.at[1]),
        ]
        for i, (there, here) in enumerate(zip(slot_hbm, slot_refs)):
            small_copies.append(pltpu.make_async_copy(there, here, small_sems.at[2 + i]))
        for pair in copies[:1] + [small_copies] + copies[1:]:
            for copy in pair:
                copy.start()

        def widen(value):
            lines = jnp.concatenate(
                [
                    jnp.zeros((node_rows, 2), F32),
                    value,
                    jnp.zeros((node_rows, TILE - 2 - node_cols), F32),
                ],
                axis=1,
            )
            edge = jnp.zeros((2, TILE), F32)
            return jnp.concatenate([edge, lines, edge], axis=0)

        blk_even = is_even("blk")
        rim_edges = (blk_even * (cell_cols - 1), (1 - blk_even) * (cell_cols - 1))

        def column(x):
            if x % piece == 0:
                for copy in copies[x // piece]:
                    copy.wait()
            for ref, edge in zip(rim_refs, rim_edges):
                for k in range(4):
                    row = basis_ref[k, x, pl.ds(edge, 1), :]
                    for i, span in enumerate(spans):
                        line = (k * len(spans) + i) * cell_rows + x
                        ref[line : line + 1, :] = row[:, span]
            return basis_terms(x, source_ref[x], lambda k: basis_ref[k, x])

        for copy in small_copies:
            copy.wait()
        parts = [jnp.zeros((TILE, TILE), F32), widen(cdiag_ref[...])]
        parts = parts + [widen(ratio_ref[d]) for d in range(4)]
        parts.append(jnp.zeros((TILE, LANES - TILE * len(parts)), F32))
        table = jnp.concatenate(parts, axis=1)

        tile = restrict_tile((column(x) for x in range(cell_rows)), None, cell_rows, cell_cols)
        tile = tile + table
        tile_ref[...] = tile
        even = is_even("lay")
        edges = (even * (cell_rows - 1), (1 - even) * (cell_rows - 1))
        for load, edge in zip(loads, edges):
            for k in range(4):
                for i, span in enumerate(spans):
                    start = (k * len(spans) + i) * cell_cols
                    load[start : start + cell_cols, :] = basis_ref[k, edge, :, span]
            load[layer_rows:, :] = tile

    outs = [(basis.shape, F32), (block, F32), ((TILE, LANES), F32)]
    outs = outs + [(value.shape, value.dtype) for value in slot_arrays]
    outs = outs + [(load_one, F32)] * (2 + lay_pairs)
    basis, matrix_source, tile_own, *rest = run(
        kernel_a,
        outs,
        [
            pltpu.with_memory_space_constraint(value, pltpu.HBM)
            for value in (basis, matrix_source, coarse_diag, coarse_ratio, *slot_arrays)
        ],
        scratch=(
            pltpu.VMEM(coarse_diag.shape, F32),
            pltpu.VMEM(coarse_ratio.shape, F32),
            pltpu.SemaphoreType.DMA((2, pieces)),
            pltpu.SemaphoreType.DMA((2 + slot_kinds,)),
        ),
        in_place=range(4 + slot_kinds),
    )
    slot_cell, rim_even, rim_odd, *loads = rest
    slot_source = frac_source.reshape(small)
    lay_one = swap_pairs(loads[0], loads[-1], "lay")

    def lay_sides(refs, window):
        even = is_even("lay")
        first = refs[0][window]
        second = refs[1][window] if len(refs) > 1 else jnp.zeros(first.shape, F32)
        return low_high(even, first, second)

    def blk_sides(even_ref, odd_ref, window):
        return low_high(is_even("blk"), even_ref[window], odd_ref[window])

    def kernel_e(tile_ref, rim_even_ref, rim_odd_ref, *refs):
        got, (join_ref, even_ref, odd_ref) = refs[:-3], refs[-3:]
        low, high = lay_sides(got, (slice(layer_rows, layer_rows + TILE), slice(0, LANES)))
        joined = join_rows(tile_ref[...], low, high)
        join_ref[...] = joined
        even_ref[layer_rows:, :] = joined
        odd_ref[layer_rows:, :] = joined

    outs = [((TILE, LANES), F32), (load_one, F32), (load_one, F32)]
    joined_one, even_one, odd_one = run(
        kernel_e, outs, (tile_own, rim_even, rim_odd, *lay_one), aliases={1: 1, 2: 2}
    )
    blk_one = swap_pairs(even_one, odd_one, "blk")

    links = frac_trans.shape[0]

    def kernel_p(
        basis_ref, cell_ref, row_ref, depth_ref, node_ref, weight_ref
    ):
        cell = as_line(cell_ref[...])
        at_row = lax.shift_right_logical(cell, depth_bits)
        at_depth = jnp.bitwise_and(cell, depth - 1)
        hot_row = (iota((cells, slots), 0) == at_row).astype(F32).astype(BF16)
        hot_depth = (iota((depth, slots), 0) == at_depth).astype(F32).astype(BF16)
        row_ref[...] = hot_row
        depth_ref[...] = hot_depth
        fields = [basis_ref[k].reshape(cells, depth) for k in range(4)]
        weights = gather_cells(fields, hot_row, hot_depth, 2)
        along = jnp.bitwise_and(at_row, cell_cols - 1)
        across = lax.shift_right_logical(at_row, cell_cols.bit_length() - 1)
        lane = iota((LANES, slots), 0)
        line = iota((TILE, slots), 0)
        match = (own_nodes(across) + 2 == line, side_nodes(across) + 2 == line)
        for j, nodes in enumerate((own_nodes(along), side_nodes(along))):
            part = slice(j * slots, (j + 1) * slots)
            node_ref[:, part] = (lane == nodes + 2).astype(F32).astype(BF16)
            weight_ref[:, part] = jnp.where(match[0], weights[2 * j], 0.0) + jnp.where(
                match[1], weights[2 * j + 1], 0.0
            )

    outs = [
        ((cells, slots), BF16),
        ((depth, slots), BF16),
        ((LANES, 2 * slots), BF16),
        ((TILE, 2 * slots), F32),
    ]
    hot_row, hot_depth, hot_node, node_weight = run(kernel_p, outs, (basis, slot_cell))

    tables = 8

    def kernel_q(
        faces_ref, accum_ref, basis_ref, source_ref, row_ref, depth_ref, link_ref, facc_ref,
        trans_ref, node_ref, count_ref, sface_ref, forward_ref, back_ref, ssource_ref, scale_ref, edge_ref,
        sedge_ref, frac_ref, turned_ref, linked_ref,
    ):
        turned_ref[...] = node_ref[...].astype(F32).T.astype(BF16)
        live = (iota((1, slots), 1) < count_ref[0]).astype(F32)
        couple = live * as_line(link_ref[...])
        frac_diag = as_line(facc_ref[...]) + couple
        for j in range(links):
            frac_diag = frac_diag + trans_ref[j : j + 1, :]
        frac_ref[0:1, :] = couple
        frac_ref[1:2, :] = OMEGA * live / frac_diag
        linked_ref[...] = scatter_cells(couple, row_ref[...], depth_ref[...])

        lane = iota((cell_cols, depth), 1)
        place = jnp.bitwise_and(iota((cell_cols, depth), 0), BLOCK - 1)
        for x in range(cell_rows):
            diag = accum_ref[x] + linked_ref[x * cell_cols : (x + 1) * cell_cols, :]
            for d in range(6):
                diag = diag + faces_ref[d, x]
            scale = OMEGA / diag
            scale_ref[x] = scale
            ssource_ref[x] = scale * source_ref[x]
            deep = jnp.where(lane < depth - 1, faces_ref[4, x], 0.0)
            shallow = jnp.where(lane > 0, faces_ref[5, x], 0.0)
            for d in range(4):
                sface_ref[d, x] = scale * faces_ref[d, x]
            sface_ref[4, x] = scale * deep
            sface_ref[5, x] = scale * shallow
            near = {}
            for k in range(4):
                value = basis_ref[k, x]
                near[k] = (
                    deep * pltpu.roll(value, depth - 1, 1)
                    + shallow * pltpu.roll(value, 1, 1)
                    - diag * value
                )
            for i in range(2):
                own_up, own_down = shift_rows(basis_ref[i, x])
                side_up, side_down = shift_rows(basis_ref[2 + i, x])
                far = None
                for face, own, side, swap_at, far_at in (
                    (faces_ref[3, x], own_down, side_down, 0, BLOCK // 2),
                    (faces_ref[2, x], own_up, side_up, BLOCK - 1, BLOCK // 2 - 1),
                ):
                    own, side = face * own, face * side
                    swap, beyond = place == swap_at, place == far_at
                    near[i] = near[i] + jnp.where(swap, side, own)
                    near[2 + i] = near[2 + i] + jnp.where(
                        swap, own, jnp.where(beyond, 0.0, side)
                    )
                    far = jnp.where(beyond, side, 0.0 if far is None else far)
                near[4 + i] = far
            nodes = (own_node(x), side_node(x), 2 * own_node(x) - side_node(x))
            for other, d in ((x - 1, 1), (x + 1, 0)):
                if not 0 <= other < cell_rows:
                    continue
                face = faces_ref[d, x]
                for i, node in enumerate((own_node(other), side_node(other))):
                    kind = nodes.index(node)
                    for j in range(2):
                        table = kind + 2 * j if kind < 2 else 6 + j
                        part = face * basis_ref[2 * j + i, other]
                        near[table] = near[table] + part if table in near else part
            for table, _, _ in near_terms(x):
                back_ref[table, x] = near[table]
                value = scale * near[table]
                forward_ref[table, x] = basis_ref[table, x] + value if table < 4 else value
            edge_ref[2, x : x + 1, :] = faces_ref[3, x, 0:1, :]
            edge_ref[3, x : x + 1, :] = faces_ref[2, x, cell_cols - 1 : cell_cols, :]
            sedge_ref[0, x : x + 1, :] = sface_ref[3, x, 0:1, :]
            sedge_ref[1, x : x + 1, :] = sface_ref[2, x, cell_cols - 1 : cell_cols, :]
        edge_ref[0] = faces_ref[1, 0]
        edge_ref[1] = faces_ref[0, cell_rows - 1]

    outs = [
        (faces.shape, F32),
        ((tables, *block), F32),
        ((tables, *block), F32),
        (block, F32),
        (block, F32),
        ((4, cell_cols, depth), F32),
        ((2, cell_rows, depth), F32),
        ((TILE, slots), F32),
        ((2 * slots, LANES), BF16),
    ]
    sfaces, forward, back, ssource, scale, edge_faces, sedges, frac_pack, node_hot = run(
        kernel_q,
        outs,
        (
            faces,
            accum,
            basis,
            matrix_source,
            hot_row,
            hot_depth,
            frac_link.reshape(small),
            frac_accum.reshape(small),
            frac_trans,
            hot_node,
            frac_count,
        ),
        smem=(10,),
        scratch=(pltpu.VMEM((cells, depth), F32),),
    )

    layer = (slice(0, layer_rows), slice(0, LANES))

    def widen_layer(value, start):
        first = start * edge_size
        parts = [
            value[first + i * cell_cols : first + (i + 1) * cell_cols, :]
            for i in range(len(spans))
        ]
        return jnp.concatenate(parts, axis=1)


    def rims_of(lay_refs, blk_even, blk_odd):
        lay_low, lay_high = lay_sides(lay_refs, layer)
        blk_low, blk_high = blk_sides(blk_even, blk_odd, layer)

        def pick(value):
            return lambda k: widen_layer(value, k)

        return pick(lay_low), pick(lay_high), pick(blk_low), pick(blk_high)

    last = cell_rows - 1

    def kernel_b(
        sface_ref, forward_ref, back_ref, ssource_ref, edge_ref, sedge_ref, node_ref, turned_ref,
        weight_ref, frac_ref, fsrc_ref, own_ref, joined_ref, blk_even, blk_odd, *refs,
    ):
        lay_refs = refs[:lay_pairs]
        p2_ref, rows_ref, f_ref, tile_ref, parts_ref = refs[lay_pairs : lay_pairs + 5]
        loads = refs[lay_pairs + 5 :]
        at_tile = (slice(layer_rows, layer_rows + TILE), slice(0, LANES))
        low, high = blk_sides(blk_even, blk_odd, at_tile)
        table = join_lanes(joined_ref[...], low, high)
        parts = coarse_parts(table)
        for i, part in enumerate(parts):
            parts_ref[i] = part
        second = coarse_solve(table, parts)
        fields = Fields(second, cell_rows, cell_cols)
        x_low, x_high, y_low, y_high = rims_of(lay_refs, blk_even, blk_odd)
        left_rim = sface_ref[1, 0] * fields.column(-1, x_low)
        right_rim = sface_ref[0, last] * fields.column(cell_rows, x_high)
        low_rim = sedge_ref[0] * fields.row(-1, y_low)
        high_rim = sedge_ref[1] * fields.row(cell_cols, y_high)

        couple = frac_ref[0:1, :]
        pressure_at = nodes_at_slots(second, node_ref[...], weight_ref[...])
        fracture = frac_ref[1:2, :] * (as_line(fsrc_ref[...]) + couple * pressure_at)
        f_ref[...] = fracture
        linked = slots_at_nodes(couple * fracture, turned_ref[...], weight_ref[...])

        def columns():
            for x in range(cell_rows):
                value = ssource_ref[x] + fields.terms(x, lambda t: forward_ref[t, x])
                if x == 0:
                    value = value + left_rim
                if x == last:
                    value = value + right_rim
                value = add_edge_rows(value, low_rim[x : x + 1, :], high_rim[x : x + 1, :])
                p2_ref[x] = value
                rows_ref[0, x : x + 1, :] = value[0:1, :]
                rows_ref[1, x : x + 1, :] = value[cell_cols - 1 : cell_cols, :]
                if x == 0:
                    yield basis_terms(-1, edge_ref[0] * value, x_low)
                if x == last:
                    yield basis_terms(cell_rows, edge_ref[1] * value, x_high)
                yield value, [(kind, node, back_ref[t, x]) for t, kind, node in near_terms(x)]

        def rows():
            yield -1, edge_ref[2] * rows_ref[0], y_low
            yield cell_cols, edge_ref[3] * rows_ref[1], y_high

        tile = restrict_tile(columns(), rows, cell_rows, cell_cols) + linked
        tile = tile + jnp.where(iota((TILE, LANES), 1) < TILE, own_ref[...], 0.0)
        tile_ref[...] = tile
        even = is_even("lay")
        edges = (even * last, (1 - even) * last)
        for load, edge in zip(loads, edges):
            for i, span in enumerate(spans):
                load[i * cell_cols : (i + 1) * cell_cols, :] = p2_ref[edge, :, span]
            load[edge_size:, :] = pack_slots(tile, fracture)

    parts_shape = (5, TILE, LANES)
    row_pair = (2, cell_rows, depth)
    outs = [(block, F32), (row_pair, F32), ((1, slots), F32), ((TILE, LANES), F32)]
    outs = outs + [(parts_shape, F32)] + [(load_two, F32)] * lay_pairs
    pressure, edge_rows, fracture, tile_two, coarse, *loads = run(
        kernel_b,
        outs,
        (
            sfaces, forward, back, ssource, edge_faces, sedges, hot_node, node_hot,
            node_weight, frac_pack, slot_source, tile_own, joined_one, *blk_one, *lay_one,
        ),
    )
    lay_two = swap_pairs(loads[0], loads[-1], "lay")

    tail_rows = (slice(edge_size, edge_size + TILE), slice(0, LANES))

    def kernel_f(tile_ref, rows_ref, *refs):
        got, (join_ref, even_ref, odd_ref) = refs[:-3], refs[-3:]
        low, high = lay_sides(got, tail_rows)
        joined = join_rows(tile_ref[...], low, high)
        join_ref[...] = joined
        even = is_even("blk")
        tail = jnp.where(iota((TILE, LANES), 1) < LANES // 2, joined, got[0][tail_rows])
        for ref, side in ((even_ref, even), (odd_ref, 1 - even)):
            for i, span in enumerate(spans):
                ref[i * cell_rows : (i + 1) * cell_rows, :] = rows_ref[side, :, span]
            ref[edge_size:, :] = tail

    outs = [((TILE, LANES), F32), (load_two, F32), (load_two, F32)]
    joined_two, even_two, odd_two = run(kernel_f, outs, (tile_two, edge_rows, *lay_two))
    blk_two = swap_pairs(even_two, odd_two, "blk")

    def kernel_m(
        sface_ref, ssource_ref, scale_ref, p2_ref, f_ref, row_ref, depth_ref, frac_ref, peer_ref,
        base_ref, at_ref, high_ref, low_ref,
    ):
        owner = lax.axis_index("blk") * lay_size + lax.axis_index("lay")
        peer = as_line(peer_ref[...] - (owner - 1) * slots)
        low_ref[...] = (
            (iota((LANES, peer.shape[1]), 0) == jnp.bitwise_and(peer, LANES - 1))
            .astype(F32)
            .astype(BF16)
        )
        high_ref[...] = lax.shift_right_logical(peer, 7)
        hot_row, hot_depth = row_ref[...], depth_ref[...]
        flat = p2_ref[...].reshape(cells, depth)
        at_ref[...] = gather_cells([flat], hot_row, hot_depth)[0]
        linked = scatter_cells(frac_ref[0:1, :] * f_ref[...], hot_row, hot_depth)
        for x in range(cell_rows):
            centre = p2_ref[x]
            left = p2_ref[x - 1] if x else None
            right = p2_ref[x + 1] if x < last else None
            around = neighbour_sum(sface_ref, x, left, centre, right)
            part = linked[x * cell_cols : (x + 1) * cell_cols, :]
            base_ref[x] = ssource_ref[x] + scale_ref[x] * part + (1.0 - OMEGA) * centre + around

    outs = [
        (block, F32),
        ((1, slots), F32),
        ((1, links * slots), jnp.int32),
        ((LANES, links * slots), BF16),
    ]
    base, slot_pressure, peer_high, hot_low = run(
        kernel_m,
        outs,
        (sfaces, ssource, scale, pressure, fracture, hot_row, hot_depth, frac_pack, frac_peer),
    )
    ring = []
    if lay_size != 2:
        owners = lax.axis_size("blk") * lay_size
        ahead = [(i, i + 1) for i in range(owners - 1)]
        line = fracture.reshape(small)
        ring = [
            lax.ppermute(line, ("blk", "lay"), ahead),
            lax.ppermute(line, ("blk", "lay"), [(b, a) for a, b in ahead]),
        ]

    def kernel_c(
        sface_ref, forward_ref, base_ref, sedge_ref, node_ref, weight_ref, frac_ref, high_ref,
        low_ref, fsrc_ref, trans_ref, f_ref, at_ref, joined_ref, parts_ref,
        one_even, one_odd, two_even, two_odd, *refs,
    ):
        lay_first, lay_second = refs[:lay_pairs], refs[lay_pairs : 2 * lay_pairs]
        ring_refs = refs[2 * lay_pairs : -5]
        p_hbm, f_hbm, p_out, f_out, sems = refs[-5:]
        low, high = blk_sides(two_even, two_odd, tail_rows)
        tile = join_lanes(joined_ref[...], low, high)
        second = coarse_solve(tile, [parts_ref[i] for i in range(5)])
        fields = Fields(second, cell_rows, cell_cols)
        x_low, x_high, y_low, y_high = rims_of(lay_first, one_even, one_odd)
        window = (slice(0, edge_size), slice(0, LANES))
        p_left, p_right = [widen_layer(value, 0) for value in lay_sides(lay_second, window)]
        p_low, p_high = [widen_layer(value, 0) for value in blk_sides(two_even, two_odd, window)]

        left_rim = sface_ref[1, 0] * (p_left + fields.column(-1, x_low))
        right_rim = sface_ref[0, last] * (p_right + fields.column(cell_rows, x_high))
        low_rim = sedge_ref[0] * (p_low + fields.row(-1, y_low))
        high_rim = sedge_ref[1] * (p_high + fields.row(cell_cols, y_high))
        pressure_at = at_ref[...] + nodes_at_slots(second, node_ref[...], weight_ref[...])
        mine = as_rows(f_ref[...], LANES)
        if ring_refs:
            before, after = ring_refs[0][...], ring_refs[1][...]
        else:
            partner = lay_second[0][tail_rows]
            before = unpack_slots(by_parity(is_even("lay"), low, partner))
            after = unpack_slots(by_parity(is_even("lay"), partner, high))
        width = mine.shape[0]
        wide = jnp.concatenate(
            [before, mine, after]
            + [jnp.zeros((-3 * width % TILE, LANES), F32)] * (3 * width % TILE > 0),
            axis=0,
        )
        product = jnp.dot(stacked([wide]), low_ref[...], preferred_element_type=F32)
        picked = unstack(product, wide.shape[0])[0]
        match = iota(picked.shape, 0) == high_ref[...]
        peers = jnp.sum(jnp.where(match, picked, 0.0), axis=0, keepdims=True)
        flux = as_line(fsrc_ref[...]) + frac_ref[0:1, :] * pressure_at
        for j in range(links):
            flux = flux + trans_ref[j : j + 1, :] * peers[:, j * slots : (j + 1) * slots]
        result = (1.0 - OMEGA) * f_ref[...] + frac_ref[1:2, :] * flux
        copies = []
        for x in range(cell_rows):
            value = base_ref[x] + fields.terms(x, lambda t: forward_ref[t, x])
            if x == 0:
                value = value + left_rim
            if x == last:
                value = value + right_rim
            p_out[x] = add_edge_rows(value, low_rim[x : x + 1, :], high_rim[x : x + 1, :])
            if (x + 1) % piece == 0:
                part = pl.ds(x + 1 - piece, piece)
                copies.append(
                    pltpu.make_async_copy(p_out.at[part], p_hbm.at[part], sems.at[x // piece])
                )
                copies[-1].start()
        f_out[...] = as_rows(result, LANES)
        copies.append(pltpu.make_async_copy(f_out, f_hbm, sems.at[pieces]))
        copies[-1].start()
        for copy in copies:
            copy.wait()

    final, frac_final = run(
        kernel_c,
        [(block, F32), (small, F32)],
        (
            sfaces, forward, base, sedges, hot_node, node_weight, frac_pack, peer_high,
            hot_low, slot_source, frac_trans, fracture, slot_pressure, joined_two, coarse,
            *blk_one, *blk_two, *lay_one, *lay_two, *ring,
        ),
        scratch=(
            pltpu.VMEM(block, F32),
            pltpu.VMEM(small, F32),
            pltpu.SemaphoreType.DMA((pieces + 1,)),
        ),
        out_place=(0, 1),
    )
    return final, frac_final.reshape(slots)


def solution(mesh):
    return jax.shard_map(
        local,
        mesh=mesh,
        in_specs=(
            P("lay", "blk", None),
            P("lay", "blk", None),
            P(None, "lay", "blk", None),
            P(None, "lay", "blk", None),
            P("lay", "blk"),
            P(None, "lay", "blk"),
            P(("blk", "lay")),
            P(("blk", "lay")),
            P(("blk", "lay")),
            P(None, ("blk", "lay")),
            P(("blk", "lay")),
            P(None, ("blk", "lay")),
            P(("blk", "lay")),
        ),
        out_specs=(P("lay", "blk", None), P(("blk", "lay"))),
        check_vma=False,
    )
```

```python
import jax
import jax.numpy as jnp
from jax import lax
from jax.experimental import pallas as pl
from jax.experimental.pallas import tpu as pltpu
from jax.sharding import PartitionSpec as P

BLOCK = 4
OMEGA = 0.8
TILE = 8
LANES = 128
F32 = jnp.float32
BF16 = jnp.bfloat16


def pair_lists(count):
    even = [(i, i ^ 1) for i in range(count) if i ^ 1 < count]
    odd = [(i, i + 1 if i % 2 else i - 1) for i in range(1, count)]
    return even, [(a, b) for a, b in odd if 0 < b < count]


def swap_pairs(even_load, odd_load, axis):
    even, odd = pair_lists(lax.axis_size(axis))
    got = [lax.ppermute(even_load, axis, even)]
    if odd:
        got.append(lax.ppermute(odd_load, axis, odd))
    return got


def run(kernel, outs, args, scratch=(), smem=(), in_place=(), out_place=(), aliases={}):
    spec = pl.BlockSpec(memory_space=pltpu.VMEM)
    scalar = pl.BlockSpec(memory_space=pltpu.SMEM)
    there = pl.BlockSpec(memory_space=pltpu.HBM)

    def place(i):
        return scalar if i in smem else there if i in in_place else spec

    return pl.pallas_call(
        kernel,
        out_shape=[jax.ShapeDtypeStruct(shape, dtype) for shape, dtype in outs],
        in_specs=[place(i) for i in range(len(args))],
        out_specs=[there if i in out_place else spec for i in range(len(outs))],
        scratch_shapes=list(scratch),
        input_output_aliases=aliases,
        compiler_params=pltpu.CompilerParams(vmem_limit_bytes=24 << 20),
    )(*args)


def iota(shape, dim):
    return lax.broadcasted_iota(jnp.int32, shape, dim)


def own_node(cell):
    return cell // BLOCK


def side_node(cell):
    return cell // BLOCK + (-1 if cell % BLOCK < BLOCK // 2 else 1)


def near_terms(x):
    own, near = own_node(x) + 2, side_node(x) + 2
    terms = [(0, 0, own), (1, 0, near), (2, 1, own), (3, 1, near), (4, 2, own), (5, 2, near)]
    if 0 < x % BLOCK < BLOCK - 1:
        terms = terms + [(6, 0, 2 * own - near), (7, 1, 2 * own - near)]
    return terms


def own_nodes(cells):
    return lax.shift_right_arithmetic(cells, 2)


def side_nodes(cells):
    low = jnp.bitwise_and(cells, BLOCK - 1) < BLOCK // 2
    return own_nodes(cells) + jnp.where(low, -1, 1)


def node_masks(cells):
    index = iota((cells, LANES), 0)
    lane = iota((cells, LANES), 1)
    own, side = own_nodes(index) + 2, side_nodes(index) + 2
    return own == lane, side == lane, 2 * own - side == lane


def fold_lanes(value):
    total = value[:, :LANES]
    for start in range(LANES, value.shape[1], LANES):
        total = total + value[:, start : start + LANES]
    return total


def by_parity(is_even, even_value, odd_value):
    return jnp.where(jnp.full(even_value.shape, is_even, jnp.int32) > 0, even_value, odd_value)


def low_high(is_even, even_got, odd_got):
    low = by_parity(is_even, odd_got, even_got)
    high = by_parity(is_even, even_got, odd_got)
    return low, high


def basis_terms(x, residual, weight):
    own, near = own_node(x) + 2, side_node(x) + 2
    nodes = (own, near, own, near)
    return residual, [(k // 2, nodes[k], weight(k)) for k in range(4)]


def restrict_tile(columns, rows, cell_rows, cell_cols):
    sums = {}
    for value, terms in columns:
        for kind, node, weight in terms:
            part = fold_lanes(weight * value)
            key = (kind, node)
            sums[key] = sums[key] + part if key in sums else part
    masks = node_masks(cell_cols)
    row_index = iota((TILE, LANES), 0)
    tile = jnp.zeros((TILE, LANES), F32)
    nodes = sorted({node for _, node in sums})
    wide = {}
    if rows:
        lane = iota((cell_rows, LANES), 1)
        for y, residual, weight in rows():
            for k in range(4):
                node = (own_node(y) if k < 2 else side_node(y)) + 2
                part = jnp.sum(fold_lanes(weight(k) * residual), axis=1, keepdims=True)
                part = jnp.where(lane == node, part, 0.0)
                wide[k % 2] = wide[k % 2] + part if k % 2 in wide else part
        x_index = iota((cell_rows, LANES), 0)
        x_nodes = (own_nodes(x_index) + 2, side_nodes(x_index) + 2)
    for node in nodes:
        total = jnp.zeros((cell_cols, LANES), F32)
        for kind in range(3):
            if (kind, node) in sums:
                lane_sum = jnp.sum(sums[(kind, node)], axis=1, keepdims=True)
                total = total + jnp.where(masks[kind], lane_sum, 0.0)
        line = jnp.sum(total, axis=0, keepdims=True)
        if rows:
            extra = jnp.where(x_nodes[0] == node, wide[0], 0.0) + jnp.where(
                x_nodes[1] == node, wide[1], 0.0
            )
            line = line + jnp.sum(extra, axis=0, keepdims=True)
        tile = jnp.where(row_index == node, line, tile)
    return tile


def join_rows(tile, low, high):
    row = iota((TILE, LANES), 0)
    half = TILE // 2
    return (
        tile
        + jnp.where(row < half, pltpu.roll(low, half, 0), 0.0)
        + jnp.where(row >= half, pltpu.roll(high, half, 0), 0.0)
    )


def join_lanes(tile, low, high):
    part = jnp.bitwise_and(iota((TILE, LANES), 1), TILE - 1)
    half = TILE // 2
    return (
        tile
        + jnp.where(part < half, pltpu.roll(low, LANES - half, 1), 0.0)
        + jnp.where(part >= half, pltpu.roll(high, half, 1), 0.0)
    )


def coarse_parts(table):
    lane = iota((TILE, LANES), 1)
    diag = pltpu.roll(table, LANES - TILE, 1)
    live = (lane < TILE) & (diag > 0.0)
    parts = [jnp.where(live, 1.0 / jnp.where(live, diag, 1.0), 0.0)]
    for direction in range(4):
        ratio = pltpu.roll(table, LANES - TILE * (2 + direction), 1)
        parts.append(jnp.where(lane < TILE, ratio, 0.0))
    return parts


def coarse_solve(tile, parts):
    first = tile * parts[0]
    near = (
        pltpu.roll(first, 1, 0),
        pltpu.roll(first, TILE - 1, 0),
        pltpu.roll(first, 1, 1),
        pltpu.roll(first, LANES - 1, 1),
    )
    second = first
    for direction in range(4):
        second = second + parts[1 + direction] * near[direction]
    return second


class Fields:
    def __init__(self, second, cell_rows, cell_cols):
        masks = node_masks(cell_cols)
        self.columns = {}
        for node in range(1, TILE - 1):
            line = jnp.broadcast_to(second[node : node + 1, :], (cell_cols, LANES))
            for kind in range(3):
                self.columns[(kind, node)] = jnp.sum(
                    jnp.where(masks[kind], line, 0.0), axis=1, keepdims=True
                )
        x_index = iota((cell_rows, LANES), 0)
        self.wide = []
        for nodes in (own_nodes(x_index) + 2, side_nodes(x_index) + 2):
            value = jnp.zeros((cell_rows, LANES), F32)
            for node in range(1, TILE - 1):
                value = jnp.where(nodes == node, second[node : node + 1, :], value)
            self.wide.append(value)

    def column(self, x, weight):
        own, side = own_node(x) + 2, side_node(x) + 2
        return (
            weight(0) * self.columns[(0, own)]
            + weight(1) * self.columns[(0, side)]
            + weight(2) * self.columns[(1, own)]
            + weight(3) * self.columns[(1, side)]
        )

    def terms(self, x, weight):
        total = None
        for table, kind, node in near_terms(x):
            part = weight(table) * self.columns[(kind, node)]
            total = part if total is None else total + part
        return total

    def row(self, y, weight):
        lane = iota(self.wide[0].shape, 1)

        def pick(kind, node):
            return jnp.sum(jnp.where(lane == node, self.wide[kind], 0.0), axis=1, keepdims=True)

        own, side = own_node(y) + 2, side_node(y) + 2
        return (
            weight(0) * pick(0, own)
            + weight(1) * pick(1, own)
            + weight(2) * pick(0, side)
            + weight(3) * pick(1, side)
        )


def shift_rows(value):
    row = iota((TILE, value.shape[1]), 0)
    parts = [value[i : i + TILE, :] for i in range(0, value.shape[0], TILE)]
    up = [pltpu.roll(part, TILE - 1, 0) for part in parts]
    down = [pltpu.roll(part, 1, 0) for part in parts]
    above = [
        jnp.where(row == TILE - 1, end, part) for end, part in zip(up[1:] + [0.0], up)
    ]
    below = [jnp.where(row == 0, end, part) for end, part in zip([0.0] + down[:-1], down)]
    return jnp.concatenate(above, axis=0), jnp.concatenate(below, axis=0)


def neighbour_sum(faces, x, left, centre, right):
    depth = centre.shape[1]
    above, below = shift_rows(centre)
    total = faces[2, x] * above + faces[3, x] * below
    total = total + faces[4, x] * pltpu.roll(centre, depth - 1, 1)
    total = total + faces[5, x] * pltpu.roll(centre, 1, 1)
    if right is not None:
        total = total + faces[0, x] * right
    if left is not None:
        total = total + faces[1, x] * left
    return total


def add_edge_rows(value, low_row, high_row):
    row = iota((TILE, value.shape[1]), 0)
    low = value[:TILE, :] + jnp.where(row == 0, low_row, 0.0)
    high = value[-TILE:, :] + jnp.where(row == TILE - 1, high_row, 0.0)
    return jnp.concatenate([low, value[TILE:-TILE, :], high] if value.shape[0] > 2 * TILE else [low, high], axis=0)


def split3(value):
    high = value.astype(BF16)
    rest = value - high.astype(F32)
    mid = rest.astype(BF16)
    return high, mid, (rest - mid.astype(F32)).astype(BF16)


def stacked(values, count=3):
    return jnp.concatenate([part for value in values for part in split3(value)[:count]], axis=0)


def unstack(product, rows, count=3):
    parts = [product[i : i + rows, :] for i in range(0, product.shape[0], rows)]
    return [sum(parts[i + 1 : i + count], parts[i]) for i in range(0, len(parts), count)]


def gather_cells(fields, hot_row, hot_depth, count=3):
    product = jnp.dot(stacked(fields, count), hot_depth, preferred_element_type=F32)
    at_row = hot_row.astype(F32)
    return [
        jnp.sum(picked * at_row, axis=0, keepdims=True)
        for picked in unstack(product, fields[0].shape[0], count)
    ]


def scatter_cells(values, hot_row, hot_depth):
    spread = jnp.concatenate([hot_row * part for part in split3(values)], axis=0)
    product = lax.dot_general(
        spread, hot_depth, (((1,), (1,)), ((), ())), preferred_element_type=F32
    )
    return unstack(product, hot_row.shape[0])[0]


def nodes_at_slots(second, hot_node, node_weight):
    product = jnp.dot(stacked([second]), hot_node, preferred_element_type=F32)
    picked = unstack(product, TILE)[0]
    total = jnp.sum(picked * node_weight, axis=0, keepdims=True)
    half = total.shape[1] // 2
    return total[:, :half] + total[:, half:]


def slots_at_nodes(values, node_hot, node_weight):
    weighted = node_weight * jnp.concatenate([values, values], axis=1)
    product = jnp.dot(stacked([weighted]), node_hot, preferred_element_type=F32)
    return unstack(product, TILE)[0]


def as_line(value):
    return jnp.concatenate([value[i : i + 1, :] for i in range(value.shape[0])], axis=1)


def pack_slots(tile, line):
    rows = as_rows(line, LANES)
    wide = jnp.concatenate([pltpu.roll(rows, LANES // 2, 1), rows], axis=0)
    return jnp.where(iota((TILE, LANES), 1) < LANES // 2, tile, wide)


def unpack_slots(tile):
    half = TILE // 2
    low = iota((half, LANES), 1) < LANES // 2
    return jnp.where(low, pltpu.roll(tile[:half, :], LANES // 2, 1), tile[half:, :])


def as_rows(line, width):
    return jnp.concatenate(
        [line[:, start : start + width] for start in range(0, line.shape[1], width)], axis=0
    )


def local(
    matrix_source,
    accum,
    faces,
    basis,
    coarse_diag,
    coarse_ratio,
    frac_source,
    frac_accum,
    frac_link,
    frac_trans,
    frac_cell,
    frac_peer,
    frac_count,
):
    slots = frac_source.shape[0]
    cell_rows, cell_cols, depth = matrix_source.shape
    cells = cell_rows * cell_cols
    node_rows, node_cols = cell_rows // BLOCK, cell_cols // BLOCK
    assert node_rows + 4 == TILE and node_cols + 4 == TILE
    assert depth & (depth - 1) == 0 and cell_rows == cell_cols
    depth_bits = depth.bit_length() - 1
    lay_size = lax.axis_size("lay")
    lay_pairs = len([p for p in pair_lists(lay_size) if p])
    spans = [slice(start, start + LANES) for start in range(0, depth, LANES)]
    layer_rows = 4 * len(spans) * cell_cols
    load_one = (layer_rows + TILE, LANES)
    edge_size = len(spans) * cell_cols
    load_two = (edge_size + TILE, LANES)
    assert slots == TILE * LANES // 2
    block = matrix_source.shape

    def is_even(axis):
        return 1 - jnp.bitwise_and(lax.axis_index(axis), 1)

    piece = BLOCK
    pieces = cell_rows // piece

    small = (slots // LANES, LANES)
    slot_arrays = [frac_cell.reshape(small)]
    slot_kinds = len(slot_arrays)

    def kernel_a(basis_hbm, source_hbm, cdiag_hbm, ratio_hbm, *refs):
        slot_hbm, refs = refs[:slot_kinds], refs[slot_kinds:]
        (basis_ref, source_ref, tile_ref), refs = refs[:3], refs[3:]
        slot_refs, refs = refs[:slot_kinds], refs[slot_kinds:]
        loads, (cdiag_ref, ratio_ref, sems, small_sems) = refs[:-4], refs[-4:]
        copies = []
        for i in range(pieces):
            part = pl.ds(i * piece, piece)
            copies.append(
                (
                    pltpu.make_async_copy(source_hbm.at[part], source_ref.at[part], sems.at[0, i]),
                    pltpu.make_async_copy(
                        basis_hbm.at[:, part], basis_ref.at[:, part], sems.at[1, i]
                    ),
                )
            )
        small_copies = [
            pltpu.make_async_copy(cdiag_hbm, cdiag_ref, small_sems.at[0]),
            pltpu.make_async_copy(ratio_hbm, ratio_ref, small_sems.at[1]),
        ]
        for i, (there, here) in enumerate(zip(slot_hbm, slot_refs)):
            small_copies.append(pltpu.make_async_copy(there, here, small_sems.at[2 + i]))
        for pair in copies[:1] + [small_copies] + copies[1:]:
            for copy in pair:
                copy.start()

        def widen(value):
            lines = jnp.concatenate(
                [
                    jnp.zeros((node_rows, 2), F32),
                    value,
                    jnp.zeros((node_rows, TILE - 2 - node_cols), F32),
                ],
                axis=1,
            )
            edge = jnp.zeros((2, TILE), F32)
            return jnp.concatenate([edge, lines, edge], axis=0)

        def column(x):
            if x % piece == 0:
                for copy in copies[x // piece]:
                    copy.wait()
            return basis_terms(x, source_ref[x], lambda k: basis_ref[k, x])

        for copy in small_copies:
            copy.wait()
        parts = [jnp.zeros((TILE, TILE), F32), widen(cdiag_ref[...])]
        parts = parts + [widen(ratio_ref[d]) for d in range(4)]
        parts.append(jnp.zeros((TILE, LANES - TILE * len(parts)), F32))
        table = jnp.concatenate(parts, axis=1)

        tile = restrict_tile((column(x) for x in range(cell_rows)), None, cell_rows, cell_cols)
        tile = tile + table
        tile_ref[...] = tile
        even = is_even("lay")
        edges = (even * (cell_rows - 1), (1 - even) * (cell_rows - 1))
        for load, edge in zip(loads, edges):
            for k in range(4):
                for i, span in enumerate(spans):
                    start = (k * len(spans) + i) * cell_cols
                    load[start : start + cell_cols, :] = basis_ref[k, edge, :, span]
            load[layer_rows:, :] = tile

    outs = [(basis.shape, F32), (block, F32), ((TILE, LANES), F32)]
    outs = outs + [(value.shape, value.dtype) for value in slot_arrays]
    outs = outs + [(load_one, F32)] * lay_pairs
    basis, matrix_source, tile_own, *rest = run(
        kernel_a,
        outs,
        [
            pltpu.with_memory_space_constraint(value, pltpu.HBM)
            for value in (basis, matrix_source, coarse_diag, coarse_ratio, *slot_arrays)
        ],
        scratch=(
            pltpu.VMEM(coarse_diag.shape, F32),
            pltpu.VMEM(coarse_ratio.shape, F32),
            pltpu.SemaphoreType.DMA((2, pieces)),
            pltpu.SemaphoreType.DMA((2 + slot_kinds,)),
        ),
        in_place=range(4 + slot_kinds),
    )
    slot_cell, *loads = rest
    slot_source = frac_source.reshape(small)
    lay_one = swap_pairs(loads[0], loads[-1], "lay")

    def lay_sides(refs, window):
        even = is_even("lay")
        first = refs[0][window]
        second = refs[1][window] if len(refs) > 1 else jnp.zeros(first.shape, F32)
        return low_high(even, first, second)

    def blk_sides(even_ref, odd_ref, window):
        return low_high(is_even("blk"), even_ref[window], odd_ref[window])


    links = frac_trans.shape[0]

    def kernel_p(
        basis_ref, cell_ref, row_ref, depth_ref, node_ref, weight_ref, *rim_refs
    ):
        blk_even = is_even("blk")
        rim_edges = (blk_even * (cell_cols - 1), (1 - blk_even) * (cell_cols - 1))
        for x in range(cell_rows):
            for ref, edge in zip(rim_refs, rim_edges):
                for k in range(4):
                    row = basis_ref[k, x, pl.ds(edge, 1), :]
                    for i, span in enumerate(spans):
                        line = (k * len(spans) + i) * cell_rows + x
                        ref[line : line + 1, :] = row[:, span]
        cell = as_line(cell_ref[...])
        at_row = lax.shift_right_logical(cell, depth_bits)
        at_depth = jnp.bitwise_and(cell, depth - 1)
        hot_row = (iota((cells, slots), 0) == at_row).astype(F32).astype(BF16)
        hot_depth = (iota((depth, slots), 0) == at_depth).astype(F32).astype(BF16)
        row_ref[...] = hot_row
        depth_ref[...] = hot_depth
        fields = [basis_ref[k].reshape(cells, depth) for k in range(4)]
        weights = gather_cells(fields, hot_row, hot_depth, 2)
        along = jnp.bitwise_and(at_row, cell_cols - 1)
        across = lax.shift_right_logical(at_row, cell_cols.bit_length() - 1)
        lane = iota((LANES, slots), 0)
        line = iota((TILE, slots), 0)
        match = (own_nodes(across) + 2 == line, side_nodes(across) + 2 == line)
        for j, nodes in enumerate((own_nodes(along), side_nodes(along))):
            part = slice(j * slots, (j + 1) * slots)
            node_ref[:, part] = (lane == nodes + 2).astype(F32).astype(BF16)
            weight_ref[:, part] = jnp.where(match[0], weights[2 * j], 0.0) + jnp.where(
                match[1], weights[2 * j + 1], 0.0
            )

    outs = [
        ((cells, slots), BF16),
        ((depth, slots), BF16),
        ((LANES, 2 * slots), BF16),
        ((TILE, 2 * slots), F32),
        (load_one, F32),
        (load_one, F32),
    ]
    hot_row, hot_depth, hot_node, node_weight, rim_even, rim_odd = run(
        kernel_p, outs, (basis, slot_cell)
    )

    def kernel_e(tile_ref, rim_even_ref, rim_odd_ref, *refs):
        got, (join_ref, even_ref, odd_ref) = refs[:-3], refs[-3:]
        low, high = lay_sides(got, (slice(layer_rows, layer_rows + TILE), slice(0, LANES)))
        joined = join_rows(tile_ref[...], low, high)
        join_ref[...] = joined
        even_ref[layer_rows:, :] = joined
        odd_ref[layer_rows:, :] = joined

    outs = [((TILE, LANES), F32), (load_one, F32), (load_one, F32)]
    joined_one, even_one, odd_one = run(
        kernel_e, outs, (tile_own, rim_even, rim_odd, *lay_one), aliases={1: 1, 2: 2}
    )
    blk_one = swap_pairs(even_one, odd_one, "blk")

    tables = 8

    def kernel_q(
        faces_ref, accum_ref, basis_ref, source_ref, row_ref, depth_ref, link_ref, facc_ref,
        trans_ref, node_ref, count_ref, sface_ref, forward_ref, back_ref, ssource_ref, scale_ref, edge_ref,
        sedge_ref, frac_ref, turned_ref, linked_ref,
    ):
        turned_ref[...] = node_ref[...].astype(F32).T.astype(BF16)
        live = (iota((1, slots), 1) < count_ref[0]).astype(F32)
        couple = live * as_line(link_ref[...])
        frac_diag = as_line(facc_ref[...]) + couple
        for j in range(links):
            frac_diag = frac_diag + trans_ref[j : j + 1, :]
        frac_ref[0:1, :] = couple
        frac_ref[1:2, :] = OMEGA * live / frac_diag
        linked_ref[...] = scatter_cells(couple, row_ref[...], depth_ref[...])

        lane = iota((cell_cols, depth), 1)
        place = jnp.bitwise_and(iota((cell_cols, depth), 0), BLOCK - 1)
        for x in range(cell_rows):
            diag = accum_ref[x] + linked_ref[x * cell_cols : (x + 1) * cell_cols, :]
            for d in range(6):
                diag = diag + faces_ref[d, x]
            scale = OMEGA / diag
            scale_ref[x] = scale
            ssource_ref[x] = scale * source_ref[x]
            deep = jnp.where(lane < depth - 1, faces_ref[4, x], 0.0)
            shallow = jnp.where(lane > 0, faces_ref[5, x], 0.0)
            for d in range(4):
                sface_ref[d, x] = scale * faces_ref[d, x]
            sface_ref[4, x] = scale * deep
            sface_ref[5, x] = scale * shallow
            near = {}
            for k in range(4):
                value = basis_ref[k, x]
                near[k] = (
                    deep * pltpu.roll(value, depth - 1, 1)
                    + shallow * pltpu.roll(value, 1, 1)
                    - diag * value
                )
            for i in range(2):
                own_up, own_down = shift_rows(basis_ref[i, x])
                side_up, side_down = shift_rows(basis_ref[2 + i, x])
                far = None
                for face, own, side, swap_at, far_at in (
                    (faces_ref[3, x], own_down, side_down, 0, BLOCK // 2),
                    (faces_ref[2, x], own_up, side_up, BLOCK - 1, BLOCK // 2 - 1),
                ):
                    own, side = face * own, face * side
                    swap, beyond = place == swap_at, place == far_at
                    near[i] = near[i] + jnp.where(swap, side, own)
                    near[2 + i] = near[2 + i] + jnp.where(
                        swap, own, jnp.where(beyond, 0.0, side)
                    )
                    far = jnp.where(beyond, side, 0.0 if far is None else far)
                near[4 + i] = far
            nodes = (own_node(x), side_node(x), 2 * own_node(x) - side_node(x))
            for other, d in ((x - 1, 1), (x + 1, 0)):
                if not 0 <= other < cell_rows:
                    continue
                face = faces_ref[d, x]
                for i, node in enumerate((own_node(other), side_node(other))):
                    kind = nodes.index(node)
                    for j in range(2):
                        table = kind + 2 * j if kind < 2 else 6 + j
                        part = face * basis_ref[2 * j + i, other]
                        near[table] = near[table] + part if table in near else part
            for table, _, _ in near_terms(x):
                back_ref[table, x] = near[table]
                value = scale * near[table]
                forward_ref[table, x] = basis_ref[table, x] + value if table < 4 else value
            edge_ref[2, x : x + 1, :] = faces_ref[3, x, 0:1, :]
            edge_ref[3, x : x + 1, :] = faces_ref[2, x, cell_cols - 1 : cell_cols, :]
            sedge_ref[0, x : x + 1, :] = sface_ref[3, x, 0:1, :]
            sedge_ref[1, x : x + 1, :] = sface_ref[2, x, cell_cols - 1 : cell_cols, :]
        edge_ref[0] = faces_ref[1, 0]
        edge_ref[1] = faces_ref[0, cell_rows - 1]

    outs = [
        (faces.shape, F32),
        ((tables, *block), F32),
        ((tables, *block), F32),
        (block, F32),
        (block, F32),
        ((4, cell_cols, depth), F32),
        ((2, cell_rows, depth), F32),
        ((TILE, slots), F32),
        ((2 * slots, LANES), BF16),
    ]
    sfaces, forward, back, ssource, scale, edge_faces, sedges, frac_pack, node_hot = run(
        kernel_q,
        outs,
        (
            faces,
            accum,
            basis,
            matrix_source,
            hot_row,
            hot_depth,
            frac_link.reshape(small),
            frac_accum.reshape(small),
            frac_trans,
            hot_node,
            frac_count,
        ),
        smem=(10,),
        scratch=(pltpu.VMEM((cells, depth), F32),),
    )

    layer = (slice(0, layer_rows), slice(0, LANES))

    def widen_layer(value, start):
        first = start * edge_size
        parts = [
            value[first + i * cell_cols : first + (i + 1) * cell_cols, :]
            for i in range(len(spans))
        ]
        return jnp.concatenate(parts, axis=1)


    def rims_of(lay_refs, blk_even, blk_odd):
        lay_low, lay_high = lay_sides(lay_refs, layer)
        blk_low, blk_high = blk_sides(blk_even, blk_odd, layer)

        def pick(value):
            return lambda k: widen_layer(value, k)

        return pick(lay_low), pick(lay_high), pick(blk_low), pick(blk_high)

    last = cell_rows - 1

    def kernel_b(
        sface_ref, forward_ref, back_ref, ssource_ref, edge_ref, sedge_ref, node_ref, turned_ref,
        weight_ref, frac_ref, fsrc_ref, own_ref, joined_ref, blk_even, blk_odd, *refs,
    ):
        lay_refs = refs[:lay_pairs]
        p2_ref, rows_ref, f_ref, tile_ref, parts_ref = refs[lay_pairs : lay_pairs + 5]
        loads = refs[lay_pairs + 5 :]
        at_tile = (slice(layer_rows, layer_rows + TILE), slice(0, LANES))
        low, high = blk_sides(blk_even, blk_odd, at_tile)
        table = join_lanes(joined_ref[...], low, high)
        parts = coarse_parts(table)
        for i, part in enumerate(parts):
            parts_ref[i] = part
        second = coarse_solve(table, parts)
        fields = Fields(second, cell_rows, cell_cols)
        x_low, x_high, y_low, y_high = rims_of(lay_refs, blk_even, blk_odd)
        left_rim = sface_ref[1, 0] * fields.column(-1, x_low)
        right_rim = sface_ref[0, last] * fields.column(cell_rows, x_high)
        low_rim = sedge_ref[0] * fields.row(-1, y_low)
        high_rim = sedge_ref[1] * fields.row(cell_cols, y_high)

        couple = frac_ref[0:1, :]
        pressure_at = nodes_at_slots(second, node_ref[...], weight_ref[...])
        fracture = frac_ref[1:2, :] * (as_line(fsrc_ref[...]) + couple * pressure_at)
        f_ref[...] = fracture
        linked = slots_at_nodes(couple * fracture, turned_ref[...], weight_ref[...])

        def columns():
            for x in range(cell_rows):
                value = ssource_ref[x] + fields.terms(x, lambda t: forward_ref[t, x])
                if x == 0:
                    value = value + left_rim
                if x == last:
                    value = value + right_rim
                value = add_edge_rows(value, low_rim[x : x + 1, :], high_rim[x : x + 1, :])
                p2_ref[x] = value
                rows_ref[0, x : x + 1, :] = value[0:1, :]
                rows_ref[1, x : x + 1, :] = value[cell_cols - 1 : cell_cols, :]
                if x == 0:
                    yield basis_terms(-1, edge_ref[0] * value, x_low)
                if x == last:
                    yield basis_terms(cell_rows, edge_ref[1] * value, x_high)
                yield value, [(kind, node, back_ref[t, x]) for t, kind, node in near_terms(x)]

        def rows():
            yield -1, edge_ref[2] * rows_ref[0], y_low
            yield cell_cols, edge_ref[3] * rows_ref[1], y_high

        tile = restrict_tile(columns(), rows, cell_rows, cell_cols) + linked
        tile = tile + jnp.where(iota((TILE, LANES), 1) < TILE, own_ref[...], 0.0)
        tile_ref[...] = tile
        even = is_even("lay")
        edges = (even * last, (1 - even) * last)
        for load, edge in zip(loads, edges):
            for i, span in enumerate(spans):
                load[i * cell_cols : (i + 1) * cell_cols, :] = p2_ref[edge, :, span]
            load[edge_size:, :] = pack_slots(tile, fracture)

    parts_shape = (5, TILE, LANES)
    row_pair = (2, cell_rows, depth)
    outs = [(block, F32), (row_pair, F32), ((1, slots), F32), ((TILE, LANES), F32)]
    outs = outs + [(parts_shape, F32)] + [(load_two, F32)] * lay_pairs
    pressure, edge_rows, fracture, tile_two, coarse, *loads = run(
        kernel_b,
        outs,
        (
            sfaces, forward, back, ssource, edge_faces, sedges, hot_node, node_hot,
            node_weight, frac_pack, slot_source, tile_own, joined_one, *blk_one, *lay_one,
        ),
    )
    lay_two = swap_pairs(loads[0], loads[-1], "lay")

    tail_rows = (slice(edge_size, edge_size + TILE), slice(0, LANES))

    def kernel_f(tile_ref, rows_ref, *refs):
        got, (join_ref, even_ref, odd_ref) = refs[:-3], refs[-3:]
        low, high = lay_sides(got, tail_rows)
        joined = join_rows(tile_ref[...], low, high)
        join_ref[...] = joined
        even = is_even("blk")
        tail = jnp.where(iota((TILE, LANES), 1) < LANES // 2, joined, got[0][tail_rows])
        for ref, side in ((even_ref, even), (odd_ref, 1 - even)):
            for i, span in enumerate(spans):
                ref[i * cell_rows : (i + 1) * cell_rows, :] = rows_ref[side, :, span]
            ref[edge_size:, :] = tail

    outs = [((TILE, LANES), F32), (load_two, F32), (load_two, F32)]
    joined_two, even_two, odd_two = run(kernel_f, outs, (tile_two, edge_rows, *lay_two))
    blk_two = swap_pairs(even_two, odd_two, "blk")

    def kernel_m(
        sface_ref, ssource_ref, scale_ref, p2_ref, f_ref, row_ref, depth_ref, frac_ref, peer_ref,
        base_ref, at_ref, high_ref, low_ref,
    ):
        owner = lax.axis_index("blk") * lay_size + lax.axis_index("lay")
        peer = as_line(peer_ref[...] - (owner - 1) * slots)
        low_ref[...] = (
            (iota((LANES, peer.shape[1]), 0) == jnp.bitwise_and(peer, LANES - 1))
            .astype(F32)
            .astype(BF16)
        )
        high_ref[...] = lax.shift_right_logical(peer, 7)
        hot_row, hot_depth = row_ref[...], depth_ref[...]
        flat = p2_ref[...].reshape(cells, depth)
        at_ref[...] = gather_cells([flat], hot_row, hot_depth)[0]
        linked = scatter_cells(frac_ref[0:1, :] * f_ref[...], hot_row, hot_depth)
        for x in range(cell_rows):
            centre = p2_ref[x]
            left = p2_ref[x - 1] if x else None
            right = p2_ref[x + 1] if x < last else None
            around = neighbour_sum(sface_ref, x, left, centre, right)
            part = linked[x * cell_cols : (x + 1) * cell_cols, :]
            base_ref[x] = ssource_ref[x] + scale_ref[x] * part + (1.0 - OMEGA) * centre + around

    outs = [
        (block, F32),
        ((1, slots), F32),
        ((1, links * slots), jnp.int32),
        ((LANES, links * slots), BF16),
    ]
    base, slot_pressure, peer_high, hot_low = run(
        kernel_m,
        outs,
        (sfaces, ssource, scale, pressure, fracture, hot_row, hot_depth, frac_pack, frac_peer),
    )
    ring = []
    if lay_size != 2:
        owners = lax.axis_size("blk") * lay_size
        ahead = [(i, i + 1) for i in range(owners - 1)]
        line = fracture.reshape(small)
        ring = [
            lax.ppermute(line, ("blk", "lay"), ahead),
            lax.ppermute(line, ("blk", "lay"), [(b, a) for a, b in ahead]),
        ]

    def kernel_c(
        sface_ref, forward_ref, base_ref, sedge_ref, node_ref, weight_ref, frac_ref, high_ref,
        low_ref, fsrc_ref, trans_ref, f_ref, at_ref, joined_ref, parts_ref,
        one_even, one_odd, two_even, two_odd, *refs,
    ):
        lay_first, lay_second = refs[:lay_pairs], refs[lay_pairs : 2 * lay_pairs]
        ring_refs = refs[2 * lay_pairs : -5]
        p_hbm, f_hbm, p_out, f_out, sems = refs[-5:]
        low, high = blk_sides(two_even, two_odd, tail_rows)
        tile = join_lanes(joined_ref[...], low, high)
        second = coarse_solve(tile, [parts_ref[i] for i in range(5)])
        fields = Fields(second, cell_rows, cell_cols)
        x_low, x_high, y_low, y_high = rims_of(lay_first, one_even, one_odd)
        window = (slice(0, edge_size), slice(0, LANES))
        p_left, p_right = [widen_layer(value, 0) for value in lay_sides(lay_second, window)]
        p_low, p_high = [widen_layer(value, 0) for value in blk_sides(two_even, two_odd, window)]

        left_rim = sface_ref[1, 0] * (p_left + fields.column(-1, x_low))
        right_rim = sface_ref[0, last] * (p_right + fields.column(cell_rows, x_high))
        low_rim = sedge_ref[0] * (p_low + fields.row(-1, y_low))
        high_rim = sedge_ref[1] * (p_high + fields.row(cell_cols, y_high))
        pressure_at = at_ref[...] + nodes_at_slots(second, node_ref[...], weight_ref[...])
        mine = as_rows(f_ref[...], LANES)
        if ring_refs:
            before, after = ring_refs[0][...], ring_refs[1][...]
        else:
            partner = lay_second[0][tail_rows]
            before = unpack_slots(by_parity(is_even("lay"), low, partner))
            after = unpack_slots(by_parity(is_even("lay"), partner, high))
        width = mine.shape[0]
        wide = jnp.concatenate(
            [before, mine, after]
            + [jnp.zeros((-3 * width % TILE, LANES), F32)] * (3 * width % TILE > 0),
            axis=0,
        )
        product = jnp.dot(stacked([wide]), low_ref[...], preferred_element_type=F32)
        picked = unstack(product, wide.shape[0])[0]
        match = iota(picked.shape, 0) == high_ref[...]
        peers = jnp.sum(jnp.where(match, picked, 0.0), axis=0, keepdims=True)
        flux = as_line(fsrc_ref[...]) + frac_ref[0:1, :] * pressure_at
        for j in range(links):
            flux = flux + trans_ref[j : j + 1, :] * peers[:, j * slots : (j + 1) * slots]
        result = (1.0 - OMEGA) * f_ref[...] + frac_ref[1:2, :] * flux
        copies = []
        for x in range(cell_rows):
            value = base_ref[x] + fields.terms(x, lambda t: forward_ref[t, x])
            if x == 0:
                value = value + left_rim
            if x == last:
                value = value + right_rim
            p_out[x] = add_edge_rows(value, low_rim[x : x + 1, :], high_rim[x : x + 1, :])
            if (x + 1) % piece == 0:
                part = pl.ds(x + 1 - piece, piece)
                copies.append(
                    pltpu.make_async_copy(p_out.at[part], p_hbm.at[part], sems.at[x // piece])
                )
                copies[-1].start()
        f_out[...] = as_rows(result, LANES)
        copies.append(pltpu.make_async_copy(f_out, f_hbm, sems.at[pieces]))
        copies[-1].start()
        for copy in copies:
            copy.wait()

    final, frac_final = run(
        kernel_c,
        [(block, F32), (small, F32)],
        (
            sfaces, forward, base, sedges, hot_node, node_weight, frac_pack, peer_high,
            hot_low, slot_source, frac_trans, fracture, slot_pressure, joined_two, coarse,
            *blk_one, *blk_two, *lay_one, *lay_two, *ring,
        ),
        scratch=(
            pltpu.VMEM(block, F32),
            pltpu.VMEM(small, F32),
            pltpu.SemaphoreType.DMA((pieces + 1,)),
        ),
        out_place=(0, 1),
    )
    return final, frac_final.reshape(slots)


def solution(mesh):
    return jax.shard_map(
        local,
        mesh=mesh,
        in_specs=(
            P("lay", "blk", None),
            P("lay", "blk", None),
            P(None, "lay", "blk", None),
            P(None, "lay", "blk", None),
            P("lay", "blk"),
            P(None, "lay", "blk"),
            P(("blk", "lay")),
            P(("blk", "lay")),
            P(("blk", "lay")),
            P(None, ("blk", "lay")),
            P(("blk", "lay")),
            P(None, ("blk", "lay")),
            P(("blk", "lay")),
        ),
        out_specs=(P("lay", "blk", None), P(("blk", "lay"))),
        check_vma=False,
    )
```
